128 devices in a mesh: gx: 16 (over z, y), gy: 8 (over x, core).
Axes of the slice: x: 4, y: 4, z: 4, core: 2. Of those that a mesh axis runs over, the one named last changes fastest.
Arguments:
- head_old: float32 [10, 256, 4096], P(None, 'gx', 'gy'), may hold values from -4 to 4
- soil_type: int32 [10, 256, 4096], P(None, 'gx', 'gy'), may hold values from 0 to 11
- soil_table: float32 [3, 12], replicated, may hold values from 0.2 to 3, as said below
- forcing: float32 [4, 256, 4096], P(None, 'gx', 'gy'), may hold values from 0 to 2, as said below
- canopy: float32 [13, 1048576], P(None, ('gx', 'gy')), may hold values from 0.05 to 6, as said below
- column_slot: int32 [256, 4096], P('gx', 'gy'), may hold values from -1 to 8191, as said below
Outputs:
- head_new: float32 [10, 256, 4096], P(None, 'gx', 'gy')
- surface_flux: float32 [2, 256, 4096], P(None, 'gx', 'gy')
The draws below stay inside these ranges and needn't reach their ends.
Inputs may be any that keep to these rules, and one draw needn't show every extreme that they name: `soil_table`: Rows: conductivity 0.2 to 2, steepness 0.5 to 3, capacity 0.2 to 0.5. `forcing`: Rows: sunlight 0.5 to 2, air temperature 0.8 to 1.2, humidity 0 to 0.5, rainfall 0.1 to 2. `canopy`: Rows: leaf area 0.5 to 6, albedo 0.1 to 0.3, resistance 0.2 to 5, root weights 0.05 to 1. `column_slot`: the land cells of one device's tile name distinct values; the value v sends the column to the device of index v // 64 along gx+gy into slot v % 64; in every draw some device uses every value.
All inputs are finite; a program needn't handle non-finite values.
Results may differ from the reference program's by a relative error of at most 0.00029.
Values sent between devices are 32-bit elements; how exact they have to be, the bound alone decides.
A program may use at most 64 MiB of HBM per device.

```python
import math
import jax
import jax.numpy as jnp
from jax import lax

NZ = 10
CX = 16
CY = 512
CAP = 64
NSOIL = 12
NEWTON = 2
KRYLOV = 3
NX = 256
NY = 4096
SLOTS = 8192
COLS = 1048576


def ranged(key, shape, lower, upper, logscale):
    unit = jax.random.uniform(key, shape, jnp.float32)
    if logscale:
        return jnp.exp(math.log(lower) + (math.log(upper) - math.log(lower)) * unit)
    return lower + (upper - lower) * unit


def draw_soil_table(key, part):
    keys = jax.random.split(key, 3)
    conduct = ranged(keys[0], (NSOIL,), 0.2, 2.0, True)
    steep = ranged(keys[1], (NSOIL,), 0.5, 3.0, True)
    capacity = ranged(keys[2], (NSOIL,), 0.2, 0.5, False)
    return jnp.stack([conduct, steep, capacity]).astype(jnp.float32)


def draw_forcing(key, part):
    keys = jax.random.split(key, 4)
    sunlight = ranged(keys[0], (NX, NY), 0.5, 2.0, False)
    air_temp = ranged(keys[1], (NX, NY), 0.8, 1.2, False)
    humidity = ranged(keys[2], (NX, NY), 0.0, 0.5, False)
    rainfall = ranged(keys[3], (NX, NY), 0.1, 2.0, True)
    return jnp.stack([sunlight, air_temp, humidity, rainfall]).astype(jnp.float32)


def draw_canopy(key, part):
    keys = jax.random.split(key, 4)
    leaf_area = ranged(keys[0], (1, COLS), 0.5, 6.0, True)
    albedo = ranged(keys[1], (1, COLS), 0.1, 0.3, False)
    resist = ranged(keys[2], (1, COLS), 0.2, 5.0, True)
    roots = ranged(keys[3], (NZ, COLS), 0.05, 1.0, True)
    return jnp.concatenate([leaf_area, albedo, resist, roots], axis=0).astype(jnp.float32)


def draw_column_slot(key, part):
    grid_x = NX // CX
    grid_y = NY // CY
    devices = grid_x * grid_y
    top = CX * CY
    keys = jax.random.split(key, 5)
    level = jax.random.randint(keys[0], (devices,), 2, 11)
    forced = jax.random.randint(keys[1], (), 0, devices)
    level = jnp.where(jnp.arange(devices) == forced, 10, level)
    chance = jax.random.randint(keys[2], (devices, top), 0, 10)
    candidate = chance < level[:, None]
    order = jax.vmap(lambda sub_key: jax.random.permutation(sub_key, top))(jax.random.split(keys[3], devices))
    shuffled = jax.vmap(lambda sub_key: jax.random.permutation(sub_key, SLOTS))(jax.random.split(keys[4], devices))
    ordered = jnp.take_along_axis(candidate, order, axis=1)
    rank = jnp.cumsum(ordered.astype(jnp.int32), axis=1) - 1
    kept = ordered & (rank < SLOTS)
    chosen = jnp.take_along_axis(shuffled, jnp.clip(rank, 0, SLOTS - 1), axis=1)
    values = jnp.where(kept, chosen, -1).astype(jnp.int32)
    placed = jax.vmap(lambda positions, entries: jnp.zeros((top,), jnp.int32).at[positions].set(entries))(order, values)
    return placed.reshape(grid_x, grid_y, CX, CY).transpose(0, 2, 1, 3).reshape(NX, NY).astype(jnp.int32)


def set_ends(result, stream_key, low, top_value):
    shape = result.shape
    spot = [jax.random.randint(jax.random.fold_in(stream_key, axis), (), 0, shape[axis]) for axis in range(len(shape))]
    result = result.at[tuple(spot)].set(low)
    longest = shape.index(max(shape))
    spot[longest] = (spot[longest] + 1) % shape[longest]
    return result.at[tuple(spot)].set(top_value)


def block_scale(own_key, extent, cuts, low, high):
    def one(dim, blocks):
        draws = jax.random.uniform(jax.random.fold_in(jax.random.fold_in(own_key, 6), dim), (blocks,), jnp.float32, low / len(cuts), high / len(cuts))
        return jnp.repeat(jnp.exp(draws), extent[dim] // blocks).reshape((-1,) + (1,) * (len(extent) - dim - 1))

    factor_of = one(*cuts[0])
    for cut in cuts[1:]:
        factor_of = factor_of * one(*cut)
    return factor_of


def scatter_about(rng, dims, width, reach, pieces=(), held_as=jnp.bfloat16):
    gain = block_scale(rng, dims, pieces, -0.22, 0.18) if pieces else 1.0
    drawn = jax.random.normal(rng, dims, jnp.float32) * width * gain
    return jnp.minimum(jnp.maximum(drawn, -reach), reach).astype(held_as)


def setup_inputs(seed: int = 0) -> dict:
    splits = jax.random.split(jax.random.key(seed), 7)
    return {
        "head_old": scatter_about(splits[0], (NZ, NX, NY), 1.0, 4.0, ((1, 16), (2, 8)), jnp.float32),
        "soil_type": set_ends(jax.random.randint(splits[1], (NZ, NX, NY), 0, NSOIL), jax.random.fold_in(splits[1], 1), 0, NSOIL - 1).astype(jnp.int32),
        "soil_table": draw_soil_table(jax.random.fold_in(splits[6], 71), 0),
        "forcing": draw_forcing(jax.random.fold_in(splits[6], 71), 0),
        "canopy": draw_canopy(jax.random.fold_in(splits[6], 71), 0),
        "column_slot": draw_column_slot(jax.random.fold_in(splits[6], 71), 0),
    }


storage_weight = 4.0
norm_epsilon = 1e-06

def soil_fields(soil_type, soil_table):
    conduct = jnp.zeros(soil_type.shape, jnp.float32)
    steep = jnp.zeros(soil_type.shape, jnp.float32)
    capacity = jnp.zeros(soil_type.shape, jnp.float32)
    for kind in range(soil_table.shape[1]):
        match = soil_type == kind
        conduct = jnp.where(match, soil_table[0, kind], conduct)
        steep = jnp.where(match, soil_table[1, kind], steep)
        capacity = jnp.where(match, soil_table[2, kind], capacity)
    return jnp.stack([conduct, steep, capacity])

def balance(padded, params, theta_old, source):
    sat = jax.nn.sigmoid(params[1] * padded)
    conduct = params[0] * (0.1 + 0.9 * sat * sat)
    head = padded[:, 1:-1, 1:-1]
    inner = conduct[:, 1:-1, 1:-1]
    theta = params[2][:, 1:-1, 1:-1] * sat[:, 1:-1, 1:-1]
    lateral = jnp.zeros_like(head)
    for near_head, near_cond in ((padded[:, 2:, 1:-1], conduct[:, 2:, 1:-1]), (padded[:, :-2, 1:-1], conduct[:, :-2, 1:-1]), (padded[:, 1:-1, 2:], conduct[:, 1:-1, 2:]), (padded[:, 1:-1, :-2], conduct[:, 1:-1, :-2])):
        lateral = lateral + 0.5 * (inner + near_cond) * (head - near_head)
    face = 0.5 * (inner[:-1] + inner[1:]) * (head[:-1] - head[1:] + 1.0)
    below = jnp.concatenate([face, inner[-1:]], axis=0)
    above = jnp.concatenate([jnp.zeros_like(head[:1]), face], axis=0)
    return storage_weight * (theta - theta_old) + lateral + below - above - source

def land_column(wet, ks_top, forcing, records):
    sunlight, air_temp, humidity, rainfall = (forcing[0], forcing[1], forcing[2], forcing[3])
    leaf_area, albedo, resist = (records[0], records[1], records[2])
    roots = records[3:]
    uptake = roots * wet
    total = lax.optimization_barrier(jnp.sum(uptake, axis=0))
    wetness = total / lax.optimization_barrier(jnp.sum(roots, axis=0))
    conductance = wetness * leaf_area / (leaf_area + resist)
    exchange_coef = 0.5 + 0.3 * leaf_area
    radiation = (1.0 - albedo) * sunlight + 0.3
    surface = air_temp
    for sweep_index in range(2):
        vapour = 0.5 * jnp.exp(2.0 * (surface - air_temp))
        square = surface * surface
        excess = radiation - 0.3 * square * square - exchange_coef * (surface - air_temp) - conductance * (vapour - humidity)
        slope = -1.2 * square * surface - exchange_coef - 2.0 * conductance * vapour
        surface = surface - excess / slope
    vapour = 0.5 * jnp.exp(2.0 * (surface - air_temp))
    evaporation = conductance * (vapour - humidity)
    infiltration = rainfall * ks_top / (rainfall + ks_top)
    sink = evaporation * uptake / total
    return (sink, evaporation, infiltration)

def surface_terms(land, sink, evaporation, infiltration):
    source = jnp.where(land, -sink, 0.0)
    source = source.at[0].add(jnp.where(land, infiltration, 0.0))
    flux = jnp.stack([jnp.where(land, evaporation, 0.0), jnp.where(land, infiltration, 0.0)])
    return (source, flux)

def small_solve(hessen, initial_norm):
    gram = jnp.dot(hessen.T, hessen, precision=lax.Precision.HIGHEST)
    target = hessen[0] * initial_norm
    factor = jnp.linalg.cholesky(gram)
    size = gram.shape[0]
    forward = []
    for row in range(size):
        value = target[row]
        for other in range(row):
            value = value - factor[row, other] * forward[other]
        forward.append(value / factor[row, row])
    backward = [None] * size
    for row in reversed(range(size)):
        value = forward[row]
        for other in range(row + 1, size):
            value = value - factor[other, row] * backward[other]
        backward[row] = value / factor[row, row]
    return jnp.stack(backward)

def pad_cells(field):
    return jnp.pad(field, ((0, 0), (1, 1), (1, 1)))

def reference(head_old, soil_type, soil_table, forcing, canopy, column_slot):
    params = soil_fields(soil_type, soil_table)
    wet = jax.nn.sigmoid(params[1] * head_old)
    theta_old = params[2] * wet
    land = column_slot >= 0
    slot = jnp.maximum(column_slot, 0)
    device = (jnp.arange(NX, dtype=jnp.int32) // CX)[:, None] * (NY // CY) + (jnp.arange(NY, dtype=jnp.int32) // CY)[None, :]
    record = slot // CAP * SLOTS + device * CAP + slot % CAP
    cell_records = jnp.take(canopy, record.reshape(-1).astype(jnp.int32), axis=1).reshape(-1, NX, NY)
    sink, evaporation, infiltration = land_column(wet, params[0, 0], forcing, cell_records)
    source, surface_flux = surface_terms(land, sink, evaporation, infiltration)
    padded_params = jnp.pad(params, ((0, 0), (0, 0), (1, 1), (1, 1)))
    head = head_old
    for newton_step in range(NEWTON):
        padded = pad_cells(head)

        def residual_of(field):
            return balance(field, padded_params, theta_old, source)
        residual_now = residual_of(padded)
        initial_norm = jnp.sqrt(jnp.sum(residual_now * residual_now) + norm_epsilon)
        basis = [residual_now / initial_norm]
        hessen = jnp.zeros((KRYLOV + 1, KRYLOV), jnp.float32)
        for krylov_step in range(KRYLOV):
            direction = jax.jvp(residual_of, (padded,), (pad_cells(basis[krylov_step]),))[1]
            for index, earlier in enumerate(basis):
                product = jnp.sum(direction * earlier)
                direction = direction - product * earlier
                hessen = hessen.at[index, krylov_step].set(product)
            length = jnp.sqrt(jnp.sum(direction * direction) + norm_epsilon)
            hessen = hessen.at[krylov_step + 1, krylov_step].set(length)
            if krylov_step + 1 < KRYLOV:
                basis.append(direction / length)
        weights = small_solve(hessen, initial_norm)
        for index, earlier in enumerate(basis):
            head = head - weights[index] * earlier
    return (head, surface_flux)
```

```python
import functools

import jax
import jax.numpy as jnp
from jax import lax
from jax.experimental import pallas as pl
from jax.experimental.pallas import tpu as pltpu
from jax.sharding import PartitionSpec as P

NEWTON = 2
KRYLOV = 3
CAP = 64

STORAGE = 4.0
EPSILON = 1e-06

SHIFT = 3.0
SCALE = 3.0

MESH = pl.DeviceIdType.MESH
ROWS = 24
LANES = 640


def logistic(u):
    return 1.0 / (1.0 + jnp.exp(-u))


def ahead(x, axis):
    return pltpu.roll(x, x.shape[axis] - 1, axis)


def behind(x, axis):
    return pltpu.roll(x, 1, axis)


def krylov_weights(gram):
    def inner(vector, image):
        terms = [a * b for a, b in zip(vector, image) if a is not None]
        return functools.reduce(lambda a, b: a + b, terms)

    def image_of(vector):
        return [inner(vector, [gram[i][k] for i in range(4)]) for k in range(4)]

    beta = jnp.sqrt(gram[0][0] + EPSILON)
    basis = [[1.0 / beta, None, None, None]]
    images = [image_of(basis[0])]
    hessen = [[None] * KRYLOV for _ in range(KRYLOV + 1)]
    for j in range(KRYLOV):
        v = basis[j]
        w = [None] * 4
        for i in range(j + 2):
            if i <= j:
                w[i] = SHIFT * v[i]
            if i >= 1:
                term = SCALE * v[i - 1]
                w[i] = term if w[i] is None else w[i] + term
        for i in range(j + 1):
            product = inner(w, images[i])
            hessen[i][j] = product
            w = [a if b is None else a - product * b for a, b in zip(w, basis[i])]
        square = jnp.maximum(inner(w, image_of(w)), 0.0)
        length = jnp.sqrt(square + EPSILON)
        hessen[j + 1][j] = length
        if j + 1 < KRYLOV:
            basis.append([None if a is None else a / length for a in w])
            images.append(image_of(basis[-1]))

    def column(a, b):
        pairs = [(hessen[i][a], hessen[i][b]) for i in range(KRYLOV + 1)]
        terms = [x * y for x, y in pairs if x is not None and y is not None]
        return functools.reduce(lambda x, y: x + y, terms)

    factor = [[None] * KRYLOV for _ in range(KRYLOV)]
    for i in range(KRYLOV):
        for j in range(i + 1):
            value = column(i, j)
            for k in range(j):
                value = value - factor[i][k] * factor[j][k]
            factor[i][j] = jnp.sqrt(value) if i == j else value / factor[j][j]
    forward = []
    for row in range(KRYLOV):
        value = hessen[0][row] * beta
        for other in range(row):
            value = value - factor[row][other] * forward[other]
        forward.append(value / factor[row][row])
    y = [None] * KRYLOV
    for row in reversed(range(KRYLOV)):
        value = forward[row]
        for other in range(row + 1, KRYLOV):
            value = value - factor[other][row] * y[other]
        y[row] = value / factor[row][row]
    weights = []
    for i in range(KRYLOV):
        terms = [y[j] * basis[j][i] for j in range(KRYLOV) if basis[j][i] is not None]
        weights.append(functools.reduce(lambda a, b: a + b, terms))
    return weights


def kernel(
    sizes,
    head_ref,
    soil_ref,
    table_ref,
    forcing_ref,
    canopy_ref,
    slot_ref,
    out_ref,
    flux_ref,
    send_c,
    recv_c,
    split,
    records,
    head,
    soil,
    conduct,
    slope,
    ksat,
    steep,
    cap,
    coef,
    basis,
    wet,
    theta_old,
    source,
    mask,
    send_x,
    recv_x,
    send_y,
    recv_y,
    part,
    gather_x,
    gather_y,
    sem_c,
    sem_x,
    sem_y,
    sem_gx,
    sem_gy,
):
    size_x, size_y = sizes
    devices = size_x * size_y
    layers = head_ref.shape[0]
    half = layers // 2
    gx, gy = lax.axis_index("gx"), lax.axis_index("gy")
    me = gx * size_y + gy

    def device(d):
        return (d // size_y, lax.rem(d, size_y))

    barrier = pltpu.get_barrier_semaphore()

    def greet(i, carry):
        pl.semaphore_signal(
            barrier, inc=1, device_id=device(lax.rem(me + i, devices)), device_id_type=MESH
        )
        return carry

    lax.fori_loop(1, devices, greet, 0)

    lane8 = lax.broadcasted_iota(jnp.int32, (8, 128), 1)
    low8 = lane8 < CAP

    def pack(q, carry):
        lanes = pl.ds(pl.multiple_of(q * 128, 128), 128)
        first, second = canopy_ref[0:8, lanes], canopy_ref[5:13, lanes]
        send_c[2 * q] = jnp.where(low8, first, pltpu.roll(second, CAP, 1))
        send_c[2 * q + 1] = jnp.where(low8, pltpu.roll(first, CAP, 1), second)
        return carry

    lax.fori_loop(0, devices // 2, pack, 0)
    recv_c[pl.ds(pl.multiple_of(me * 8, 8), 8), :] = send_c[me]

    row = lax.broadcasted_iota(jnp.int32, (ROWS, LANES), 0)
    col = lax.broadcasted_iota(jnp.int32, (ROWS, LANES), 1)
    one, zero = jnp.float32(1.0), jnp.float32(0.0)
    has_next_x = jnp.where(gx < size_x - 1, one, zero)
    has_prev_x = jnp.where(gx > 0, one, zero)
    has_next_y = jnp.where(gy < size_y - 1, one, zero)
    has_prev_y = jnp.where(gy > 0, one, zero)
    inside_x = jnp.where(row < 16, 1.0, jnp.where(row < 20, has_next_x, has_prev_x))
    inside_y = jnp.where(
        col < 512,
        1.0,
        jnp.where(col < 516, has_next_y, jnp.where(col >= LANES - 4, has_prev_y, 0.0)),
    )
    mask[...] = inside_x * inside_y

    def own(ref, k):
        return ref[k, 0:16, 0:512]

    def clear(k, carry):
        head[k] = jnp.zeros((ROWS, LANES), jnp.float32)
        soil[k] = jnp.zeros((ROWS, LANES), jnp.float32)
        basis[0, k] = jnp.zeros((ROWS, LANES), jnp.float32)
        head[k, 0:16, 0:512] = head_ref[k]
        soil[k, 0:16, 0:512] = soil_ref[k].astype(jnp.float32)
        return carry

    lax.fori_loop(0, layers, clear, 0)

    sub512 = lax.broadcasted_iota(jnp.int32, (8, 512), 0)
    early = sub512 < 4

    def wrap(value, size):
        return lax.rem(value + size, size)

    next_x, prev_x = (wrap(gx + 1, size_x), gy), (wrap(gx - 1, size_x), gy)
    next_y, prev_y = (gx, wrap(gy + 1, size_y)), (gx, wrap(gy - 1, size_y))

    def copies(send, recv, sem, number, slot, count, targets):
        return [
            pltpu.make_async_remote_copy(
                src_ref=send.at[side, pl.ds(slot, count)],
                dst_ref=recv.at[side, pl.ds(slot, count)],
                send_sem=sem.at[0, number, side],
                recv_sem=sem.at[1, number, side],
                device_id=target,
                device_id_type=MESH,
            )
            for side, target in enumerate(targets)
        ]

    def start_x(number, slot, fields):
        def pack_rows(k, carry):
            for f, (ref, index) in enumerate(fields):
                at = lambda k: ref[index + (k, slice(0, 16), slice(0, 512))]
                upper, lower = at(k), at(k + half)
                send_x[0, slot + f, k] = jnp.where(early, pltpu.roll(lower[8:16], 4, 0), upper[8:16])
                send_x[1, slot + f, k] = jnp.where(early, upper[0:8], pltpu.roll(lower[0:8], 4, 0))
            return carry

        lax.fori_loop(0, half, pack_rows, 0)
        moves = copies(send_x, recv_x, sem_x, number, slot, len(fields), (next_x, prev_x))
        for move in moves:
            move.start()
        return moves

    def finish_x(moves, slot, fields):
        for move in moves:
            move.wait()
        edge = mask[16:24, 0:512]

        def place_rows(k, carry):
            for f, (ref, index) in enumerate(fields):
                before, after = recv_x[0, slot + f, k], recv_x[1, slot + f, k]
                ref[index + (k, slice(16, 24), slice(0, 512))] = edge * jnp.where(early, after, before)
                other = pltpu.roll(jnp.where(early, before, after), 4, 0)
                ref[index + (k + half, slice(16, 24), slice(0, 512))] = edge * other
            return carry

        lax.fori_loop(0, half, place_rows, 0)

    lane24 = lax.broadcasted_iota(jnp.int32, (ROWS, 128), 1)
    group24 = lane24 // 4

    def start_y(number, slot, fields):
        for f, (ref, index) in enumerate(fields):
            up = jnp.zeros((ROWS, 128), jnp.float32)
            down = jnp.zeros((ROWS, 128), jnp.float32)
            for k in range(layers):
                last = ref[index + (k, slice(0, ROWS), slice(384, 512))]
                first = ref[index + (k, slice(0, ROWS), slice(0, 128))]
                here = group24 == k
                up = jnp.where(here, pltpu.roll(last, 4 * k + 4, 1), up)
                down = jnp.where(here, pltpu.roll(first, 4 * k, 1) if k else first, down)
            send_y[0, slot + f] = up
            send_y[1, slot + f] = down
        moves = copies(send_y, recv_y, sem_y, number, slot, len(fields), (next_y, prev_y))
        for move in moves:
            move.start()
        return moves

    def finish_y(moves, slot, fields):
        for move in moves:
            move.wait()
        edge = mask[:, 512:640]
        for f, (ref, index) in enumerate(fields):
            before, after = recv_y[0, slot + f], recv_y[1, slot + f]
            for k in range(layers):
                left = pltpu.roll(before, 128 - (4 * k + 4), 1)
                right = pltpu.roll(after, 128 - 4 * k, 1) if k else after
                both = jnp.where(lane24 < 4, right, jnp.where(lane24 >= 124, left, 0.0))
                ref[index + (k, slice(0, ROWS), slice(512, 640))] = edge * both

    def exchange(number, slot, fields):
        finish_x(start_x(number, slot, fields), slot, fields)
        finish_y(start_y(number, slot, fields), slot, fields)

    pl.semaphore_wait(barrier, devices - 1)

    opening = [(head, ()), (soil, ())]
    moves = start_x(0, 0, opening)

    def scatter(i, carry):
        d = lax.rem(me + i, devices)
        pltpu.make_async_remote_copy(
            src_ref=send_c.at[d],
            dst_ref=recv_c.at[pl.ds(pl.multiple_of(me * 8, 8), 8)],
            send_sem=sem_c.at[0],
            recv_sem=sem_c.at[1],
            device_id=device(d),
            device_id_type=MESH,
        ).start()
        return carry

    lax.fori_loop(1, devices, scatter, 0)

    finish_x(moves, 0, opening)
    finish_y(start_y(0, 0, opening), 0, opening)

    def look_up(k, carry):
        kind = soil[k]
        values = [jnp.zeros((ROWS, LANES), jnp.float32) for _ in range(3)]
        for c in range(table_ref.shape[1]):
            match = kind == float(c)
            values = [jnp.where(match, table_ref[p, c], v) for p, v in enumerate(values)]
        ksat[k] = values[0] * mask[...]
        steep[k] = values[1]
        cap[k] = values[2]
        return carry

    lax.fori_loop(0, layers, look_up, 0)

    def saturate(first):
        def layer(k, carry):
            a, ks, c = steep[k], ksat[k], cap[k]
            s = logistic(a * head[k])
            rise = a * s * (1.0 - s)
            conduct[k] = ks * (0.1 + 0.9 * s * s)
            slope[k] = 0.9 * ks * s * rise
            coef[0, k] = STORAGE * c * rise
            theta = (c * s)[0:16, 0:512]
            if first:
                wet[k] = s[0:16, 0:512]
                theta_old[k] = theta
            else:
                basis[0, k, 0:16, 0:512] = STORAGE * (theta - theta_old[k]) - source[k]
            return carry

        lax.fori_loop(0, layers, layer, 0)

    def linearize(first):
        scaled = mask[...] * (1.0 / SCALE)

        def layer(k, carry):
            h, kk, dk = head[k], conduct[k], slope[k]
            diagonal = coef[0, k] - SHIFT
            total = None
            for axis, at in ((0, 1), (1, 3)):
                drop = h - ahead(h, axis)
                mean = 0.5 * (kk + ahead(kk, axis))
                mine = dk * drop + mean
                other = ahead(dk, axis) * drop - mean
                flow = mean * drop
                net = flow - behind(flow, axis)
                total = net if total is None else total + net
                diagonal = diagonal + mine - behind(other, axis)
                coef[at, k] = other * scaled
                coef[at + 1, k] = -behind(mine, axis) * scaled
            below, above = jnp.minimum(k + 1, layers - 1), jnp.maximum(k - 1, 0)
            bottom, top = k == layers - 1, k == 0
            drop = h - head[below] + 1.0
            mean = 0.5 * (kk + conduct[below])
            mine = jnp.where(bottom, 2.0 * dk, dk * drop + mean)
            other = jnp.where(bottom, 0.0, slope[below] * drop - mean)
            flow = jnp.where(bottom, kk, mean * drop)
            diagonal = diagonal + mine
            coef[5, k] = other * scaled
            total = total + flow
            drop = head[above] - h + 1.0
            mean = 0.5 * (kk + conduct[above])
            mine = jnp.where(top, 0.0, slope[above] * drop + mean)
            other = jnp.where(top, 0.0, dk * drop - mean)
            flow = jnp.where(top, 0.0, mean * drop)
            diagonal = diagonal - other
            coef[6, k] = -mine * scaled
            total = total - flow
            coef[0, k] = diagonal * scaled
            if first:
                basis[0, k, 0:16, 0:512] = total[0:16, 0:512]
            else:
                basis[0, k, 0:16, 0:512] += total[0:16, 0:512]
            return carry

        lax.fori_loop(0, layers, layer, 0)

    saturate(True)
    linearize(True)

    everything = pltpu.make_async_copy(
        recv_c.at[pl.ds(0, 8 * (devices - 1))], recv_c.at[pl.ds(0, 8 * (devices - 1))], sem_c.at[1]
    )
    everything.wait()
    blocks = devices // 4
    low = lax.broadcasted_iota(jnp.int32, (blocks, 128), 1) < CAP

    def put(r, left, right):
        value = jnp.concatenate([left, right], axis=1)
        high = value.astype(jnp.bfloat16)
        split[blocks * r : blocks * (r + 1), 0:256] = high
        split[blocks * r : blocks * (r + 1), 256:512] = (value - high.astype(jnp.float32)).astype(
            jnp.bfloat16
        )

    for r in range(8):
        plain = [recv_c[pl.ds(8 * c + r, blocks, stride=32), :] for c in range(4)]
        moved = [pltpu.roll(x, CAP, 1) for x in plain]
        put(r, jnp.where(low, plain[0], moved[1]), jnp.where(low, plain[2], moved[3]))
        if r >= 3:
            put(r + 5, jnp.where(low, moved[0], plain[1]), jnp.where(low, moved[2], plain[3]))

    within = lax.broadcasted_iota(jnp.int32, (256, 512), 0)
    which = lax.broadcasted_iota(jnp.int32, (blocks, 512), 0)

    def select(x, carry):
        slot = jnp.maximum(slot_ref[pl.ds(x, 1), :], 0)
        hot = jnp.where(within == (slot & 255), 1.0, 0.0).astype(jnp.bfloat16)
        found = jnp.dot(
            split[...], jnp.concatenate([hot, hot], axis=0), preferred_element_type=jnp.float32
        )
        match = which == (slot >> 8)
        for r in range(13):
            piece = jnp.where(match, found[blocks * r : blocks * (r + 1)], 0.0)
            records[r, pl.ds(x, 1), :] = jnp.sum(piece, axis=0, keepdims=True)
        return carry

    lax.fori_loop(0, 16, select, 0)

    sunlight, air, humidity, rainfall = (forcing_ref[i] for i in range(4))
    leaf, albedo, resist = (records[i] for i in range(3))
    total, roots = jnp.zeros_like(leaf), jnp.zeros_like(leaf)
    for k in range(layers):
        total = total + records[3 + k] * wet[k]
        roots = roots + records[3 + k]
    conductance = total / roots * leaf / (leaf + resist)
    exchange_coef = 0.5 + 0.3 * leaf
    radiation = (1.0 - albedo) * sunlight + 0.3
    surface = air
    for _ in range(2):
        vapour = 0.5 * jnp.exp(2.0 * (surface - air))
        square = surface * surface
        excess = (
            radiation
            - 0.3 * square * square
            - exchange_coef * (surface - air)
            - conductance * (vapour - humidity)
        )
        tangent = -1.2 * square * surface - exchange_coef - 2.0 * conductance * vapour
        surface = surface - excess / tangent
    evaporation = conductance * (0.5 * jnp.exp(2.0 * (surface - air)) - humidity)
    ks_top = own(ksat, 0)
    infiltration = rainfall * ks_top / (rainfall + ks_top)
    land = slot_ref[...] >= 0
    evaporation = jnp.where(land, evaporation, 0.0)
    infiltration = jnp.where(land, infiltration, 0.0)
    flux_ref[0] = evaporation
    flux_ref[1] = infiltration
    share = evaporation / total
    for k in range(layers):
        gain = -jnp.where(land, share * records[3 + k] * wet[k], 0.0)
        if k == 0:
            gain = gain + infiltration
        source[k] = gain
        basis[0, k, 0:16, 0:512] -= gain

    def fold(product):
        tall = product[0:8] + product[8:16]
        return (tall[:, 0:128] + tall[:, 128:256]) + (tall[:, 256:384] + tall[:, 384:512])

    def accumulate(n, at, sums):
        for i, value in enumerate(sums):
            part[n, 0, at + i : at + i + 1, :] = jnp.sum(value, axis=0, keepdims=True)

    def matvec(n, j, at):
        def layer(k, carry):
            v = basis[j, k]
            below, above = jnp.minimum(k + 1, layers - 1), jnp.maximum(k - 1, 0)
            w = coef[0, k] * v
            w = w + coef[1, k] * ahead(v, 0) + coef[2, k] * behind(v, 0)
            w = w + coef[3, k] * ahead(v, 1) + coef[4, k] * behind(v, 1)
            w = w + coef[5, k] * basis[j, below] + coef[6, k] * basis[j, above]
            if j + 1 < KRYLOV:
                basis[j + 1, k] = w
            mine = w[0:16, 0:512]
            sums = [fold(mine * basis[i, k, 0:16, 0:512]) for i in range(j + 1)]
            sums.append(fold(mine * mine))
            return tuple(a + b for a, b in zip(carry, sums))

        zeros = tuple(jnp.zeros((8, 128), jnp.float32) for _ in range(j + 2))
        accumulate(n, at, lax.fori_loop(0, layers, layer, zeros))

    def square_of_start(n):
        def layer(k, carry):
            value = own(basis.at[0], k)
            return carry + fold(value * value)

        accumulate(n, 0, [lax.fori_loop(0, layers, layer, jnp.zeros((8, 128), jnp.float32))])

    def reduce_all(n):
        def along(stage, gather, sem, here, size, target):
            mine = part.at[n, stage]
            gather[n, here] = mine[...]

            def send(i, carry):
                pltpu.make_async_remote_copy(
                    src_ref=mine,
                    dst_ref=gather.at[n, here],
                    send_sem=sem.at[0, n],
                    recv_sem=sem.at[1, n],
                    device_id=target(lax.rem(here + i, size)),
                    device_id_type=MESH,
                ).start()
                return carry

            lax.fori_loop(1, size, send, 0)
            rest = gather.at[n, pl.ds(0, size - 1)]
            pltpu.make_async_copy(rest, rest, sem.at[1, n]).wait()
            total = gather[n, 0]
            for i in range(1, size):
                total = total + gather[n, i]
            return total

        part[n, 1] = along(0, gather_x, sem_gx, gx, size_x, lambda d: (d, gy))
        total = along(1, gather_y, sem_gy, gy, size_y, lambda d: (gx, d))
        return jnp.sum(total, axis=1, keepdims=True)

    for n in range(NEWTON):
        if n:
            saturate(False)
            linearize(False)
        field = [(basis, (0,))]
        moves = start_x(1 + n, 2 + n, field)
        part[n, 0] = jnp.zeros((16, 128), jnp.float32)
        square_of_start(n)
        finish_x(moves, 2 + n, field)
        finish_y(start_y(1 + n, 2 + n, field), 2 + n, field)
        for j, at in ((0, 1), (1, 3), (2, 6)):
            matvec(n, j, at)
        sums = reduce_all(n)
        gram = [[None] * 4 for _ in range(4)]
        at = 0
        for i in range(4):
            for j in range(i + 1):
                gram[i][j] = gram[j][i] = sums[at : at + 1, :]
                at += 1
        weights = krylov_weights(gram)

        def update(k, carry):
            step = [weights[i] * own(basis.at[i], k) for i in range(KRYLOV)]
            value = own(head, k)
            for term in step:
                value = value - term
            if n + 1 < NEWTON:
                head[k, 0:16, 0:512] = value
            else:
                out_ref[k] = value
            return carry

        lax.fori_loop(0, layers, update, 0)
        if n + 1 < NEWTON:
            exchange(3 + n, 4 + n, [(head, ())])

    sent = send_c.at[pl.ds(0, devices - 1)]
    pltpu.make_async_copy(sent, sent, sem_c.at[0]).wait()
    for n in range(NEWTON):
        sent = gather_x.at[n, pl.ds(0, size_x - 1)]
        pltpu.make_async_copy(sent, sent, sem_gx.at[0, n]).wait()
        sent = gather_y.at[n, pl.ds(0, size_y - 1)]
        pltpu.make_async_copy(sent, sent, sem_gy.at[0, n]).wait()


def shards(sizes, head_old, soil_type, soil_table, forcing, canopy, column_slot):
    layers = head_old.shape[0]
    devices = sizes[0] * sizes[1]
    f32 = jnp.float32
    wide = (layers, ROWS, LANES)
    tile = (layers, 16, 512)
    vmem = pl.BlockSpec(memory_space=pltpu.VMEM)
    return pl.pallas_call(
        functools.partial(kernel, sizes),
        out_shape=(
            jax.ShapeDtypeStruct(head_old.shape, f32),
            jax.ShapeDtypeStruct((2, 16, 512), f32),
        ),
        in_specs=[vmem, vmem, pl.BlockSpec(memory_space=pltpu.SMEM), vmem, vmem, vmem],
        out_specs=(vmem, vmem),
        scratch_shapes=[
            pltpu.VMEM((devices, 8, 128), f32),
            pltpu.VMEM((devices * 8, 128), f32),
            pltpu.VMEM((13 * (devices // 4), 512), jnp.bfloat16),
            pltpu.VMEM((13, 16, 512), f32),
            pltpu.VMEM(wide, f32),
            pltpu.VMEM(wide, f32),
            pltpu.VMEM(wide, f32),
            pltpu.VMEM(wide, f32),
            pltpu.VMEM(wide, f32),
            pltpu.VMEM(wide, f32),
            pltpu.VMEM(wide, f32),
            pltpu.VMEM((7,) + wide, f32),
            pltpu.VMEM((KRYLOV,) + wide, f32),
            pltpu.VMEM(tile, f32),
            pltpu.VMEM(tile, f32),
            pltpu.VMEM(tile, f32),
            pltpu.VMEM((ROWS, LANES), f32),
            pltpu.VMEM((2, 5, layers // 2, 8, 512), f32),
            pltpu.VMEM((2, 5, layers // 2, 8, 512), f32),
            pltpu.VMEM((2, 5, ROWS, 128), f32),
            pltpu.VMEM((2, 5, ROWS, 128), f32),
            pltpu.VMEM((NEWTON, 2, 16, 128), f32),
            pltpu.VMEM((NEWTON, sizes[0], 16, 128), f32),
            pltpu.VMEM((NEWTON, sizes[1], 16, 128), f32),
            pltpu.SemaphoreType.DMA((2,)),
            pltpu.SemaphoreType.DMA((2, 4, 2)),
            pltpu.SemaphoreType.DMA((2, 4, 2)),
            pltpu.SemaphoreType.DMA((2, NEWTON)),
            pltpu.SemaphoreType.DMA((2, NEWTON)),
        ],
        compiler_params=pltpu.CompilerParams(collective_id=0, has_side_effects=True),
        name="coupled_step",
    )(head_old, soil_type, soil_table, forcing, canopy, column_slot)


def solution(mesh):
    sizes = (mesh.shape["gx"], mesh.shape["gy"])
    return jax.shard_map(
        functools.partial(shards, sizes),
        mesh=mesh,
        in_specs=(
            P(None, "gx", "gy"),
            P(None, "gx", "gy"),
            P(),
            P(None, "gx", "gy"),
            P(None, ("gx", "gy")),
            P("gx", "gy"),
        ),
        out_specs=(P(None, "gx", "gy"), P(None, "gx", "gy")),
        check_vma=False,
    )
```

```python
import functools

import jax
import jax.numpy as jnp
from jax import lax
from jax.experimental import pallas as pl
from jax.experimental.pallas import tpu as pltpu
from jax.sharding import PartitionSpec as P

NEWTON = 2
KRYLOV = 3
CAP = 64

STORAGE = 4.0
EPSILON = 1e-06

SHIFT = 3.0
SCALE = 3.0

MESH = pl.DeviceIdType.MESH
HALO = 3
ROWS = 24
LANES = 640


def logistic(u):
    return 1.0 / (1.0 + jnp.exp(-u))


def ahead(x, axis):
    return pltpu.roll(x, x.shape[axis] - 1, axis)


def behind(x, axis):
    return pltpu.roll(x, 1, axis)


def krylov_weights(gram):
    def inner(vector, image):
        terms = [a * b for a, b in zip(vector, image) if a is not None]
        return functools.reduce(lambda a, b: a + b, terms)

    def image_of(vector):
        return [inner(vector, [gram[i][k] for i in range(4)]) for k in range(4)]

    beta = jnp.sqrt(gram[0][0] + EPSILON)
    basis = [[1.0 / beta, None, None, None]]
    images = [image_of(basis[0])]
    hessen = [[None] * KRYLOV for _ in range(KRYLOV + 1)]
    for j in range(KRYLOV):
        v = basis[j]
        w = [None] * 4
        for i in range(j + 2):
            if i <= j:
                w[i] = SHIFT * v[i]
            if i >= 1:
                term = SCALE * v[i - 1]
                w[i] = term if w[i] is None else w[i] + term
        for i in range(j + 1):
            product = inner(w, images[i])
            hessen[i][j] = product
            w = [a if b is None else a - product * b for a, b in zip(w, basis[i])]
        square = jnp.maximum(inner(w, image_of(w)), 0.0)
        length = jnp.sqrt(square + EPSILON)
        hessen[j + 1][j] = length
        if j + 1 < KRYLOV:
            basis.append([None if a is None else a / length for a in w])
            images.append(image_of(basis[-1]))

    def column(a, b):
        pairs = [(hessen[i][a], hessen[i][b]) for i in range(KRYLOV + 1)]
        terms = [x * y for x, y in pairs if x is not None and y is not None]
        return functools.reduce(lambda x, y: x + y, terms)

    factor = [[None] * KRYLOV for _ in range(KRYLOV)]
    for i in range(KRYLOV):
        for j in range(i + 1):
            value = column(i, j)
            for k in range(j):
                value = value - factor[i][k] * factor[j][k]
            factor[i][j] = jnp.sqrt(value) if i == j else value / factor[j][j]
    forward = []
    for row in range(KRYLOV):
        value = hessen[0][row] * beta
        for other in range(row):
            value = value - factor[row][other] * forward[other]
        forward.append(value / factor[row][row])
    y = [None] * KRYLOV
    for row in reversed(range(KRYLOV)):
        value = forward[row]
        for other in range(row + 1, KRYLOV):
            value = value - factor[other][row] * y[other]
        y[row] = value / factor[row][row]
    weights = []
    for i in range(KRYLOV):
        terms = [y[j] * basis[j][i] for j in range(KRYLOV) if basis[j][i] is not None]
        weights.append(functools.reduce(lambda a, b: a + b, terms))
    return weights


def kernel(
    sizes,
    head_in,
    soil_in,
    table_ref,
    forcing_in,
    canopy_in,
    slot_in,
    out_ref,
    flux_ref,
    soil_ref,
    forcing_ref,
    canopy_ref,
    slot_ref,
    send_c,
    recv_c,
    split,
    hot,
    records,
    head,
    soil,
    conduct,
    slope,
    ksat,
    steep,
    cap,
    coef,
    basis,
    wet,
    theta_old,
    source,
    mask,
    send_x,
    recv_x,
    send_y,
    recv_y,
    recv_k,
    part,
    gather_x,
    gather_y,
    sem_in,
    sem_c,
    sem_e,
    sem_gx,
    sem_gy,
):
    size_x, size_y = sizes
    devices = size_x * size_y
    layers = out_ref.shape[0]
    gx, gy = lax.axis_index("gx"), lax.axis_index("gy")
    me = gx * size_y + gy

    loads = [
        pltpu.make_async_copy(src, dst, sem_in.at[i])
        for i, (src, dst) in enumerate(
            (
                (canopy_in, canopy_ref),
                (head_in, head.at[:, 0:16, 0:512]),
                (soil_in, soil_ref),
                (slot_in, slot_ref),
                (forcing_in, forcing_ref),
            )
        )
    ]
    for load in loads:
        load.start()

    def wrap(value, size):
        return lax.rem(value + size, size)

    def others(visit):
        for dy in range(1, size_y):
            visit(gx, lax.rem(gy + dy, size_y))

        def ring(i, carry):
            far = (i + 1) // 2
            x = wrap(gx + jnp.where(lax.rem(i, 2) == 1, far, -far), size_x)
            for dy in range(size_y):
                visit(x, lax.rem(gy + dy, size_y))
            return carry

        lax.fori_loop(1, size_x, ring, 0)

    barrier = pltpu.get_barrier_semaphore()
    others(lambda x, y: pl.semaphore_signal(barrier, inc=1, device_id=(x, y), device_id_type=MESH))

    row = lax.broadcasted_iota(jnp.int32, (ROWS, LANES), 0)
    col = lax.broadcasted_iota(jnp.int32, (ROWS, LANES), 1)
    one, zero = jnp.float32(1.0), jnp.float32(0.0)
    has_next_x = jnp.where(gx < size_x - 1, one, zero)
    has_prev_x = jnp.where(gx > 0, one, zero)
    has_next_y = jnp.where(gy < size_y - 1, one, zero)
    has_prev_y = jnp.where(gy > 0, one, zero)
    inside_x = jnp.where(
        row < 16,
        1.0,
        jnp.where(row < 16 + HALO, has_next_x, jnp.where(row >= ROWS - HALO, has_prev_x, 0.0)),
    )
    inside_y = jnp.where(
        col < 512,
        1.0,
        jnp.where(col < 512 + HALO, has_next_y, jnp.where(col >= LANES - HALO, has_prev_y, 0.0)),
    )
    mask[...] = inside_x * inside_y

    def own(ref, k):
        return ref[k, 0:16, 0:512]

    def clear(k, carry):
        for ref in (head, soil, basis.at[0]):
            ref[k, 16:24, 0:512] = jnp.zeros((8, 512), jnp.float32)
            ref[k, 0:24, 512:640] = jnp.zeros((24, 128), jnp.float32)
        return carry

    lax.fori_loop(0, layers, clear, 0)
    for side in range(2):
        for slot in range(5):
            send_x[side, slot, 24:32, :] = jnp.zeros((8, 512), jnp.float32)

    lane8 = lax.broadcasted_iota(jnp.int32, (8, 128), 1)
    low8 = lane8 < CAP

    def pack(q, carry):
        lanes = pl.ds(pl.multiple_of(q * 128, 128), 128)
        first, second = canopy_ref[0:8, lanes], canopy_ref[5:13, lanes]
        send_c[2 * q] = jnp.where(low8, first, pltpu.roll(second, CAP, 1))
        send_c[2 * q + 1] = jnp.where(low8, pltpu.roll(first, CAP, 1), second)
        return carry

    loads[0].wait()
    lax.fori_loop(0, devices // 2, pack, 0, unroll=4)
    recv_c[pl.ds(pl.multiple_of(me * 8, 8), 8), :] = send_c[me]

    next_x, prev_x = wrap(gx + 1, size_x), wrap(gx - 1, size_x)
    next_y, prev_y = wrap(gy + 1, size_y), wrap(gy - 1, size_y)
    lane16 = lax.broadcasted_iota(jnp.int32, (16, 128), 1)
    group16 = lane16 // 4
    lane24 = lax.broadcasted_iota(jnp.int32, (ROWS, 128), 1)
    early8 = lax.broadcasted_iota(jnp.int32, (8, 128), 0) < 4

    def start(number, slot, fields):
        for f, (ref, index) in enumerate(fields):
            up = jnp.zeros((16, 128), jnp.float32)
            down = jnp.zeros((16, 128), jnp.float32)
            for k in range(layers):
                rows = slice(HALO * k, HALO * (k + 1))
                send_x[0, slot + f, rows, :] = ref[index + (k, slice(16 - HALO, 16), slice(0, 512))]
                send_x[1, slot + f, rows, :] = ref[index + (k, slice(0, HALO), slice(0, 512))]
                last = ref[index + (k, slice(0, 16), slice(384, 512))]
                first = ref[index + (k, slice(0, 16), slice(0, 128))]
                here = group16 == k
                up = jnp.where(here, pltpu.roll(last, 4 * k + 4, 1), up)
                down = jnp.where(here, pltpu.roll(first, 4 * k, 1) if k else first, down)
            send_y[0, slot + f] = up
            send_y[1, slot + f] = down
        slots = pl.ds(slot, len(fields))
        plan = []
        for side, y in enumerate((next_y, prev_y)):
            for turn, x in enumerate((next_x, prev_x)):
                edge = pl.ds(8 * (1 - turn), 8)
                plan.append(
                    (send_y.at[side, slots, edge], recv_k.at[side, turn, slots], (x, y))
                )
        for side, x in enumerate((next_x, prev_x)):
            plan.append((send_x.at[side, slots], recv_x.at[side, slots], (x, gy)))
        for side, y in enumerate((next_y, prev_y)):
            plan.append((send_y.at[side, slots], recv_y.at[side, slots], (gx, y)))
        moves = [
            pltpu.make_async_remote_copy(
                src_ref=src,
                dst_ref=dst,
                send_sem=sem_e.at[0, number, i],
                recv_sem=sem_e.at[1, number, i],
                device_id=target,
                device_id_type=MESH,
            )
            for i, (src, dst, target) in enumerate(plan)
        ]
        for move in moves:
            move.start()
        return moves

    def finish(moves, slot, fields):
        for move in moves[6:] + moves[:4]:
            move.wait()
        edge = mask[:, 512:640]
        for f, (ref, index) in enumerate(fields):
            sides = [
                jnp.concatenate(
                    [
                        recv_y[side, slot + f],
                        jnp.where(early8, recv_k[side, 1, slot + f], recv_k[side, 0, slot + f]),
                    ],
                    axis=0,
                )
                for side in range(2)
            ]
            for k in range(layers):
                left = pltpu.roll(sides[0], 128 - (4 * k + 4), 1)
                right = pltpu.roll(sides[1], 128 - 4 * k, 1) if k else sides[1]
                both = jnp.where(lane24 < 64, right, left)
                ref[index + (k, slice(0, ROWS), slice(512, 640))] = jnp.where(edge > 0.0, both, 0.0)
        for move in moves[4:6]:
            move.wait()
        for f, (ref, index) in enumerate(fields):
            for k in range(layers):
                rows = slice(HALO * k, HALO * (k + 1))
                after = recv_x[1, slot + f, rows, :] * has_next_x
                before = recv_x[0, slot + f, rows, :] * has_prev_x
                ref[index + (k, slice(16, 16 + HALO), slice(0, 512))] = after
                ref[index + (k, slice(ROWS - HALO, ROWS), slice(0, 512))] = before

    loads[1].wait()
    loads[2].wait()

    def convert(k, carry):
        soil[k, 0:16, 0:512] = soil_ref[k].astype(jnp.float32)
        return carry

    lax.fori_loop(0, layers, convert, 0)

    pl.semaphore_wait(barrier, devices - 1)

    def scatter(x, y):
        pltpu.make_async_remote_copy(
            src_ref=send_c.at[x * size_y + y],
            dst_ref=recv_c.at[pl.ds(pl.multiple_of(me * 8, 8), 8)],
            send_sem=sem_c.at[0],
            recv_sem=sem_c.at[1],
            device_id=(x, y),
            device_id_type=MESH,
        ).start()

    others(scatter)
    opening = [(head, ()), (soil, ())]
    moves = start(0, 0, opening)

    def look_up(rows, lanes):
        def layer(k, carry):
            kind = soil[k, rows, lanes]
            values = [jnp.zeros(kind.shape, jnp.float32) for _ in range(3)]
            for c in range(table_ref.shape[1]):
                match = kind == float(c)
                values = [jnp.where(match, table_ref[p, c], v) for p, v in enumerate(values)]
            ksat[k, rows, lanes] = values[0] * mask[rows, lanes]
            steep[k, rows, lanes] = values[1]
            cap[k, rows, lanes] = values[2]
            return carry

        lax.fori_loop(0, layers, layer, 0)

    look_up(slice(0, 16), slice(0, 512))

    loads[3].wait()
    within = lax.broadcasted_iota(jnp.int32, (256, 512), 0)

    def spot(x, carry):
        slot = jnp.maximum(slot_ref[pl.ds(x, 1), :], 0)
        hot[x] = jnp.where(within == (slot & 255), 1.0, 0.0).astype(jnp.bfloat16)
        return carry

    lax.fori_loop(0, 16, spot, 0)

    finish(moves, 0, opening)
    look_up(slice(16, 24), slice(0, 512))
    look_up(slice(0, 24), slice(512, 640))

    def saturate(first):
        def layer(k, carry):
            a, ks, c = steep[k], ksat[k], cap[k]
            s = logistic(a * head[k])
            rise = a * s * (1.0 - s)
            conduct[k] = ks * (0.1 + 0.9 * s * s)
            slope[k] = 0.9 * ks * s * rise
            coef[0, k] = STORAGE * c * rise
            theta = (c * s)[0:16, 0:512]
            if first:
                wet[k] = s[0:16, 0:512]
                theta_old[k] = theta
            else:
                basis[0, k, 0:16, 0:512] = STORAGE * (theta - theta_old[k]) - source[k]
            return carry

        lax.fori_loop(0, layers, layer, 0, unroll=2)

    def saturate_again():
        def layer(k, carry):
            a, ks = steep[k], ksat[k]
            s = logistic(a * head[k])
            rise = a * s * (1.0 - s)
            conduct[k] = ks * (0.1 + 0.9 * s * s)
            slope[k] = 0.9 * ks * s * rise
            coef[0, k] = STORAGE * cap[k] * rise
            return carry

        lax.fori_loop(0, layers, layer, 0, unroll=2)

    def around(k):
        return jnp.minimum(k + 1, layers - 1), jnp.maximum(k - 1, 0)

    def balance():
        def layer(k, carry):
            h, kk = head[k], conduct[k]
            total = basis[0, k, 0:16, 0:512]
            for axis in range(2):
                flow = 0.5 * (kk + ahead(kk, axis)) * (h - ahead(h, axis))
                total = total + (flow - behind(flow, axis))[0:16, 0:512]
            below, above = around(k)
            h, kk = own(head, k), own(conduct, k)
            flow = 0.5 * (kk + own(conduct, below)) * (h - own(head, below) + 1.0)
            total = total + jnp.where(k == layers - 1, kk, flow)
            flow = 0.5 * (own(conduct, above) + kk) * (own(head, above) - h + 1.0)
            basis[0, k, 0:16, 0:512] = total - jnp.where(k == 0, 0.0, flow)
            return carry

        lax.fori_loop(0, layers, layer, 0, unroll=2)

    def linearize():
        scaled = mask[...] * (1.0 / SCALE)

        def layer(k, carry):
            h, kk, dk = head[k], conduct[k], slope[k]
            diagonal = coef[0, k] - SHIFT
            for axis, at in ((0, 1), (1, 3)):
                drop = h - ahead(h, axis)
                mean = 0.5 * (kk + ahead(kk, axis))
                mine = dk * drop + mean
                other = ahead(dk, axis) * drop - mean
                diagonal = diagonal + mine - behind(other, axis)
                coef[at, k] = other * scaled
                coef[at + 1, k] = -behind(mine, axis) * scaled
            below, above = around(k)
            bottom, top = k == layers - 1, k == 0
            drop = h - head[below] + 1.0
            mean = 0.5 * (kk + conduct[below])
            diagonal = diagonal + jnp.where(bottom, 2.0 * dk, dk * drop + mean)
            coef[5, k] = jnp.where(bottom, 0.0, slope[below] * drop - mean) * scaled
            drop = head[above] - h + 1.0
            mean = 0.5 * (kk + conduct[above])
            diagonal = diagonal - jnp.where(top, 0.0, dk * drop - mean)
            coef[6, k] = -jnp.where(top, 0.0, slope[above] * drop + mean) * scaled
            coef[0, k] = diagonal * scaled
            return carry

        lax.fori_loop(0, layers, layer, 0)

    saturate(True)
    linearize()

    def nothing(k, carry):
        basis[0, k, 0:16, 0:512] = jnp.zeros((16, 512), jnp.float32)
        return carry

    lax.fori_loop(0, layers, nothing, 0)
    balance()

    everything = pltpu.make_async_copy(
        recv_c.at[pl.ds(0, 8 * (devices - 1))], recv_c.at[pl.ds(0, 8 * (devices - 1))], sem_c.at[1]
    )
    everything.wait()
    blocks = devices // 4
    low = lax.broadcasted_iota(jnp.int32, (blocks, 128), 1) < CAP

    def put(r, left, right):
        value = jnp.concatenate([left, right], axis=1)
        high = value.astype(jnp.bfloat16)
        split[blocks * r : blocks * (r + 1), 0:256] = high
        split[blocks * r : blocks * (r + 1), 256:512] = (value - high.astype(jnp.float32)).astype(
            jnp.bfloat16
        )

    for r in range(8):
        plain = [recv_c[pl.ds(8 * c + r, blocks, stride=32), :] for c in range(4)]
        moved = [pltpu.roll(x, CAP, 1) for x in plain]
        put(r, jnp.where(low, plain[0], moved[1]), jnp.where(low, plain[2], moved[3]))
        if r >= 3:
            put(r + 5, jnp.where(low, moved[0], plain[1]), jnp.where(low, moved[2], plain[3]))

    which = lax.broadcasted_iota(jnp.int32, (blocks, 512), 0)

    def select(x, carry):
        slot = jnp.maximum(slot_ref[pl.ds(x, 1), :], 0)
        found = jnp.dot(
            split[...], jnp.concatenate([hot[x], hot[x]], axis=0), preferred_element_type=jnp.float32
        )
        match = which == (slot >> 8)
        for r in range(13):
            piece = jnp.where(match, found[blocks * r : blocks * (r + 1)], 0.0)
            records[r, pl.ds(x, 1), :] = jnp.sum(piece, axis=0, keepdims=True)
        return carry

    lax.fori_loop(0, 16, select, 0, unroll=2)
    loads[4].wait()

    sunlight, air, humidity, rainfall = (forcing_ref[i] for i in range(4))
    leaf, albedo, resist = (records[i] for i in range(3))
    total, roots = jnp.zeros_like(leaf), jnp.zeros_like(leaf)
    for k in range(layers):
        total = total + records[3 + k] * wet[k]
        roots = roots + records[3 + k]
    conductance = total / roots * leaf / (leaf + resist)
    exchange_coef = 0.5 + 0.3 * leaf
    radiation = (1.0 - albedo) * sunlight + 0.3
    surface = air
    for _ in range(2):
        vapour = 0.5 * jnp.exp(2.0 * (surface - air))
        square = surface * surface
        excess = (
            radiation
            - 0.3 * square * square
            - exchange_coef * (surface - air)
            - conductance * (vapour - humidity)
        )
        tangent = -1.2 * square * surface - exchange_coef - 2.0 * conductance * vapour
        surface = surface - excess / tangent
    evaporation = conductance * (0.5 * jnp.exp(2.0 * (surface - air)) - humidity)
    ks_top = own(ksat, 0)
    infiltration = rainfall * ks_top / (rainfall + ks_top)
    land = slot_ref[...] >= 0
    evaporation = jnp.where(land, evaporation, 0.0)
    infiltration = jnp.where(land, infiltration, 0.0)
    flux_ref[0] = evaporation
    flux_ref[1] = infiltration
    share = evaporation / total
    for k in range(layers):
        gain = -jnp.where(land, share * records[3 + k] * wet[k], 0.0)
        if k == 0:
            gain = gain + infiltration
        source[k] = gain
        basis[0, k, 0:16, 0:512] -= gain

    def fold(product):
        tall = product[0:8] + product[8:16]
        return (tall[:, 0:128] + tall[:, 128:256]) + (tall[:, 256:384] + tall[:, 384:512])

    lane1 = lax.broadcasted_iota(jnp.int32, (1, 128), 1)

    def place(partial, at, sums):
        for i, value in enumerate(sums):
            line = jnp.sum(value, axis=0, keepdims=True)
            partial = jnp.where(lane1 == at + i, jnp.sum(line, axis=1, keepdims=True), partial)
        return partial

    def matvec(j):
        rows, lanes = (slice(0, ROWS), slice(0, LANES)) if j + 1 < KRYLOV else (slice(0, 16), slice(0, 512))

        def layer(k, carry):
            v = basis[j, k]
            below, above = around(k)

            def term(i, value):
                return coef[i, k, rows, lanes] * value[rows, lanes]

            w = term(0, v)
            w = w + term(1, ahead(v, 0)) + term(2, behind(v, 0))
            w = w + term(3, ahead(v, 1)) + term(4, behind(v, 1))
            w = w + coef[5, k, rows, lanes] * basis[j, below, rows, lanes]
            w = w + coef[6, k, rows, lanes] * basis[j, above, rows, lanes]
            if j + 1 < KRYLOV:
                basis[j + 1, k] = w
            mine = w[0:16, 0:512]
            sums = [fold(mine * basis[i, k, 0:16, 0:512]) for i in range(j + 1)]
            sums.append(fold(mine * mine))
            return tuple(a + b for a, b in zip(carry, sums))

        zeros = tuple(jnp.zeros((8, 128), jnp.float32) for _ in range(j + 2))
        return lax.fori_loop(0, layers, layer, zeros, unroll=2)

    def square_of_start():
        def layer(k, carry):
            value = basis[0, k, 0:16, 0:512]
            return carry + fold(value * value)

        return [lax.fori_loop(0, layers, layer, jnp.zeros((8, 128), jnp.float32))]

    def reduce_all(n, partial):
        def along(stage, value, gather, sem, here, size, target):
            mine = part.at[n, stage]
            mine[...] = value
            gather[n, here] = value
            for i in range(1, size):
                pltpu.make_async_remote_copy(
                    src_ref=mine,
                    dst_ref=gather.at[n, here],
                    send_sem=sem.at[0, n],
                    recv_sem=sem.at[1, n],
                    device_id=target(lax.rem(here + i, size)),
                    device_id_type=MESH,
                ).start()
            rest = gather.at[n, pl.ds(0, size - 1)]
            pltpu.make_async_copy(rest, rest, sem.at[1, n]).wait()
            total = gather[n, 0]
            for i in range(1, size):
                total = total + gather[n, i]
            return total

        partial = along(0, partial, gather_x, sem_gx, gx, size_x, lambda d: (d, gy))
        return along(1, partial, gather_y, sem_gy, gy, size_y, lambda d: (gx, d))

    for n in range(NEWTON):
        field = [(basis, (0,))]
        moves = start(1 + n, 2 + n, field)
        partial = place(jnp.zeros((1, 128), jnp.float32), 0, square_of_start())
        if n:
            finish(head_moves, 4, [(head, ())])
            saturate_again()
            linearize()
        finish(moves, 2 + n, field)
        for j, at in ((0, 1), (1, 3), (2, 6)):
            partial = place(partial, at, matvec(j))
        sums = reduce_all(n, partial)
        gram = [[None] * 4 for _ in range(4)]
        at = 0
        for i in range(4):
            for j in range(i + 1):
                gram[i][j] = gram[j][i] = jnp.broadcast_to(sums[:, at : at + 1], (1, 128))
                at += 1
        weights = [w[:, 0:1] for w in krylov_weights(gram)]
        last = n + 1 == NEWTON
        rows, lanes = (slice(0, 16), slice(0, 512)) if last else (slice(0, ROWS), slice(0, LANES))

        def update(k, carry):
            value = head[k, rows, lanes]
            for i in range(KRYLOV):
                value = value - weights[i] * basis[i, k, rows, lanes]
            if last:
                out_ref[k] = value
            else:
                head[k] = value
            return carry

        lax.fori_loop(0, layers, update, 0)
        if not last:
            head_moves = start(3, 4, [(head, ())])
            saturate(False)
            balance()

    sent = send_c.at[pl.ds(0, devices - 1)]
    pltpu.make_async_copy(sent, sent, sem_c.at[0]).wait()
    for n in range(NEWTON):
        sent = gather_x.at[n, pl.ds(0, size_x - 1)]
        pltpu.make_async_copy(sent, sent, sem_gx.at[0, n]).wait()
        sent = gather_y.at[n, pl.ds(0, size_y - 1)]
        pltpu.make_async_copy(sent, sent, sem_gy.at[0, n]).wait()


def shards(sizes, head_old, soil_type, soil_table, forcing, canopy, column_slot):
    layers = head_old.shape[0]
    devices = sizes[0] * sizes[1]
    f32 = jnp.float32
    wide = (layers, ROWS, LANES)
    tile = (layers, 16, 512)
    vmem, anywhere = pl.BlockSpec(memory_space=pltpu.VMEM), pl.BlockSpec(memory_space=pl.ANY)
    return pl.pallas_call(
        functools.partial(kernel, sizes),
        out_shape=(
            jax.ShapeDtypeStruct(head_old.shape, f32),
            jax.ShapeDtypeStruct((2, 16, 512), f32),
        ),
        in_specs=[anywhere, anywhere, pl.BlockSpec(memory_space=pltpu.SMEM)] + [anywhere] * 3,
        out_specs=(vmem, vmem),
        scratch_shapes=[
            pltpu.VMEM(tile, jnp.int32),
            pltpu.VMEM(forcing.shape, f32),
            pltpu.VMEM(canopy.shape, f32),
            pltpu.VMEM(column_slot.shape, jnp.int32),
            pltpu.VMEM((devices, 8, 128), f32),
            pltpu.VMEM((devices * 8, 128), f32),
            pltpu.VMEM((13 * (devices // 4), 512), jnp.bfloat16),
            pltpu.VMEM((16, 256, 512), jnp.bfloat16),
            pltpu.VMEM((13, 16, 512), f32),
            pltpu.VMEM(wide, f32),
            pltpu.VMEM(wide, f32),
            pltpu.VMEM(wide, f32),
            pltpu.VMEM(wide, f32),
            pltpu.VMEM(wide, f32),
            pltpu.VMEM(wide, f32),
            pltpu.VMEM(wide, f32),
            pltpu.VMEM((7,) + wide, f32),
            pltpu.VMEM((KRYLOV,) + wide, f32),
            pltpu.VMEM(tile, f32),
            pltpu.VMEM(tile, f32),
            pltpu.VMEM(tile, f32),
            pltpu.VMEM((ROWS, LANES), f32),
            pltpu.VMEM((2, 5, 32, 512), f32),
            pltpu.VMEM((2, 5, 32, 512), f32),
            pltpu.VMEM((2, 5, 16, 128), f32),
            pltpu.VMEM((2, 5, 16, 128), f32),
            pltpu.VMEM((2, 2, 5, 8, 128), f32),
            pltpu.VMEM((NEWTON, 2, 1, 128), f32),
            pltpu.VMEM((NEWTON, sizes[0], 1, 128), f32),
            pltpu.VMEM((NEWTON, sizes[1], 1, 128), f32),
            pltpu.SemaphoreType.DMA((5,)),
            pltpu.SemaphoreType.DMA((2,)),
            pltpu.SemaphoreType.DMA((2, 4, 8)),
            pltpu.SemaphoreType.DMA((2, NEWTON)),
            pltpu.SemaphoreType.DMA((2, NEWTON)),
        ],
        compiler_params=pltpu.CompilerParams(collective_id=0, has_side_effects=True),
        name="coupled_step",
    )(head_old, soil_type, soil_table, forcing, canopy, column_slot)


def solution(mesh):
    sizes = (mesh.shape["gx"], mesh.shape["gy"])
    return jax.shard_map(
        functools.partial(shards, sizes),
        mesh=mesh,
        in_specs=(
            P(None, "gx", "gy"),
            P(None, "gx", "gy"),
            P(),
            P(None, "gx", "gy"),
            P(None, ("gx", "gy")),
            P("gx", "gy"),
        ),
        out_specs=(P(None, "gx", "gy"), P(None, "gx", "gy")),
        check_vma=False,
    )
```

```python
import functools

import jax
import jax.numpy as jnp
from jax import lax
from jax.experimental import pallas as pl
from jax.experimental.pallas import tpu as pltpu
from jax.sharding import PartitionSpec as P

NEWTON = 2
KRYLOV = 3
CAP = 64

STORAGE = 4.0
EPSILON = 1e-06

SHIFT = 3.0
SCALE = 3.0

MESH = pl.DeviceIdType.MESH
OWN = (slice(0, 16), slice(0, 512))
RIM = ((slice(16, 24), slice(0, 512)), (slice(0, 24), slice(512, 640)))
HALO = 3
ROWS = 24
LANES = 640


def logistic(u):
    return 1.0 / (1.0 + jnp.exp(-u))


def ahead(x, axis):
    return pltpu.roll(x, x.shape[axis] - 1, axis)


def behind(x, axis):
    return pltpu.roll(x, 1, axis)


def krylov_weights(gram):
    def inner(vector, image):
        terms = [a * b for a, b in zip(vector, image) if a is not None]
        return functools.reduce(lambda a, b: a + b, terms)

    def image_of(vector):
        return [inner(vector, [gram[i][k] for i in range(4)]) for k in range(4)]

    beta = jnp.sqrt(gram[0][0] + EPSILON)
    basis = [[1.0 / beta, None, None, None]]
    images = [image_of(basis[0])]
    hessen = [[None] * KRYLOV for _ in range(KRYLOV + 1)]
    for j in range(KRYLOV):
        v = basis[j]
        w = [None] * 4
        for i in range(j + 2):
            if i <= j:
                w[i] = SHIFT * v[i]
            if i >= 1:
                term = SCALE * v[i - 1]
                w[i] = term if w[i] is None else w[i] + term
        for i in range(j + 1):
            product = inner(w, images[i])
            hessen[i][j] = product
            w = [a if b is None else a - product * b for a, b in zip(w, basis[i])]
        square = jnp.maximum(inner(w, image_of(w)), 0.0)
        length = jnp.sqrt(square + EPSILON)
        hessen[j + 1][j] = length
        if j + 1 < KRYLOV:
            basis.append([None if a is None else a / length for a in w])
            images.append(image_of(basis[-1]))

    def column(a, b):
        pairs = [(hessen[i][a], hessen[i][b]) for i in range(KRYLOV + 1)]
        terms = [x * y for x, y in pairs if x is not None and y is not None]
        return functools.reduce(lambda x, y: x + y, terms)

    factor = [[None] * KRYLOV for _ in range(KRYLOV)]
    for i in range(KRYLOV):
        for j in range(i + 1):
            value = column(i, j)
            for k in range(j):
                value = value - factor[i][k] * factor[j][k]
            factor[i][j] = jnp.sqrt(value) if i == j else value / factor[j][j]
    forward = []
    for row in range(KRYLOV):
        value = hessen[0][row] * beta
        for other in range(row):
            value = value - factor[row][other] * forward[other]
        forward.append(value / factor[row][row])
    y = [None] * KRYLOV
    for row in reversed(range(KRYLOV)):
        value = forward[row]
        for other in range(row + 1, KRYLOV):
            value = value - factor[other][row] * y[other]
        y[row] = value / factor[row][row]
    weights = []
    for i in range(KRYLOV):
        terms = [y[j] * basis[j][i] for j in range(KRYLOV) if basis[j][i] is not None]
        weights.append(functools.reduce(lambda a, b: a + b, terms))
    return weights


def kernel(
    sizes,
    head_in,
    soil_in,
    table_in,
    forcing_in,
    canopy_in,
    slot_in,
    out_ref,
    flux_ref,
    table_ref,
    soil_ref,
    forcing_ref,
    canopy_ref,
    slot_ref,
    send_c,
    recv_c,
    split,
    hot,
    records,
    head,
    soil,
    conduct,
    slope,
    ksat,
    steep,
    cap,
    coef,
    basis,
    wet,
    theta_old,
    source,
    mask,
    send_x,
    recv_x,
    send_y,
    recv_y,
    recv_k,
    part,
    gather_x,
    gather_y,
    sem_in,
    sem_c,
    sem_e,
    sem_gx,
    sem_gy,
):
    size_x, size_y = sizes
    devices = size_x * size_y
    layers = out_ref.shape[0]
    gx, gy = lax.axis_index("gx"), lax.axis_index("gy")
    me = gx * size_y + gy

    loads = [
        pltpu.make_async_copy(src, dst, sem_in.at[i])
        for i, (src, dst) in enumerate(
            (
                (canopy_in, canopy_ref),
                (head_in, head.at[:, 0:16, 0:512]),
                (soil_in, soil_ref),
                (slot_in, slot_ref),
                (forcing_in, forcing_ref),
                (table_in, table_ref),
            )
        )
    ]
    for load in loads:
        load.start()

    def wrap(value, size):
        return lax.rem(value + size, size)

    def others(visit):
        for dy in range(1, size_y):
            visit(gx, lax.rem(gy + dy, size_y))

        def ring(i, carry):
            far = (i + 1) // 2
            x = wrap(gx + jnp.where(lax.rem(i, 2) == 1, far, -far), size_x)
            for dy in range(size_y):
                visit(x, lax.rem(gy + dy, size_y))
            return carry

        lax.fori_loop(1, size_x, ring, 0)

    barrier = pltpu.get_barrier_semaphore()
    others(lambda x, y: pl.semaphore_signal(barrier, inc=1, device_id=(x, y), device_id_type=MESH))

    row = lax.broadcasted_iota(jnp.int32, (ROWS, LANES), 0)
    col = lax.broadcasted_iota(jnp.int32, (ROWS, LANES), 1)
    one, zero = jnp.float32(1.0), jnp.float32(0.0)
    has_next_x = jnp.where(gx < size_x - 1, one, zero)
    has_prev_x = jnp.where(gx > 0, one, zero)
    has_next_y = jnp.where(gy < size_y - 1, one, zero)
    has_prev_y = jnp.where(gy > 0, one, zero)
    inside_x = jnp.where(
        row < 16,
        1.0,
        jnp.where(row < 16 + HALO, has_next_x, jnp.where(row >= ROWS - HALO, has_prev_x, 0.0)),
    )
    inside_y = jnp.where(
        col < 512,
        1.0,
        jnp.where(col < 512 + HALO, has_next_y, jnp.where(col >= LANES - HALO, has_prev_y, 0.0)),
    )
    mask[...] = inside_x * inside_y

    def own(ref, k):
        return ref[k, 0:16, 0:512]

    def clear(k, carry):
        for ref in (head, soil, basis.at[0]):
            ref[k, 16:24, 0:512] = jnp.zeros((8, 512), jnp.float32)
            ref[k, 0:24, 512:640] = jnp.zeros((24, 128), jnp.float32)
        return carry

    lax.fori_loop(0, layers, clear, 0)
    for side in range(2):
        for slot in range(5):
            send_x[side, slot, 24:32, :] = jnp.zeros((8, 512), jnp.float32)

    low7 = lax.broadcasted_iota(jnp.int32, (7, 128), 1) < CAP

    def pack(q, carry):
        lanes = pl.ds(pl.multiple_of(q * 128, 128), 128)
        first, second = canopy_ref[0:7, lanes], canopy_ref[6:13, lanes]
        send_c[2 * q, 0:7] = jnp.where(low7, first, pltpu.roll(second, CAP, 1))
        send_c[2 * q + 1, 0:7] = jnp.where(low7, pltpu.roll(first, CAP, 1), second)
        return carry

    loads[0].wait()
    lax.fori_loop(0, devices // 2, pack, 0, unroll=4)
    quarter = size_x // 4

    def seat(x):
        return lax.rem(gx - x + quarter + size_x, size_x)

    def slab(x):
        return pl.ds(pl.multiple_of((seat(x) * size_y + gy) * 8, 8), 7)

    recv_c[slab(gx), :] = send_c[me, 0:7]

    next_x, prev_x = wrap(gx + 1, size_x), wrap(gx - 1, size_x)
    next_y, prev_y = wrap(gy + 1, size_y), wrap(gy - 1, size_y)
    lane16 = lax.broadcasted_iota(jnp.int32, (16, 128), 1)
    group16 = lane16 // 4
    lane24 = lax.broadcasted_iota(jnp.int32, (ROWS, 128), 1)
    early8 = lax.broadcasted_iota(jnp.int32, (8, 128), 0) < 4

    def start(number, slot, fields):
        for f, (ref, index) in enumerate(fields):
            up = jnp.zeros((16, 128), jnp.float32)
            down = jnp.zeros((16, 128), jnp.float32)
            for k in range(layers):
                rows = slice(HALO * k, HALO * (k + 1))
                send_x[0, slot + f, rows, :] = ref[index + (k, slice(16 - HALO, 16), slice(0, 512))]
                send_x[1, slot + f, rows, :] = ref[index + (k, slice(0, HALO), slice(0, 512))]
                last = ref[index + (k, slice(0, 16), slice(384, 512))]
                first = ref[index + (k, slice(0, 16), slice(0, 128))]
                here = group16 == k
                up = jnp.where(here, pltpu.roll(last, 4 * k + 4, 1), up)
                down = jnp.where(here, pltpu.roll(first, 4 * k, 1) if k else first, down)
            send_y[0, slot + f] = up
            send_y[1, slot + f] = down
        slots = pl.ds(slot, len(fields))
        plan = []
        for side, y in enumerate((next_y, prev_y)):
            for turn, x in enumerate((next_x, prev_x)):
                edge = pl.ds(8 * (1 - turn), 8)
                plan.append(
                    (send_y.at[side, slots, edge], recv_k.at[side, turn, slots], (x, y))
                )
        for side, x in enumerate((next_x, prev_x)):
            plan.append((send_x.at[side, slots], recv_x.at[side, slots], (x, gy)))
        for side, y in enumerate((next_y, prev_y)):
            plan.append((send_y.at[side, slots], recv_y.at[side, slots], (gx, y)))
        moves = [
            pltpu.make_async_remote_copy(
                src_ref=src,
                dst_ref=dst,
                send_sem=sem_e.at[0, number, i],
                recv_sem=sem_e.at[1, number, i],
                device_id=target,
                device_id_type=MESH,
            )
            for i, (src, dst, target) in enumerate(plan)
        ]
        for move in moves:
            move.start()
        return moves

    def finish(moves, slot, fields):
        for move in moves[6:] + moves[:4]:
            move.wait()
        edge = mask[:, 512:640]
        for f, (ref, index) in enumerate(fields):
            sides = [
                jnp.concatenate(
                    [
                        recv_y[side, slot + f],
                        jnp.where(early8, recv_k[side, 1, slot + f], recv_k[side, 0, slot + f]),
                    ],
                    axis=0,
                )
                for side in range(2)
            ]
            for k in range(layers):
                left = pltpu.roll(sides[0], 128 - (4 * k + 4), 1)
                right = pltpu.roll(sides[1], 128 - 4 * k, 1) if k else sides[1]
                both = jnp.where(lane24 < 64, right, left)
                ref[index + (k, slice(0, ROWS), slice(512, 640))] = jnp.where(edge > 0.0, both, 0.0)
        for move in moves[4:6]:
            move.wait()
        for f, (ref, index) in enumerate(fields):
            for k in range(layers):
                rows = slice(HALO * k, HALO * (k + 1))
                after = recv_x[1, slot + f, rows, :] * has_next_x
                before = recv_x[0, slot + f, rows, :] * has_prev_x
                ref[index + (k, slice(16, 16 + HALO), slice(0, 512))] = after
                ref[index + (k, slice(ROWS - HALO, ROWS), slice(0, 512))] = before

    loads[1].wait()
    loads[2].wait()

    def convert(k, carry):
        soil[k, 0:16, 0:512] = soil_ref[k].astype(jnp.float32)
        return carry

    lax.fori_loop(0, layers, convert, 0)

    pl.semaphore_wait(barrier, devices - 1)

    def scatter(x, y):
        pltpu.make_async_remote_copy(
            src_ref=send_c.at[x * size_y + y, pl.ds(0, 7)],
            dst_ref=recv_c.at[slab(x)],
            send_sem=sem_c.at[0],
            recv_sem=sem_c.at[1 + seat(x) // (size_x // 2)],
            device_id=(x, y),
            device_id_type=MESH,
        ).start()

    opening = [(head, ()), (soil, ())]
    moves = start(0, 0, opening)
    others(scatter)

    def look_up(rows, lanes):
        def layer(k, carry):
            kind = soil[k, rows, lanes]
            values = [jnp.zeros(kind.shape, jnp.float32) for _ in range(3)]
            for c in range(table_ref.shape[1]):
                match = kind == float(c)
                values = [jnp.where(match, table_ref[p, c], v) for p, v in enumerate(values)]
            ksat[k, rows, lanes] = values[0] * mask[rows, lanes]
            steep[k, rows, lanes] = values[1]
            cap[k, rows, lanes] = values[2]
            return carry

        lax.fori_loop(0, layers, layer, 0)

    loads[5].wait()
    look_up(*OWN)

    def saturate(rows, lanes, keep):
        def layer(k, carry):
            a, ks, c = (ref[k, rows, lanes] for ref in (steep, ksat, cap))
            s = logistic(a * head[k, rows, lanes])
            rise = a * s * (1.0 - s)
            conduct[k, rows, lanes] = ks * (0.1 + 0.9 * s * s)
            slope[k, rows, lanes] = 0.9 * ks * s * rise
            coef[0, k, rows, lanes] = STORAGE * c * rise
            keep(k, s, c)
            return carry

        lax.fori_loop(0, layers, layer, 0, unroll=2)

    def keep_old(k, s, c):
        wet[k] = s
        theta_old[k] = c * s

    def keep_residual(k, s, c):
        basis[0, k, 0:16, 0:512] = STORAGE * (c * s - theta_old[k]) - source[k]

    def keep_none(k, s, c):
        pass

    saturate(*OWN, keep_old)

    loads[3].wait()
    within = lax.broadcasted_iota(jnp.int32, (256, 512), 0)

    def seats_of(x):
        slot = jnp.maximum(slot_ref[pl.ds(x, 1), :], 0)
        shift = (size_y * CAP).bit_length() - 1
        seat = ((slot >> shift) - gx + quarter) & (size_x - 1)
        return (seat << shift) + (slot & (size_y * CAP - 1))

    def spot(x, carry):
        slot = seats_of(x)
        hot[x] = jnp.where(within == (slot & 255), 1.0, 0.0).astype(jnp.bfloat16)
        return carry

    lax.fori_loop(0, 16, spot, 0)

    blocks = devices // 8
    low = lax.broadcasted_iota(jnp.int32, (blocks, 128), 1) < CAP
    which = lax.broadcasted_iota(jnp.int32, (blocks, 512), 0)

    def choose(part_of):
        arrived = send_c.at[pl.ds(0, devices // 2 - (1 - part_of)), pl.ds(0, 7)]
        pltpu.make_async_copy(arrived, arrived, sem_c.at[1 + part_of]).wait()

        def put(r, left, right):
            value = jnp.concatenate([left, right], axis=1)
            high = value.astype(jnp.bfloat16)
            rows = slice(blocks * r, blocks * (r + 1))
            split[rows, 0:256] = high
            split[rows, 256:512] = (value - high.astype(jnp.float32)).astype(jnp.bfloat16)

        for r in range(7):
            first = 32 * blocks * part_of + r
            plain = [recv_c[pl.ds(first + 8 * c, blocks, stride=32), :] for c in range(4)]
            moved = [pltpu.roll(x, CAP, 1) for x in plain]
            put(r, jnp.where(low, plain[0], moved[1]), jnp.where(low, plain[2], moved[3]))
            if r >= 1:
                put(r + 6, jnp.where(low, moved[0], plain[1]), jnp.where(low, moved[2], plain[3]))

        def select(x, carry):
            found = jnp.dot(
                split[...], jnp.concatenate([hot[x], hot[x]], axis=0), preferred_element_type=jnp.float32
            )
            match = which == (seats_of(x) >> 8) - blocks * part_of
            for r in range(13):
                piece = jnp.where(match, found[blocks * r : blocks * (r + 1)], 0.0)
                value = jnp.sum(piece, axis=0, keepdims=True)
                if part_of:
                    value = value + records[r, pl.ds(x, 1), :]
                records[r, pl.ds(x, 1), :] = value
            return carry

        lax.fori_loop(0, 16, select, 0, unroll=2)

    choose(0)
    finish(moves, 0, opening)
    for region in RIM:
        look_up(*region)

    def around(k):
        return jnp.minimum(k + 1, layers - 1), jnp.maximum(k - 1, 0)

    def balance():
        def layer(k, carry):
            h, kk = head[k], conduct[k]
            total = basis[0, k, 0:16, 0:512]
            for axis in range(2):
                flow = 0.5 * (kk + ahead(kk, axis)) * (h - ahead(h, axis))
                total = total + (flow - behind(flow, axis))[0:16, 0:512]
            below, above = around(k)
            h, kk = own(head, k), own(conduct, k)
            flow = 0.5 * (kk + own(conduct, below)) * (h - own(head, below) + 1.0)
            total = total + jnp.where(k == layers - 1, kk, flow)
            flow = 0.5 * (own(conduct, above) + kk) * (own(head, above) - h + 1.0)
            basis[0, k, 0:16, 0:512] = total - jnp.where(k == 0, 0.0, flow)
            return carry

        lax.fori_loop(0, layers, layer, 0, unroll=2)

    def linearize(rows, lanes, flows=False):
        def at(x):
            return x[rows, lanes]

        def layer(k, carry):
            scaled = mask[rows, lanes] * (1.0 / SCALE)
            h, kk, dk = head[k], conduct[k], slope[k]
            diagonal = coef[0, k, rows, lanes] - SHIFT
            total = None
            for axis, i in ((0, 1), (1, 3)):
                drop = h - ahead(h, axis)
                mean = 0.5 * (kk + ahead(kk, axis))
                mine = dk * drop + mean
                other = ahead(dk, axis) * drop - mean
                diagonal = diagonal + at(mine) - at(behind(other, axis))
                coef[i, k, rows, lanes] = at(other) * scaled
                coef[i + 1, k, rows, lanes] = -at(behind(mine, axis)) * scaled
                if flows:
                    flow = mean * drop
                    net = at(flow) - at(behind(flow, axis))
                    total = net if total is None else total + net
            below, above = around(k)
            bottom, top = k == layers - 1, k == 0
            h, kk, dk = at(h), at(kk), at(dk)
            drop = h - head[below, rows, lanes] + 1.0
            mean = 0.5 * (kk + conduct[below, rows, lanes])
            diagonal = diagonal + jnp.where(bottom, 2.0 * dk, dk * drop + mean)
            coef[5, k, rows, lanes] = (
                jnp.where(bottom, 0.0, slope[below, rows, lanes] * drop - mean) * scaled
            )
            if flows:
                total = total + jnp.where(bottom, kk, mean * drop)
            drop = head[above, rows, lanes] - h + 1.0
            mean = 0.5 * (kk + conduct[above, rows, lanes])
            diagonal = diagonal - jnp.where(top, 0.0, dk * drop - mean)
            coef[6, k, rows, lanes] = (
                -jnp.where(top, 0.0, slope[above, rows, lanes] * drop + mean) * scaled
            )
            if flows:
                basis[0, k, rows, lanes] = total - jnp.where(top, 0.0, mean * drop)
            coef[0, k, rows, lanes] = diagonal * scaled
            return carry

        lax.fori_loop(0, layers, layer, 0)

    for region in RIM:
        saturate(*region, keep_none)
    linearize(*OWN, flows=True)
    for region in RIM:
        linearize(*region)

    choose(1)
    loads[4].wait()
    sunlight, air, humidity, rainfall = (forcing_ref[i] for i in range(4))
    leaf, albedo, resist = (records[i] for i in range(3))
    total, roots = jnp.zeros_like(leaf), jnp.zeros_like(leaf)
    for k in range(layers):
        total = total + records[3 + k] * wet[k]
        roots = roots + records[3 + k]
    conductance = total / roots * leaf / (leaf + resist)
    exchange_coef = 0.5 + 0.3 * leaf
    radiation = (1.0 - albedo) * sunlight + 0.3
    surface = air
    for _ in range(2):
        vapour = 0.5 * jnp.exp(2.0 * (surface - air))
        square = surface * surface
        excess = (
            radiation
            - 0.3 * square * square
            - exchange_coef * (surface - air)
            - conductance * (vapour - humidity)
        )
        tangent = -1.2 * square * surface - exchange_coef - 2.0 * conductance * vapour
        surface = surface - excess / tangent
    evaporation = conductance * (0.5 * jnp.exp(2.0 * (surface - air)) - humidity)
    ks_top = own(ksat, 0)
    infiltration = rainfall * ks_top / (rainfall + ks_top)
    land = slot_ref[...] >= 0
    evaporation = jnp.where(land, evaporation, 0.0)
    infiltration = jnp.where(land, infiltration, 0.0)
    flux_ref[0] = evaporation
    flux_ref[1] = infiltration
    share = evaporation / total
    for k in range(layers):
        gain = -jnp.where(land, share * records[3 + k] * wet[k], 0.0)
        if k == 0:
            gain = gain + infiltration
        source[k] = gain
        basis[0, k, 0:16, 0:512] -= gain

    def fold(product):
        tall = product[0:8] + product[8:16]
        return (tall[:, 0:128] + tall[:, 128:256]) + (tall[:, 256:384] + tall[:, 384:512])

    lane1 = lax.broadcasted_iota(jnp.int32, (1, 128), 1)

    def place(partial, at, sums):
        for i, value in enumerate(sums):
            line = jnp.sum(value, axis=0, keepdims=True)
            partial = jnp.where(lane1 == at + i, jnp.sum(line, axis=1, keepdims=True), partial)
        return partial

    def matvec(j):
        rows, lanes = (slice(0, ROWS), slice(0, LANES)) if j + 1 < KRYLOV else (slice(0, 16), slice(0, 512))

        def layer(k, carry):
            v = basis[j, k]
            below, above = around(k)

            def term(i, value):
                return coef[i, k, rows, lanes] * value[rows, lanes]

            w = term(0, v)
            w = w + term(1, ahead(v, 0)) + term(2, behind(v, 0))
            w = w + term(3, ahead(v, 1)) + term(4, behind(v, 1))
            w = w + coef[5, k, rows, lanes] * basis[j, below, rows, lanes]
            w = w + coef[6, k, rows, lanes] * basis[j, above, rows, lanes]
            if j + 1 < KRYLOV:
                basis[j + 1, k] = w
            mine = w[0:16, 0:512]
            sums = [fold(mine * basis[i, k, 0:16, 0:512]) for i in range(j + 1)]
            sums.append(fold(mine * mine))
            return tuple(a + b for a, b in zip(carry, sums))

        zeros = tuple(jnp.zeros((8, 128), jnp.float32) for _ in range(j + 2))
        return lax.fori_loop(0, layers, layer, zeros, unroll=2)

    def square_of_start():
        def layer(k, carry):
            value = basis[0, k, 0:16, 0:512]
            return carry + fold(value * value)

        return [lax.fori_loop(0, layers, layer, jnp.zeros((8, 128), jnp.float32))]

    def reduce_all(n, partial):
        def along(stage, value, gather, sem, here, size, target):
            mine = part.at[n, stage]
            mine[...] = value
            gather[n, here] = value
            for i in range(1, size):
                pltpu.make_async_remote_copy(
                    src_ref=mine,
                    dst_ref=gather.at[n, here],
                    send_sem=sem.at[0, n],
                    recv_sem=sem.at[1, n],
                    device_id=target(lax.rem(here + i, size)),
                    device_id_type=MESH,
                ).start()
            rest = gather.at[n, pl.ds(0, size - 1)]
            pltpu.make_async_copy(rest, rest, sem.at[1, n]).wait()
            total = gather[n, 0]
            for i in range(1, size):
                total = total + gather[n, i]
            return total

        partial = along(0, partial, gather_x, sem_gx, gx, size_x, lambda d: (d, gy))
        return along(1, partial, gather_y, sem_gy, gy, size_y, lambda d: (gx, d))

    for n in range(NEWTON):
        field = [(basis, (0,))]
        moves = start(1 + n, 2 + n, field)
        partial = place(jnp.zeros((1, 128), jnp.float32), 0, square_of_start())
        if n:
            linearize(*OWN)
            finish(head_moves, 4, [(head, ())])
            for region in RIM:
                saturate(*region, keep_none)
            for region in RIM:
                linearize(*region)
        finish(moves, 2 + n, field)
        for j, at in ((0, 1), (1, 3), (2, 6)):
            partial = place(partial, at, matvec(j))
        sums = reduce_all(n, partial)
        gram = [[None] * 4 for _ in range(4)]
        at = 0
        for i in range(4):
            for j in range(i + 1):
                gram[i][j] = gram[j][i] = jnp.broadcast_to(sums[:, at : at + 1], (1, 128))
                at += 1
        weights = [w[:, 0:1] for w in krylov_weights(gram)]
        last = n + 1 == NEWTON
        rows, lanes = (slice(0, 16), slice(0, 512)) if last else (slice(0, ROWS), slice(0, LANES))

        def update(k, carry):
            value = head[k, rows, lanes]
            for i in range(KRYLOV):
                value = value - weights[i] * basis[i, k, rows, lanes]
            if last:
                out_ref[k] = value
            else:
                head[k] = value
            return carry

        lax.fori_loop(0, layers, update, 0)
        if not last:
            head_moves = start(3, 4, [(head, ())])
            saturate(*OWN, keep_residual)
            for region in RIM:
                saturate(*region, keep_none)
            balance()

    sent = send_c.at[pl.ds(0, devices - 1), pl.ds(0, 7)]
    pltpu.make_async_copy(sent, sent, sem_c.at[0]).wait()
    for n in range(NEWTON):
        sent = gather_x.at[n, pl.ds(0, size_x - 1)]
        pltpu.make_async_copy(sent, sent, sem_gx.at[0, n]).wait()
        sent = gather_y.at[n, pl.ds(0, size_y - 1)]
        pltpu.make_async_copy(sent, sent, sem_gy.at[0, n]).wait()


def shards(sizes, head_old, soil_type, soil_table, forcing, canopy, column_slot):
    layers = head_old.shape[0]
    devices = sizes[0] * sizes[1]
    f32 = jnp.float32
    wide = (layers, ROWS, LANES)
    tile = (layers, 16, 512)
    vmem, hbm = pl.BlockSpec(memory_space=pltpu.VMEM), pl.BlockSpec(memory_space=pltpu.HBM)
    return pl.pallas_call(
        functools.partial(kernel, sizes),
        out_shape=(
            jax.ShapeDtypeStruct(head_old.shape, f32),
            jax.ShapeDtypeStruct((2, 16, 512), f32),
        ),
        in_specs=[hbm] * 6,
        out_specs=(vmem, vmem),
        scratch_shapes=[
            pltpu.SMEM(soil_table.shape, f32),
            pltpu.VMEM(tile, jnp.int32),
            pltpu.VMEM(forcing.shape, f32),
            pltpu.VMEM(canopy.shape, f32),
            pltpu.VMEM(column_slot.shape, jnp.int32),
            pltpu.VMEM((devices, 8, 128), f32),
            pltpu.VMEM((devices * 8, 128), f32),
            pltpu.VMEM((13 * (devices // 8), 512), jnp.bfloat16),
            pltpu.VMEM((16, 256, 512), jnp.bfloat16),
            pltpu.VMEM((13, 16, 512), f32),
            pltpu.VMEM(wide, f32),
            pltpu.VMEM(wide, f32),
            pltpu.VMEM(wide, f32),
            pltpu.VMEM(wide, f32),
            pltpu.VMEM(wide, f32),
            pltpu.VMEM(wide, f32),
            pltpu.VMEM(wide, f32),
            pltpu.VMEM((7,) + wide, f32),
            pltpu.VMEM((KRYLOV,) + wide, f32),
            pltpu.VMEM(tile, f32),
            pltpu.VMEM(tile, f32),
            pltpu.VMEM(tile, f32),
            pltpu.VMEM((ROWS, LANES), f32),
            pltpu.VMEM((2, 5, 32, 512), f32),
            pltpu.VMEM((2, 5, 32, 512), f32),
            pltpu.VMEM((2, 5, 16, 128), f32),
            pltpu.VMEM((2, 5, 16, 128), f32),
            pltpu.VMEM((2, 2, 5, 8, 128), f32),
            pltpu.VMEM((NEWTON, 2, 1, 128), f32),
            pltpu.VMEM((NEWTON, sizes[0], 1, 128), f32),
            pltpu.VMEM((NEWTON, sizes[1], 1, 128), f32),
            pltpu.SemaphoreType.DMA((6,)),
            pltpu.SemaphoreType.DMA((3,)),
            pltpu.SemaphoreType.DMA((2, 4, 8)),
            pltpu.SemaphoreType.DMA((2, NEWTON)),
            pltpu.SemaphoreType.DMA((2, NEWTON)),
        ],
        compiler_params=pltpu.CompilerParams(
            collective_id=0, has_side_effects=True, vmem_limit_bytes=40 * 1024 * 1024
        ),
        name="coupled_step",
    )(head_old, soil_type, soil_table, forcing, canopy, column_slot)


def solution(mesh):
    sizes = (mesh.shape["gx"], mesh.shape["gy"])
    return jax.shard_map(
        functools.partial(shards, sizes),
        mesh=mesh,
        in_specs=(
            P(None, "gx", "gy"),
            P(None, "gx", "gy"),
            P(),
            P(None, "gx", "gy"),
            P(None, ("gx", "gy")),
            P("gx", "gy"),
        ),
        out_specs=(P(None, "gx", "gy"), P(None, "gx", "gy")),
        check_vma=False,
    )
```

```python
import functools

import jax
import jax.numpy as jnp
from jax import lax
from jax.experimental import pallas as pl
from jax.experimental.pallas import tpu as pltpu
from jax.sharding import PartitionSpec as P

NEWTON = 2
KRYLOV = 3
CAP = 64

STORAGE = 4.0
EPSILON = 1e-06

SHIFT = 3.0
SCALE = 3.0

MESH = pl.DeviceIdType.MESH
OWN = (slice(0, 16), slice(0, 512))
RIM = ((slice(16, 24), slice(0, 512)), (slice(0, 24), slice(512, 640)))
HALO = 3
ROWS = 24
LANES = 640


def logistic(u):
    return 1.0 / (1.0 + jnp.exp(-u))


def ahead(x, axis):
    return pltpu.roll(x, x.shape[axis] - 1, axis)


def behind(x, axis):
    return pltpu.roll(x, 1, axis)


def krylov_weights(gram):
    def inner(vector, image):
        terms = [a * b for a, b in zip(vector, image) if a is not None]
        return functools.reduce(lambda a, b: a + b, terms)

    def image_of(vector):
        return [inner(vector, [gram[i][k] for i in range(4)]) for k in range(4)]

    beta = jnp.sqrt(gram[0][0] + EPSILON)
    basis = [[1.0 / beta, None, None, None]]
    images = [image_of(basis[0])]
    hessen = [[None] * KRYLOV for _ in range(KRYLOV + 1)]
    for j in range(KRYLOV):
        v = basis[j]
        w = [None] * 4
        for i in range(j + 2):
            if i <= j:
                w[i] = SHIFT * v[i]
            if i >= 1:
                term = SCALE * v[i - 1]
                w[i] = term if w[i] is None else w[i] + term
        for i in range(j + 1):
            product = inner(w, images[i])
            hessen[i][j] = product
            w = [a if b is None else a - product * b for a, b in zip(w, basis[i])]
        square = jnp.maximum(inner(w, image_of(w)), 0.0)
        length = jnp.sqrt(square + EPSILON)
        hessen[j + 1][j] = length
        if j + 1 < KRYLOV:
            basis.append([None if a is None else a / length for a in w])
            images.append(image_of(basis[-1]))

    def column(a, b):
        pairs = [(hessen[i][a], hessen[i][b]) for i in range(KRYLOV + 1)]
        terms = [x * y for x, y in pairs if x is not None and y is not None]
        return functools.reduce(lambda x, y: x + y, terms)

    factor = [[None] * KRYLOV for _ in range(KRYLOV)]
    for i in range(KRYLOV):
        for j in range(i + 1):
            value = column(i, j)
            for k in range(j):
                value = value - factor[i][k] * factor[j][k]
            factor[i][j] = jnp.sqrt(value) if i == j else value / factor[j][j]
    forward = []
    for row in range(KRYLOV):
        value = hessen[0][row] * beta
        for other in range(row):
            value = value - factor[row][other] * forward[other]
        forward.append(value / factor[row][row])
    y = [None] * KRYLOV
    for row in reversed(range(KRYLOV)):
        value = forward[row]
        for other in range(row + 1, KRYLOV):
            value = value - factor[other][row] * y[other]
        y[row] = value / factor[row][row]
    weights = []
    for i in range(KRYLOV):
        terms = [y[j] * basis[j][i] for j in range(KRYLOV) if basis[j][i] is not None]
        weights.append(functools.reduce(lambda a, b: a + b, terms))
    return weights


def kernel(
    sizes,
    head_in,
    soil_in,
    table_in,
    forcing_in,
    canopy_in,
    slot_in,
    out_ref,
    flux_ref,
    table_ref,
    soil_ref,
    forcing_ref,
    canopy_ref,
    slot_ref,
    send_c,
    recv_c,
    split,
    hot,
    records,
    head,
    soil,
    conduct,
    slope,
    ksat,
    steep,
    cap,
    coef,
    basis,
    wet,
    theta_old,
    source,
    mask,
    send_x,
    recv_x,
    send_y,
    recv_y,
    recv_k,
    part,
    gather_x,
    gather_y,
    sem_in,
    sem_c,
    sem_e,
    sem_gx,
    sem_gy,
):
    size_x, size_y = sizes
    devices = size_x * size_y
    layers = out_ref.shape[0]
    gx, gy = lax.axis_index("gx"), lax.axis_index("gy")
    me = gx * size_y + gy

    loads = [
        pltpu.make_async_copy(src, dst, sem_in.at[i])
        for i, (src, dst) in enumerate(
            (
                (canopy_in, canopy_ref),
                (head_in, head.at[:, 0:16, 0:512]),
                (soil_in, soil_ref),
                (slot_in, slot_ref),
                (forcing_in, forcing_ref),
                (table_in, table_ref),
            )
        )
    ]
    for load in loads:
        load.start()

    def wrap(value, size):
        return lax.rem(value + size, size)

    def others(visit):
        for dy in range(1, size_y):
            visit(gx, lax.rem(gy + dy, size_y))

        def ring(i, carry):
            far = (i + 1) // 2
            x = wrap(gx + jnp.where(lax.rem(i, 2) == 1, far, -far), size_x)
            for dy in range(size_y):
                visit(x, lax.rem(gy + dy, size_y))
            return carry

        lax.fori_loop(1, size_x, ring, 0)

    barrier = pltpu.get_barrier_semaphore()
    others(lambda x, y: pl.semaphore_signal(barrier, inc=1, device_id=(x, y), device_id_type=MESH))

    row = lax.broadcasted_iota(jnp.int32, (ROWS, LANES), 0)
    col = lax.broadcasted_iota(jnp.int32, (ROWS, LANES), 1)
    one, zero = jnp.float32(1.0), jnp.float32(0.0)
    has_next_x = jnp.where(gx < size_x - 1, one, zero)
    has_prev_x = jnp.where(gx > 0, one, zero)
    has_next_y = jnp.where(gy < size_y - 1, one, zero)
    has_prev_y = jnp.where(gy > 0, one, zero)
    inside_x = jnp.where(
        row < 16,
        1.0,
        jnp.where(row < 16 + HALO, has_next_x, jnp.where(row >= ROWS - HALO, has_prev_x, 0.0)),
    )
    inside_y = jnp.where(
        col < 512,
        1.0,
        jnp.where(col < 512 + HALO, has_next_y, jnp.where(col >= LANES - HALO, has_prev_y, 0.0)),
    )
    mask[...] = inside_x * inside_y

    def own(ref, k):
        return ref[k, 0:16, 0:512]

    def clear(k, carry):
        for ref in (head, soil, basis.at[0]):
            ref[k, 16:24, 0:512] = jnp.zeros((8, 512), jnp.float32)
            ref[k, 0:24, 512:640] = jnp.zeros((24, 128), jnp.float32)
        return carry

    lax.fori_loop(0, layers, clear, 0)
    for side in range(2):
        for slot in range(5):
            send_x[side, slot, 24:32, :] = jnp.zeros((8, 512), jnp.float32)

    low7 = lax.broadcasted_iota(jnp.int32, (7, 128), 1) < CAP

    def pack(q, carry):
        lanes = pl.ds(pl.multiple_of(q * 128, 128), 128)
        first, second = canopy_ref[0:7, lanes], canopy_ref[6:13, lanes]
        send_c[2 * q, 0:7] = jnp.where(low7, first, pltpu.roll(second, CAP, 1))
        send_c[2 * q + 1, 0:7] = jnp.where(low7, pltpu.roll(first, CAP, 1), second)
        return carry

    loads[0].wait()
    lax.fori_loop(0, devices // 2, pack, 0, unroll=4)
    quarter = size_x // 4

    def seat(x):
        return lax.rem(gx - x + quarter + size_x, size_x)

    def slab(x):
        return pl.ds(pl.multiple_of((seat(x) * size_y + gy) * 8, 8), 7)

    recv_c[slab(gx), :] = send_c[me, 0:7]

    next_x, prev_x = wrap(gx + 1, size_x), wrap(gx - 1, size_x)
    next_y, prev_y = wrap(gy + 1, size_y), wrap(gy - 1, size_y)
    lane16 = lax.broadcasted_iota(jnp.int32, (16, 128), 1)
    group16 = lane16 // 4
    lane24 = lax.broadcasted_iota(jnp.int32, (ROWS, 128), 1)
    early8 = lax.broadcasted_iota(jnp.int32, (8, 128), 0) < 4

    def start(number, slot, fields):
        for f, (ref, index) in enumerate(fields):
            up = jnp.zeros((16, 128), jnp.float32)
            down = jnp.zeros((16, 128), jnp.float32)
            for k in range(layers):
                rows = slice(HALO * k, HALO * (k + 1))
                send_x[0, slot + f, rows, :] = ref[index + (k, slice(16 - HALO, 16), slice(0, 512))]
                send_x[1, slot + f, rows, :] = ref[index + (k, slice(0, HALO), slice(0, 512))]
                last = ref[index + (k, slice(0, 16), slice(384, 512))]
                first = ref[index + (k, slice(0, 16), slice(0, 128))]
                here = group16 == k
                up = jnp.where(here, pltpu.roll(last, 4 * k + 4, 1), up)
                down = jnp.where(here, pltpu.roll(first, 4 * k, 1) if k else first, down)
            send_y[0, slot + f] = up
            send_y[1, slot + f] = down
        slots = pl.ds(slot, len(fields))
        plan = []
        for side, y in enumerate((next_y, prev_y)):
            for turn, x in enumerate((next_x, prev_x)):
                edge = pl.ds(8 * (1 - turn), 8)
                plan.append(
                    (send_y.at[side, slots, edge], recv_k.at[side, turn, slots], (x, y))
                )
        for side, x in enumerate((next_x, prev_x)):
            plan.append((send_x.at[side, slots], recv_x.at[side, slots], (x, gy)))
        for side, y in enumerate((next_y, prev_y)):
            plan.append((send_y.at[side, slots], recv_y.at[side, slots], (gx, y)))
        moves = [
            pltpu.make_async_remote_copy(
                src_ref=src,
                dst_ref=dst,
                send_sem=sem_e.at[0, number, i],
                recv_sem=sem_e.at[1, number, i],
                device_id=target,
                device_id_type=MESH,
            )
            for i, (src, dst, target) in enumerate(plan)
        ]
        for move in moves:
            move.start()
        return moves

    def finish(moves, slot, fields):
        for move in moves[6:] + moves[:4]:
            move.wait()
        edge = mask[:, 512:640]
        for f, (ref, index) in enumerate(fields):
            sides = [
                jnp.concatenate(
                    [
                        recv_y[side, slot + f],
                        jnp.where(early8, recv_k[side, 1, slot + f], recv_k[side, 0, slot + f]),
                    ],
                    axis=0,
                )
                for side in range(2)
            ]
            for k in range(layers):
                left = pltpu.roll(sides[0], 128 - (4 * k + 4), 1)
                right = pltpu.roll(sides[1], 128 - 4 * k, 1) if k else sides[1]
                both = jnp.where(lane24 < 64, right, left)
                ref[index + (k, slice(0, ROWS), slice(512, 640))] = jnp.where(edge > 0.0, both, 0.0)
        for move in moves[4:6]:
            move.wait()
        for f, (ref, index) in enumerate(fields):
            for k in range(layers):
                rows = slice(HALO * k, HALO * (k + 1))
                after = recv_x[1, slot + f, rows, :] * has_next_x
                before = recv_x[0, slot + f, rows, :] * has_prev_x
                ref[index + (k, slice(16, 16 + HALO), slice(0, 512))] = after
                ref[index + (k, slice(ROWS - HALO, ROWS), slice(0, 512))] = before

    loads[1].wait()
    loads[2].wait()

    def convert(k, carry):
        soil[k, 0:16, 0:512] = soil_ref[k].astype(jnp.float32)
        return carry

    lax.fori_loop(0, layers, convert, 0)

    pl.semaphore_wait(barrier, devices - 1)

    def scatter(x, y):
        pltpu.make_async_remote_copy(
            src_ref=send_c.at[x * size_y + y, pl.ds(0, 7)],
            dst_ref=recv_c.at[slab(x)],
            send_sem=sem_c.at[0],
            recv_sem=sem_c.at[1],
            device_id=(x, y),
            device_id_type=MESH,
        ).start()

    opening = [(head, ()), (soil, ())]
    moves = start(0, 0, opening)
    others(scatter)

    def look_up(rows, lanes):
        def layer(k, carry):
            kind = soil[k, rows, lanes]
            values = [jnp.zeros(kind.shape, jnp.float32) for _ in range(3)]
            for c in range(table_ref.shape[1]):
                match = kind == float(c)
                values = [jnp.where(match, table_ref[p, c], v) for p, v in enumerate(values)]
            ksat[k, rows, lanes] = values[0] * mask[rows, lanes]
            steep[k, rows, lanes] = values[1]
            cap[k, rows, lanes] = values[2]
            return carry

        lax.fori_loop(0, layers, layer, 0)

    loads[5].wait()
    look_up(*OWN)

    def saturate(rows, lanes, keep):
        def layer(k, carry):
            a, ks, c = (ref[k, rows, lanes] for ref in (steep, ksat, cap))
            s = logistic(a * head[k, rows, lanes])
            rise = a * s * (1.0 - s)
            conduct[k, rows, lanes] = ks * (0.1 + 0.9 * s * s)
            slope[k, rows, lanes] = 0.9 * ks * s * rise
            coef[0, k, rows, lanes] = STORAGE * c * rise
            keep(k, s, c)
            return carry

        lax.fori_loop(0, layers, layer, 0, unroll=2)

    def keep_old(k, s, c):
        wet[k] = s
        theta_old[k] = c * s

    def keep_residual(k, s, c):
        basis[0, k, 0:16, 0:512] = STORAGE * (c * s - theta_old[k]) - source[k]

    def keep_none(k, s, c):
        pass

    saturate(*OWN, keep_old)

    loads[3].wait()
    within = lax.broadcasted_iota(jnp.int32, (256, 512), 0)

    def seats_of(x):
        slot = jnp.maximum(slot_ref[pl.ds(x, 1), :], 0)
        shift = (size_y * CAP).bit_length() - 1
        seat = ((slot >> shift) - gx + quarter) & (size_x - 1)
        return (seat << shift) + (slot & (size_y * CAP - 1))

    def spot(x, carry):
        slot = seats_of(x)
        hot[x] = jnp.where(within == (slot & 255), 1.0, 0.0).astype(jnp.bfloat16)
        return carry

    lax.fori_loop(0, 16, spot, 0)

    finish(moves, 0, opening)
    for region in RIM:
        look_up(*region)

    def around(k):
        return jnp.minimum(k + 1, layers - 1), jnp.maximum(k - 1, 0)

    def balance():
        def layer(k, carry):
            h, kk = head[k], conduct[k]
            total = basis[0, k, 0:16, 0:512]
            for axis in range(2):
                flow = 0.5 * (kk + ahead(kk, axis)) * (h - ahead(h, axis))
                total = total + (flow - behind(flow, axis))[0:16, 0:512]
            below, above = around(k)
            h, kk = own(head, k), own(conduct, k)
            flow = 0.5 * (kk + own(conduct, below)) * (h - own(head, below) + 1.0)
            total = total + jnp.where(k == layers - 1, kk, flow)
            flow = 0.5 * (own(conduct, above) + kk) * (own(head, above) - h + 1.0)
            basis[0, k, 0:16, 0:512] = total - jnp.where(k == 0, 0.0, flow)
            return carry

        lax.fori_loop(0, layers, layer, 0, unroll=2)

    def linearize(flows):
        def layer(k, carry):
            scaled = mask[...] * (1.0 / SCALE)
            h, kk, dk = head[k], conduct[k], slope[k]
            diagonal = coef[0, k] - SHIFT
            total = None
            for axis, at in ((0, 1), (1, 3)):
                drop = h - ahead(h, axis)
                mean = 0.5 * (kk + ahead(kk, axis))
                mine = dk * drop + mean
                other = ahead(dk, axis) * drop - mean
                diagonal = diagonal + mine - behind(other, axis)
                coef[at, k] = other * scaled
                coef[at + 1, k] = -behind(mine, axis) * scaled
                if flows:
                    flow = mean * drop
                    net = flow - behind(flow, axis)
                    total = net if total is None else total + net
            below, above = around(k)
            bottom, top = k == layers - 1, k == 0
            drop = h - head[below] + 1.0
            mean = 0.5 * (kk + conduct[below])
            diagonal = diagonal + jnp.where(bottom, 2.0 * dk, dk * drop + mean)
            coef[5, k] = jnp.where(bottom, 0.0, slope[below] * drop - mean) * scaled
            if flows:
                total = total + jnp.where(bottom, kk, mean * drop)
            drop = head[above] - h + 1.0
            mean = 0.5 * (kk + conduct[above])
            diagonal = diagonal - jnp.where(top, 0.0, dk * drop - mean)
            coef[6, k] = -jnp.where(top, 0.0, slope[above] * drop + mean) * scaled
            if flows:
                total = total - jnp.where(top, 0.0, mean * drop)
                basis[0, k, 0:16, 0:512] = total[0:16, 0:512]
            coef[0, k] = diagonal * scaled
            return carry

        lax.fori_loop(0, layers, layer, 0)

    for region in RIM:
        saturate(*region, keep_none)
    linearize(True)

    blocks = devices // 4
    low = lax.broadcasted_iota(jnp.int32, (blocks, 128), 1) < CAP
    which = lax.broadcasted_iota(jnp.int32, (blocks, 512), 0)

    def choose():
        arrived = send_c.at[pl.ds(0, devices - 1), pl.ds(0, 7)]
        pltpu.make_async_copy(arrived, arrived, sem_c.at[1]).wait()

        def put(r, left, right):
            value = jnp.concatenate([left, right], axis=1)
            high = value.astype(jnp.bfloat16)
            rows = slice(blocks * r, blocks * (r + 1))
            split[rows, 0:256] = high
            split[rows, 256:512] = (value - high.astype(jnp.float32)).astype(jnp.bfloat16)

        for r in range(7):
            plain = [recv_c[pl.ds(r + 8 * c, blocks, stride=32), :] for c in range(4)]
            moved = [pltpu.roll(x, CAP, 1) for x in plain]
            put(r, jnp.where(low, plain[0], moved[1]), jnp.where(low, plain[2], moved[3]))
            if r >= 1:
                put(r + 6, jnp.where(low, moved[0], plain[1]), jnp.where(low, moved[2], plain[3]))

        def select(x, carry):
            found = jnp.dot(
                split[...], jnp.concatenate([hot[x], hot[x]], axis=0), preferred_element_type=jnp.float32
            )
            match = which == seats_of(x) >> 8
            for r in range(13):
                piece = jnp.where(match, found[blocks * r : blocks * (r + 1)], 0.0)
                records[r, pl.ds(x, 1), :] = jnp.sum(piece, axis=0, keepdims=True)
            return carry

        lax.fori_loop(0, 16, select, 0, unroll=2)

    choose()
    loads[4].wait()
    sunlight, air, humidity, rainfall = (forcing_ref[i] for i in range(4))
    leaf, albedo, resist = (records[i] for i in range(3))
    total, roots = jnp.zeros_like(leaf), jnp.zeros_like(leaf)
    for k in range(layers):
        total = total + records[3 + k] * wet[k]
        roots = roots + records[3 + k]
    conductance = total / roots * leaf / (leaf + resist)
    exchange_coef = 0.5 + 0.3 * leaf
    radiation = (1.0 - albedo) * sunlight + 0.3
    surface = air
    for _ in range(2):
        vapour = 0.5 * jnp.exp(2.0 * (surface - air))
        square = surface * surface
        excess = (
            radiation
            - 0.3 * square * square
            - exchange_coef * (surface - air)
            - conductance * (vapour - humidity)
        )
        tangent = -1.2 * square * surface - exchange_coef - 2.0 * conductance * vapour
        surface = surface - excess / tangent
    evaporation = conductance * (0.5 * jnp.exp(2.0 * (surface - air)) - humidity)
    ks_top = own(ksat, 0)
    infiltration = rainfall * ks_top / (rainfall + ks_top)
    land = slot_ref[...] >= 0
    evaporation = jnp.where(land, evaporation, 0.0)
    infiltration = jnp.where(land, infiltration, 0.0)
    flux_ref[0] = evaporation
    flux_ref[1] = infiltration
    share = evaporation / total
    for k in range(layers):
        gain = -jnp.where(land, share * records[3 + k] * wet[k], 0.0)
        if k == 0:
            gain = gain + infiltration
        source[k] = gain
        basis[0, k, 0:16, 0:512] -= gain

    def fold(product):
        tall = product[0:8] + product[8:16]
        return (tall[:, 0:128] + tall[:, 128:256]) + (tall[:, 256:384] + tall[:, 384:512])

    lane1 = lax.broadcasted_iota(jnp.int32, (1, 128), 1)

    def place(partial, at, sums):
        for i, value in enumerate(sums):
            line = jnp.sum(value, axis=0, keepdims=True)
            partial = jnp.where(lane1 == at + i, jnp.sum(line, axis=1, keepdims=True), partial)
        return partial

    def matvec(j):
        rows, lanes = (slice(0, ROWS), slice(0, LANES)) if j + 1 < KRYLOV else (slice(0, 16), slice(0, 512))

        def layer(k, carry):
            v = basis[j, k]
            below, above = around(k)

            def term(i, value):
                return coef[i, k, rows, lanes] * value[rows, lanes]

            w = term(0, v)
            w = w + term(1, ahead(v, 0)) + term(2, behind(v, 0))
            w = w + term(3, ahead(v, 1)) + term(4, behind(v, 1))
            w = w + coef[5, k, rows, lanes] * basis[j, below, rows, lanes]
            w = w + coef[6, k, rows, lanes] * basis[j, above, rows, lanes]
            if j + 1 < KRYLOV:
                basis[j + 1, k] = w
            mine = w[0:16, 0:512]
            sums = [fold(mine * basis[i, k, 0:16, 0:512]) for i in range(j + 1)]
            sums.append(fold(mine * mine))
            return tuple(a + b for a, b in zip(carry, sums))

        zeros = tuple(jnp.zeros((8, 128), jnp.float32) for _ in range(j + 2))
        return lax.fori_loop(0, layers, layer, zeros, unroll=2)

    def square_of_start():
        def layer(k, carry):
            value = basis[0, k, 0:16, 0:512]
            return carry + fold(value * value)

        return [lax.fori_loop(0, layers, layer, jnp.zeros((8, 128), jnp.float32))]

    def reduce_all(n, partial):
        def along(stage, value, gather, sem, here, size, target):
            mine = part.at[n, stage]
            mine[...] = value
            gather[n, here] = value
            for i in range(1, size):
                pltpu.make_async_remote_copy(
                    src_ref=mine,
                    dst_ref=gather.at[n, here],
                    send_sem=sem.at[0, n],
                    recv_sem=sem.at[1, n],
                    device_id=target(lax.rem(here + i, size)),
                    device_id_type=MESH,
                ).start()
            rest = gather.at[n, pl.ds(0, size - 1)]
            pltpu.make_async_copy(rest, rest, sem.at[1, n]).wait()
            total = gather[n, 0]
            for i in range(1, size):
                total = total + gather[n, i]
            return total

        partial = along(0, partial, gather_x, sem_gx, gx, size_x, lambda d: (d, gy))
        return along(1, partial, gather_y, sem_gy, gy, size_y, lambda d: (gx, d))

    for n in range(NEWTON):
        field = [(basis, (0,))]
        moves = start(1 + n, 2 + n, field)
        partial = place(jnp.zeros((1, 128), jnp.float32), 0, square_of_start())
        if n:
            finish(head_moves, 4, [(head, ())])
            for region in RIM:
                saturate(*region, keep_none)
            linearize(False)
        finish(moves, 2 + n, field)
        for j, at in ((0, 1), (1, 3), (2, 6)):
            partial = place(partial, at, matvec(j))
        sums = reduce_all(n, partial)
        gram = [[None] * 4 for _ in range(4)]
        at = 0
        for i in range(4):
            for j in range(i + 1):
                gram[i][j] = gram[j][i] = jnp.broadcast_to(sums[:, at : at + 1], (1, 128))
                at += 1
        weights = [w[:, 0:1] for w in krylov_weights(gram)]
        last = n + 1 == NEWTON
        rows, lanes = (slice(0, 16), slice(0, 512)) if last else (slice(0, ROWS), slice(0, LANES))

        def update(k, carry):
            value = head[k, rows, lanes]
            for i in range(KRYLOV):
                value = value - weights[i] * basis[i, k, rows, lanes]
            if last:
                out_ref[k] = value
            else:
                head[k] = value
            return carry

        lax.fori_loop(0, layers, update, 0)
        if not last:
            head_moves = start(3, 4, [(head, ())])
            saturate(*OWN, keep_residual)
            for region in RIM:
                saturate(*region, keep_none)
            balance()

    sent = send_c.at[pl.ds(0, devices - 1), pl.ds(0, 7)]
    pltpu.make_async_copy(sent, sent, sem_c.at[0]).wait()
    for n in range(NEWTON):
        sent = gather_x.at[n, pl.ds(0, size_x - 1)]
        pltpu.make_async_copy(sent, sent, sem_gx.at[0, n]).wait()
        sent = gather_y.at[n, pl.ds(0, size_y - 1)]
        pltpu.make_async_copy(sent, sent, sem_gy.at[0, n]).wait()


def shards(sizes, head_old, soil_type, soil_table, forcing, canopy, column_slot):
    layers = head_old.shape[0]
    devices = sizes[0] * sizes[1]
    f32 = jnp.float32
    wide = (layers, ROWS, LANES)
    tile = (layers, 16, 512)
    vmem, anywhere = pl.BlockSpec(memory_space=pltpu.VMEM), pl.BlockSpec(memory_space=pl.ANY)
    return pl.pallas_call(
        functools.partial(kernel, sizes),
        out_shape=(
            jax.ShapeDtypeStruct(head_old.shape, f32),
            jax.ShapeDtypeStruct((2, 16, 512), f32),
        ),
        in_specs=[anywhere] * 6,
        out_specs=(vmem, vmem),
        scratch_shapes=[
            pltpu.SMEM(soil_table.shape, f32),
            pltpu.VMEM(tile, jnp.int32),
            pltpu.VMEM(forcing.shape, f32),
            pltpu.VMEM(canopy.shape, f32),
            pltpu.VMEM(column_slot.shape, jnp.int32),
            pltpu.VMEM((devices, 8, 128), f32),
            pltpu.VMEM((devices * 8, 128), f32),
            pltpu.VMEM((13 * (devices // 4), 512), jnp.bfloat16),
            pltpu.VMEM((16, 256, 512), jnp.bfloat16),
            pltpu.VMEM((13, 16, 512), f32),
            pltpu.VMEM(wide, f32),
            pltpu.VMEM(wide, f32),
            pltpu.VMEM(wide, f32),
            pltpu.VMEM(wide, f32),
            pltpu.VMEM(wide, f32),
            pltpu.VMEM(wide, f32),
            pltpu.VMEM(wide, f32),
            pltpu.VMEM((7,) + wide, f32),
            pltpu.VMEM((KRYLOV,) + wide, f32),
            pltpu.VMEM(tile, f32),
            pltpu.VMEM(tile, f32),
            pltpu.VMEM(tile, f32),
            pltpu.VMEM((ROWS, LANES), f32),
            pltpu.VMEM((2, 5, 32, 512), f32),
            pltpu.VMEM((2, 5, 32, 512), f32),
            pltpu.VMEM((2, 5, 16, 128), f32),
            pltpu.VMEM((2, 5, 16, 128), f32),
            pltpu.VMEM((2, 2, 5, 8, 128), f32),
            pltpu.VMEM((NEWTON, 2, 1, 128), f32),
            pltpu.VMEM((NEWTON, sizes[0], 1, 128), f32),
            pltpu.VMEM((NEWTON, sizes[1], 1, 128), f32),
            pltpu.SemaphoreType.DMA((6,)),
            pltpu.SemaphoreType.DMA((3,)),
            pltpu.SemaphoreType.DMA((2, 4, 8)),
            pltpu.SemaphoreType.DMA((2, NEWTON)),
            pltpu.SemaphoreType.DMA((2, NEWTON)),
        ],
        compiler_params=pltpu.CompilerParams(collective_id=0, has_side_effects=True),
        name="coupled_step",
    )(head_old, soil_type, soil_table, forcing, canopy, column_slot)


def solution(mesh):
    sizes = (mesh.shape["gx"], mesh.shape["gy"])
    return jax.shard_map(
        functools.partial(shards, sizes),
        mesh=mesh,
        in_specs=(
            P(None, "gx", "gy"),
            P(None, "gx", "gy"),
            P(),
            P(None, "gx", "gy"),
            P(None, ("gx", "gy")),
            P("gx", "gy"),
        ),
        out_specs=(P(None, "gx", "gy"), P(None, "gx", "gy")),
        check_vma=False,
    )
```

```python
import functools

import jax
import jax.numpy as jnp
from jax import lax
from jax.experimental import pallas as pl
from jax.experimental.pallas import tpu as pltpu
from jax.sharding import PartitionSpec as P

NEWTON = 2
KRYLOV = 3
CAP = 64

STORAGE = 4.0
EPSILON = 1e-06

SHIFT = 3.0
SCALE = 3.0

MESH = pl.DeviceIdType.MESH
OWN = (slice(0, 16), slice(0, 512))
RIM = ((slice(16, 24), slice(0, 512)), (slice(0, 24), slice(512, 640)))
HALO = 3
ROWS = 24
LANES = 640


def logistic(u):
    return 1.0 / (1.0 + jnp.exp(-u))


def ahead(x, axis):
    return pltpu.roll(x, x.shape[axis] - 1, axis)


def behind(x, axis):
    return pltpu.roll(x, 1, axis)


def krylov_weights(gram):
    def inner(vector, image):
        terms = [a * b for a, b in zip(vector, image) if a is not None]
        return functools.reduce(lambda a, b: a + b, terms)

    def image_of(vector):
        return [inner(vector, [gram[i][k] for i in range(4)]) for k in range(4)]

    beta = jnp.sqrt(gram[0][0] + EPSILON)
    basis = [[1.0 / beta, None, None, None]]
    images = [image_of(basis[0])]
    hessen = [[None] * KRYLOV for _ in range(KRYLOV + 1)]
    for j in range(KRYLOV):
        v = basis[j]
        w = [None] * 4
        for i in range(j + 2):
            if i <= j:
                w[i] = SHIFT * v[i]
            if i >= 1:
                term = SCALE * v[i - 1]
                w[i] = term if w[i] is None else w[i] + term
        for i in range(j + 1):
            product = inner(w, images[i])
            hessen[i][j] = product
            w = [a if b is None else a - product * b for a, b in zip(w, basis[i])]
        square = jnp.maximum(inner(w, image_of(w)), 0.0)
        length = jnp.sqrt(square + EPSILON)
        hessen[j + 1][j] = length
        if j + 1 < KRYLOV:
            basis.append([None if a is None else a / length for a in w])
            images.append(image_of(basis[-1]))

    def column(a, b):
        pairs = [(hessen[i][a], hessen[i][b]) for i in range(KRYLOV + 1)]
        terms = [x * y for x, y in pairs if x is not None and y is not None]
        return functools.reduce(lambda x, y: x + y, terms)

    factor = [[None] * KRYLOV for _ in range(KRYLOV)]
    for i in range(KRYLOV):
        for j in range(i + 1):
            value = column(i, j)
            for k in range(j):
                value = value - factor[i][k] * factor[j][k]
            factor[i][j] = jnp.sqrt(value) if i == j else value / factor[j][j]
    forward = []
    for row in range(KRYLOV):
        value = hessen[0][row] * beta
        for other in range(row):
            value = value - factor[row][other] * forward[other]
        forward.append(value / factor[row][row])
    y = [None] * KRYLOV
    for row in reversed(range(KRYLOV)):
        value = forward[row]
        for other in range(row + 1, KRYLOV):
            value = value - factor[other][row] * y[other]
        y[row] = value / factor[row][row]
    weights = []
    for i in range(KRYLOV):
        terms = [y[j] * basis[j][i] for j in range(KRYLOV) if basis[j][i] is not None]
        weights.append(functools.reduce(lambda a, b: a + b, terms))
    return weights


def kernel(
    sizes,
    head_in,
    soil_in,
    table_in,
    forcing_in,
    canopy_in,
    slot_in,
    out_ref,
    flux_ref,
    table_ref,
    soil_ref,
    forcing_ref,
    canopy_ref,
    slot_ref,
    send_c,
    recv_c,
    split,
    hot,
    records,
    head,
    soil,
    conduct,
    slope,
    ksat,
    steep,
    cap,
    coef,
    basis,
    wet,
    theta_old,
    source,
    mask,
    send_x,
    recv_x,
    send_y,
    recv_y,
    recv_k,
    part,
    gather_x,
    gather_y,
    sem_in,
    sem_c,
    sem_e,
    sem_gx,
    sem_gy,
):
    size_x, size_y = sizes
    devices = size_x * size_y
    layers = out_ref.shape[0]
    gx, gy = lax.axis_index("gx"), lax.axis_index("gy")
    me = gx * size_y + gy

    loads = [
        pltpu.make_async_copy(src, dst, sem_in.at[i])
        for i, (src, dst) in enumerate(
            (
                (canopy_in, canopy_ref),
                (head_in, head.at[:, 0:16, 0:512]),
                (soil_in, soil_ref),
                (slot_in, slot_ref),
                (forcing_in, forcing_ref),
                (table_in, table_ref),
            )
        )
    ]
    for load in loads:
        load.start()

    def wrap(value, size):
        return lax.rem(value + size, size)

    def others(visit):
        for dy in range(1, size_y):
            visit(gx, lax.rem(gy + dy, size_y))

        def ring(i, carry):
            far = (i + 1) // 2
            x = wrap(gx + jnp.where(lax.rem(i, 2) == 1, far, -far), size_x)
            for dy in range(size_y):
                visit(x, lax.rem(gy + dy, size_y))
            return carry

        lax.fori_loop(1, size_x, ring, 0)

    barrier = pltpu.get_barrier_semaphore()
    others(lambda x, y: pl.semaphore_signal(barrier, inc=1, device_id=(x, y), device_id_type=MESH))

    row = lax.broadcasted_iota(jnp.int32, (ROWS, LANES), 0)
    col = lax.broadcasted_iota(jnp.int32, (ROWS, LANES), 1)
    one, zero = jnp.float32(1.0), jnp.float32(0.0)
    in_x, in_y = (gx < size_x - 1, gx > 0), (gy < size_y - 1, gy > 0)
    has_next_x, has_prev_x = (jnp.where(there, one, zero) for there in in_x)
    has_next_y, has_prev_y = (jnp.where(there, one, zero) for there in in_y)
    inside_x = jnp.where(
        row < 16,
        1.0,
        jnp.where(row < 16 + HALO, has_next_x, jnp.where(row >= ROWS - HALO, has_prev_x, 0.0)),
    )
    inside_y = jnp.where(
        col < 512,
        1.0,
        jnp.where(col < 512 + HALO, has_next_y, jnp.where(col >= LANES - HALO, has_prev_y, 0.0)),
    )
    mask[...] = inside_x * inside_y

    def own(ref, k):
        return ref[k, 0:16, 0:512]

    def clear(k, carry):
        for ref in (head, soil, basis.at[0]):
            ref[k, 16:24, 0:512] = jnp.zeros((8, 512), jnp.float32)
            ref[k, 0:24, 512:640] = jnp.zeros((24, 128), jnp.float32)
        return carry

    lax.fori_loop(0, layers, clear, 0)
    for side in range(2):
        for slot in range(5):
            send_x[side, slot, 24:32, :] = jnp.zeros((8, 512), jnp.float32)

    low7 = lax.broadcasted_iota(jnp.int32, (7, 128), 1) < CAP

    def pack(q, carry):
        lanes = pl.ds(pl.multiple_of(q * 128, 128), 128)
        first, second = canopy_ref[0:7, lanes], canopy_ref[6:13, lanes]
        send_c[2 * q, 0:7] = jnp.where(low7, first, pltpu.roll(second, CAP, 1))
        send_c[2 * q + 1, 0:7] = jnp.where(low7, pltpu.roll(first, CAP, 1), second)
        return carry

    loads[0].wait()
    lax.fori_loop(0, devices // 2, pack, 0, unroll=4)
    quarter = size_x // 4

    def seat(x):
        return lax.rem(gx - x + quarter + size_x, size_x)

    def slab(x):
        return pl.ds(pl.multiple_of((seat(x) * size_y + gy) * 8, 8), 7)

    recv_c[slab(gx), :] = send_c[me, 0:7]

    next_x, prev_x = wrap(gx + 1, size_x), wrap(gx - 1, size_x)
    next_y, prev_y = wrap(gy + 1, size_y), wrap(gy - 1, size_y)
    lane16 = lax.broadcasted_iota(jnp.int32, (16, 128), 1)
    group16 = lane16 // 4
    lane24 = lax.broadcasted_iota(jnp.int32, (ROWS, 128), 1)
    early8 = lax.broadcasted_iota(jnp.int32, (8, 128), 0) < 4

    def start(number, slot, fields):
        for f, (ref, index) in enumerate(fields):
            up = jnp.zeros((16, 128), jnp.float32)
            down = jnp.zeros((16, 128), jnp.float32)
            for k in range(layers):
                rows = slice(HALO * k, HALO * (k + 1))
                send_x[0, slot + f, rows, :] = ref[index + (k, slice(16 - HALO, 16), slice(0, 512))]
                send_x[1, slot + f, rows, :] = ref[index + (k, slice(0, HALO), slice(0, 512))]
                last = ref[index + (k, slice(0, 16), slice(384, 512))]
                first = ref[index + (k, slice(0, 16), slice(0, 128))]
                here = group16 == k
                up = jnp.where(here, pltpu.roll(last, 4 * k + 4, 1), up)
                down = jnp.where(here, pltpu.roll(first, 4 * k, 1) if k else first, down)
            send_y[0, slot + f] = up
            send_y[1, slot + f] = down
        slots = pl.ds(slot, len(fields))
        plan = []
        for side, y in enumerate((next_y, prev_y)):
            for turn, x in enumerate((next_x, prev_x)):
                edge = pl.ds(8 * (1 - turn), 8)
                plan.append(
                    (
                        send_y.at[side, slots, edge],
                        recv_k.at[side, turn, slots],
                        (x, y),
                        in_x[turn] & in_y[side],
                        in_x[1 - turn] & in_y[1 - side],
                    )
                )
        for side, x in enumerate((next_x, prev_x)):
            plan.append(
                (send_x.at[side, slots], recv_x.at[side, slots], (x, gy), in_x[side], in_x[1 - side])
            )
        for side, y in enumerate((next_y, prev_y)):
            plan.append(
                (send_y.at[side, slots], recv_y.at[side, slots], (gx, y), in_y[side], in_y[1 - side])
            )
        moves = []
        for i, (src, dst, target, sends, receives) in enumerate(plan):
            move = pltpu.make_async_remote_copy(
                src_ref=src,
                dst_ref=dst,
                send_sem=sem_e.at[0, number, i],
                recv_sem=sem_e.at[1, number, i],
                device_id=target,
                device_id_type=MESH,
            )
            moves.append((move, sends, receives))
        for i in (4, 5, 0, 1, 2, 3, 6, 7):
            move, sends, _ = moves[i]
            pl.when(sends)(move.start)
        return moves

    def await_all(moves):
        for move, _, receives in moves:
            pl.when(receives)(move.wait_recv)

    def drain(moves):
        for move, sends, _ in moves:
            pl.when(sends)(move.wait_send)

    def finish(moves, slot, fields):
        await_all(moves[6:] + moves[:4])
        edge = mask[:, 512:640]
        for f, (ref, index) in enumerate(fields):
            sides = [
                jnp.concatenate(
                    [
                        recv_y[side, slot + f],
                        jnp.where(early8, recv_k[side, 1, slot + f], recv_k[side, 0, slot + f]),
                    ],
                    axis=0,
                )
                for side in range(2)
            ]
            for k in range(layers):
                left = pltpu.roll(sides[0], 128 - (4 * k + 4), 1)
                right = pltpu.roll(sides[1], 128 - 4 * k, 1) if k else sides[1]
                both = jnp.where(lane24 < 64, right, left)
                ref[index + (k, slice(0, ROWS), slice(512, 640))] = jnp.where(edge > 0.0, both, 0.0)
        await_all(moves[4:6])
        for f, (ref, index) in enumerate(fields):
            for k in range(layers):
                rows = slice(HALO * k, HALO * (k + 1))
                after = jnp.where(in_x[0], recv_x[1, slot + f, rows, :], 0.0)
                before = jnp.where(in_x[1], recv_x[0, slot + f, rows, :], 0.0)
                ref[index + (k, slice(16, 16 + HALO), slice(0, 512))] = after
                ref[index + (k, slice(ROWS - HALO, ROWS), slice(0, 512))] = before

    loads[1].wait()
    loads[2].wait()

    def convert(k, carry):
        soil[k, 0:16, 0:512] = soil_ref[k].astype(jnp.float32)
        return carry

    lax.fori_loop(0, layers, convert, 0)

    pl.semaphore_wait(barrier, devices - 1)

    def scatter(x, y):
        pltpu.make_async_remote_copy(
            src_ref=send_c.at[x * size_y + y, pl.ds(0, 7)],
            dst_ref=recv_c.at[slab(x)],
            send_sem=sem_c.at[0],
            recv_sem=sem_c.at[1],
            device_id=(x, y),
            device_id_type=MESH,
        ).start()

    opening = [(head, ()), (soil, ())]
    moves = start(0, 0, opening)
    started = [moves]
    others(scatter)

    def look_up(rows, lanes):
        def layer(k, carry):
            kind = soil[k, rows, lanes]
            values = [jnp.zeros(kind.shape, jnp.float32) for _ in range(3)]
            for c in range(table_ref.shape[1]):
                match = kind == float(c)
                values = [jnp.where(match, table_ref[p, c], v) for p, v in enumerate(values)]
            ksat[k, rows, lanes] = values[0] * mask[rows, lanes]
            steep[k, rows, lanes] = values[1]
            cap[k, rows, lanes] = values[2]
            return carry

        lax.fori_loop(0, layers, layer, 0)

    loads[5].wait()
    look_up(*OWN)

    def saturate(rows, lanes, keep):
        def layer(k, carry):
            a, ks, c = (ref[k, rows, lanes] for ref in (steep, ksat, cap))
            s = logistic(a * head[k, rows, lanes])
            rise = a * s * (1.0 - s)
            conduct[k, rows, lanes] = ks * (0.1 + 0.9 * s * s)
            slope[k, rows, lanes] = 0.9 * ks * s * rise
            coef[0, k, rows, lanes] = STORAGE * c * rise
            keep(k, s, c)
            return carry

        lax.fori_loop(0, layers, layer, 0, unroll=2)

    def keep_old(k, s, c):
        wet[k] = s
        theta_old[k] = c * s

    def keep_residual(k, s, c):
        basis[0, k, 0:16, 0:512] = STORAGE * (c * s - theta_old[k]) - source[k]

    def keep_none(k, s, c):
        pass

    saturate(*OWN, keep_old)

    loads[3].wait()
    within = lax.broadcasted_iota(jnp.int32, (256, 512), 0)

    def seats_of(x):
        slot = jnp.maximum(slot_ref[pl.ds(x, 1), :], 0)
        shift = (size_y * CAP).bit_length() - 1
        seat = ((slot >> shift) - gx + quarter) & (size_x - 1)
        return (seat << shift) + (slot & (size_y * CAP - 1))

    def spot(x, carry):
        slot = seats_of(x)
        hot[x] = jnp.where(within == (slot & 255), 1.0, 0.0).astype(jnp.bfloat16)
        return carry

    lax.fori_loop(0, 16, spot, 0)

    finish(moves, 0, opening)
    for region in RIM:
        look_up(*region)

    def around(k):
        return jnp.minimum(k + 1, layers - 1), jnp.maximum(k - 1, 0)

    def balance(added):
        def layer(k, carry):
            h, kk = head[k], conduct[k]
            total = basis[0, k, 0:16, 0:512] if added else 0.0
            for axis in range(2):
                flow = 0.5 * (kk + ahead(kk, axis)) * (h - ahead(h, axis))
                total = total + (flow - behind(flow, axis))[0:16, 0:512]
            below, above = around(k)
            h, kk = own(head, k), own(conduct, k)
            flow = 0.5 * (kk + own(conduct, below)) * (h - own(head, below) + 1.0)
            total = total + jnp.where(k == layers - 1, kk, flow)
            flow = 0.5 * (own(conduct, above) + kk) * (own(head, above) - h + 1.0)
            basis[0, k, 0:16, 0:512] = total - jnp.where(k == 0, 0.0, flow)
            return carry

        lax.fori_loop(0, layers, layer, 0, unroll=2)

    def linearize():
        def layer(k, carry):
            scaled = mask[...] * (1.0 / SCALE)
            h, kk, dk = head[k], conduct[k], slope[k]
            diagonal = coef[0, k] - SHIFT
            for axis, at in ((0, 1), (1, 3)):
                drop = h - ahead(h, axis)
                mean = 0.5 * (kk + ahead(kk, axis))
                mine = dk * drop + mean
                other = ahead(dk, axis) * drop - mean
                diagonal = diagonal + mine - behind(other, axis)
                coef[at, k] = other * scaled
                coef[at + 1, k] = -behind(mine, axis) * scaled
            below, above = around(k)
            bottom, top = k == layers - 1, k == 0
            drop = h - head[below] + 1.0
            mean = 0.5 * (kk + conduct[below])
            diagonal = diagonal + jnp.where(bottom, 2.0 * dk, dk * drop + mean)
            coef[5, k] = jnp.where(bottom, 0.0, slope[below] * drop - mean) * scaled
            drop = head[above] - h + 1.0
            mean = 0.5 * (kk + conduct[above])
            diagonal = diagonal - jnp.where(top, 0.0, dk * drop - mean)
            coef[6, k] = -jnp.where(top, 0.0, slope[above] * drop + mean) * scaled
            coef[0, k] = diagonal * scaled
            return carry

        lax.fori_loop(0, layers, layer, 0)

    for region in RIM:
        saturate(*region, keep_none)
    balance(False)

    blocks = devices // 4
    low = lax.broadcasted_iota(jnp.int32, (blocks, 128), 1) < CAP
    which = lax.broadcasted_iota(jnp.int32, (blocks, 512), 0)

    def choose():
        arrived = send_c.at[pl.ds(0, devices - 1), pl.ds(0, 7)]
        pltpu.make_async_copy(arrived, arrived, sem_c.at[1]).wait()

        def put(r, left, right):
            value = jnp.concatenate([left, right], axis=1)
            high = value.astype(jnp.bfloat16)
            rows = slice(blocks * r, blocks * (r + 1))
            split[rows, 0:256] = high
            split[rows, 256:512] = (value - high.astype(jnp.float32)).astype(jnp.bfloat16)

        for r in range(7):
            plain = [recv_c[pl.ds(r + 8 * c, blocks, stride=32), :] for c in range(4)]
            moved = [pltpu.roll(x, CAP, 1) for x in plain]
            put(r, jnp.where(low, plain[0], moved[1]), jnp.where(low, plain[2], moved[3]))
            if r >= 1:
                put(r + 6, jnp.where(low, moved[0], plain[1]), jnp.where(low, moved[2], plain[3]))

        def select(x, carry):
            found = jnp.dot(
                split[...], jnp.concatenate([hot[x], hot[x]], axis=0), preferred_element_type=jnp.float32
            )
            match = which == seats_of(x) >> 8
            for r in range(13):
                piece = jnp.where(match, found[blocks * r : blocks * (r + 1)], 0.0)
                records[r, pl.ds(x, 1), :] = jnp.sum(piece, axis=0, keepdims=True)
            return carry

        lax.fori_loop(0, 16, select, 0, unroll=2)

    choose()
    loads[4].wait()
    sunlight, air, humidity, rainfall = (forcing_ref[i] for i in range(4))
    leaf, albedo, resist = (records[i] for i in range(3))
    total, roots = jnp.zeros_like(leaf), jnp.zeros_like(leaf)
    for k in range(layers):
        total = total + records[3 + k] * wet[k]
        roots = roots + records[3 + k]
    conductance = total / roots * leaf / (leaf + resist)
    exchange_coef = 0.5 + 0.3 * leaf
    radiation = (1.0 - albedo) * sunlight + 0.3
    surface = air
    for _ in range(2):
        vapour = 0.5 * jnp.exp(2.0 * (surface - air))
        square = surface * surface
        excess = (
            radiation
            - 0.3 * square * square
            - exchange_coef * (surface - air)
            - conductance * (vapour - humidity)
        )
        tangent = -1.2 * square * surface - exchange_coef - 2.0 * conductance * vapour
        surface = surface - excess / tangent
    evaporation = conductance * (0.5 * jnp.exp(2.0 * (surface - air)) - humidity)
    ks_top = own(ksat, 0)
    infiltration = rainfall * ks_top / (rainfall + ks_top)
    land = slot_ref[...] >= 0
    evaporation = jnp.where(land, evaporation, 0.0)
    infiltration = jnp.where(land, infiltration, 0.0)
    flux_ref[0] = evaporation
    flux_ref[1] = infiltration
    share = evaporation / total
    for k in range(layers):
        gain = -jnp.where(land, share * records[3 + k] * wet[k], 0.0)
        if k == 0:
            gain = gain + infiltration
        source[k] = gain
        basis[0, k, 0:16, 0:512] -= gain

    def fold(product):
        tall = product[0:8] + product[8:16]
        return (tall[:, 0:128] + tall[:, 128:256]) + (tall[:, 256:384] + tall[:, 384:512])

    lane1 = lax.broadcasted_iota(jnp.int32, (1, 128), 1)

    def place(partial, at, sums):
        for i, value in enumerate(sums):
            line = jnp.sum(value, axis=0, keepdims=True)
            partial = jnp.where(lane1 == at + i, jnp.sum(line, axis=1, keepdims=True), partial)
        return partial

    def matvec(j):
        rows, lanes = (slice(0, ROWS), slice(0, LANES)) if j + 1 < KRYLOV else (slice(0, 16), slice(0, 512))

        def layer(k, carry):
            v = basis[j, k]
            below, above = around(k)

            def term(i, value):
                return coef[i, k, rows, lanes] * value[rows, lanes]

            w = term(0, v)
            w = w + term(1, ahead(v, 0)) + term(2, behind(v, 0))
            w = w + term(3, ahead(v, 1)) + term(4, behind(v, 1))
            w = w + coef[5, k, rows, lanes] * basis[j, below, rows, lanes]
            w = w + coef[6, k, rows, lanes] * basis[j, above, rows, lanes]
            if j + 1 < KRYLOV:
                basis[j + 1, k] = w
            mine = w[0:16, 0:512]
            sums = [fold(mine * basis[i, k, 0:16, 0:512]) for i in range(j + 1)]
            sums.append(fold(mine * mine))
            return tuple(a + b for a, b in zip(carry, sums))

        zeros = tuple(jnp.zeros((8, 128), jnp.float32) for _ in range(j + 2))
        return lax.fori_loop(0, layers, layer, zeros, unroll=2)

    def square_of_start():
        def layer(k, carry):
            value = basis[0, k, 0:16, 0:512]
            return carry + fold(value * value)

        return [lax.fori_loop(0, layers, layer, jnp.zeros((8, 128), jnp.float32))]

    def reduce_all(n, partial):
        def along(stage, value, gather, sem, here, size, target):
            mine = part.at[n, stage]
            mine[...] = value
            gather[n, here] = value
            for i in range(1, size):
                pltpu.make_async_remote_copy(
                    src_ref=mine,
                    dst_ref=gather.at[n, here],
                    send_sem=sem.at[0, n],
                    recv_sem=sem.at[1, n],
                    device_id=target(lax.rem(here + i, size)),
                    device_id_type=MESH,
                ).start()
            rest = gather.at[n, pl.ds(0, size - 1)]
            pltpu.make_async_copy(rest, rest, sem.at[1, n]).wait()
            total = gather[n, 0]
            for i in range(1, size):
                total = total + gather[n, i]
            return total

        partial = along(0, partial, gather_x, sem_gx, gx, size_x, lambda d: (d, gy))
        return along(1, partial, gather_y, sem_gy, gy, size_y, lambda d: (gx, d))

    for n in range(NEWTON):
        field = [(basis, (0,))]
        moves = start(1 + n, 2 + n, field)
        started.append(moves)
        partial = place(jnp.zeros((1, 128), jnp.float32), 0, square_of_start())
        if not n:
            linearize()
        else:
            finish(head_moves, 4, [(head, ())])
            for region in RIM:
                saturate(*region, keep_none)
            linearize()
        finish(moves, 2 + n, field)
        for j, at in ((0, 1), (1, 3), (2, 6)):
            partial = place(partial, at, matvec(j))
        sums = reduce_all(n, partial)
        gram = [[None] * 4 for _ in range(4)]
        at = 0
        for i in range(4):
            for j in range(i + 1):
                gram[i][j] = gram[j][i] = jnp.broadcast_to(sums[:, at : at + 1], (1, 128))
                at += 1
        weights = [w[:, 0:1] for w in krylov_weights(gram)]
        last = n + 1 == NEWTON
        rows, lanes = (slice(0, 16), slice(0, 512)) if last else (slice(0, ROWS), slice(0, LANES))

        def update(k, carry):
            value = head[k, rows, lanes]
            for i in range(KRYLOV):
                value = value - weights[i] * basis[i, k, rows, lanes]
            if last:
                out_ref[k] = value
            else:
                head[k] = value
            return carry

        lax.fori_loop(0, layers, update, 0)
        if not last:
            head_moves = start(3, 4, [(head, ())])
            started.append(head_moves)
            saturate(*OWN, keep_residual)
            for region in RIM:
                saturate(*region, keep_none)
            balance(True)

    for moves in started:
        drain(moves)
    sent = send_c.at[pl.ds(0, devices - 1), pl.ds(0, 7)]
    pltpu.make_async_copy(sent, sent, sem_c.at[0]).wait()
    for n in range(NEWTON):
        sent = gather_x.at[n, pl.ds(0, size_x - 1)]
        pltpu.make_async_copy(sent, sent, sem_gx.at[0, n]).wait()
        sent = gather_y.at[n, pl.ds(0, size_y - 1)]
        pltpu.make_async_copy(sent, sent, sem_gy.at[0, n]).wait()


def shards(sizes, head_old, soil_type, soil_table, forcing, canopy, column_slot):
    layers = head_old.shape[0]
    devices = sizes[0] * sizes[1]
    f32 = jnp.float32
    wide = (layers, ROWS, LANES)
    tile = (layers, 16, 512)
    vmem, anywhere = pl.BlockSpec(memory_space=pltpu.VMEM), pl.BlockSpec(memory_space=pl.ANY)
    return pl.pallas_call(
        functools.partial(kernel, sizes),
        out_shape=(
            jax.ShapeDtypeStruct(head_old.shape, f32),
            jax.ShapeDtypeStruct((2, 16, 512), f32),
        ),
        in_specs=[anywhere] * 6,
        out_specs=(vmem, vmem),
        scratch_shapes=[
            pltpu.SMEM(soil_table.shape, f32),
            pltpu.VMEM(tile, jnp.int32),
            pltpu.VMEM(forcing.shape, f32),
            pltpu.VMEM(canopy.shape, f32),
            pltpu.VMEM(column_slot.shape, jnp.int32),
            pltpu.VMEM((devices, 8, 128), f32),
            pltpu.VMEM((devices * 8, 128), f32),
            pltpu.VMEM((13 * (devices // 4), 512), jnp.bfloat16),
            pltpu.VMEM((16, 256, 512), jnp.bfloat16),
            pltpu.VMEM((13, 16, 512), f32),
            pltpu.VMEM(wide, f32),
            pltpu.VMEM(wide, f32),
            pltpu.VMEM(wide, f32),
            pltpu.VMEM(wide, f32),
            pltpu.VMEM(wide, f32),
            pltpu.VMEM(wide, f32),
            pltpu.VMEM(wide, f32),
            pltpu.VMEM((7,) + wide, f32),
            pltpu.VMEM((KRYLOV,) + wide, f32),
            pltpu.VMEM(tile, f32),
            pltpu.VMEM(tile, f32),
            pltpu.VMEM(tile, f32),
            pltpu.VMEM((ROWS, LANES), f32),
            pltpu.VMEM((2, 5, 32, 512), f32),
            pltpu.VMEM((2, 5, 32, 512), f32),
            pltpu.VMEM((2, 5, 16, 128), f32),
            pltpu.VMEM((2, 5, 16, 128), f32),
            pltpu.VMEM((2, 2, 5, 8, 128), f32),
            pltpu.VMEM((NEWTON, 2, 1, 128), f32),
            pltpu.VMEM((NEWTON, sizes[0], 1, 128), f32),
            pltpu.VMEM((NEWTON, sizes[1], 1, 128), f32),
            pltpu.SemaphoreType.DMA((6,)),
            pltpu.SemaphoreType.DMA((3,)),
            pltpu.SemaphoreType.DMA((2, 4, 8)),
            pltpu.SemaphoreType.DMA((2, NEWTON)),
            pltpu.SemaphoreType.DMA((2, NEWTON)),
        ],
        compiler_params=pltpu.CompilerParams(collective_id=0, has_side_effects=True),
        name="coupled_step",
    )(head_old, soil_type, soil_table, forcing, canopy, column_slot)


def solution(mesh):
    sizes = (mesh.shape["gx"], mesh.shape["gy"])
    return jax.shard_map(
        functools.partial(shards, sizes),
        mesh=mesh,
        in_specs=(
            P(None, "gx", "gy"),
            P(None, "gx", "gy"),
            P(),
            P(None, "gx", "gy"),
            P(None, ("gx", "gy")),
            P("gx", "gy"),
        ),
        out_specs=(P(None, "gx", "gy"), P(None, "gx", "gy")),
        check_vma=False,
    )
```

```python
import functools

import jax
import jax.numpy as jnp
from jax import lax
from jax.experimental import pallas as pl
from jax.experimental.pallas import tpu as pltpu
from jax.sharding import PartitionSpec as P

NEWTON = 2
KRYLOV = 3
CAP = 64

STORAGE = 4.0
EPSILON = 1e-06

SHIFT = 3.0
SCALE = 3.0

MESH = pl.DeviceIdType.MESH
OWN = (slice(0, 16), slice(0, 512))
RIM = ((slice(16, 24), slice(0, 512)), (slice(0, 24), slice(512, 640)))
HALO = 3
ROWS = 24
LANES = 640


def logistic(u):
    return 1.0 / (1.0 + jnp.exp(-u))


def ahead(x, axis):
    return pltpu.roll(x, x.shape[axis] - 1, axis)


def behind(x, axis):
    return pltpu.roll(x, 1, axis)


def krylov_weights(gram):
    def inner(vector, image):
        terms = [a * b for a, b in zip(vector, image) if a is not None]
        return functools.reduce(lambda a, b: a + b, terms)

    def image_of(vector):
        return [inner(vector, [gram[i][k] for i in range(4)]) for k in range(4)]

    beta = jnp.sqrt(gram[0][0] + EPSILON)
    basis = [[1.0 / beta, None, None, None]]
    images = [image_of(basis[0])]
    hessen = [[None] * KRYLOV for _ in range(KRYLOV + 1)]
    for j in range(KRYLOV):
        v = basis[j]
        w = [None] * 4
        for i in range(j + 2):
            if i <= j:
                w[i] = SHIFT * v[i]
            if i >= 1:
                term = SCALE * v[i - 1]
                w[i] = term if w[i] is None else w[i] + term
        for i in range(j + 1):
            product = inner(w, images[i])
            hessen[i][j] = product
            w = [a if b is None else a - product * b for a, b in zip(w, basis[i])]
        square = jnp.maximum(inner(w, image_of(w)), 0.0)
        length = jnp.sqrt(square + EPSILON)
        hessen[j + 1][j] = length
        if j + 1 < KRYLOV:
            basis.append([None if a is None else a / length for a in w])
            images.append(image_of(basis[-1]))

    def column(a, b):
        pairs = [(hessen[i][a], hessen[i][b]) for i in range(KRYLOV + 1)]
        terms = [x * y for x, y in pairs if x is not None and y is not None]
        return functools.reduce(lambda x, y: x + y, terms)

    factor = [[None] * KRYLOV for _ in range(KRYLOV)]
    for i in range(KRYLOV):
        for j in range(i + 1):
            value = column(i, j)
            for k in range(j):
                value = value - factor[i][k] * factor[j][k]
            factor[i][j] = jnp.sqrt(value) if i == j else value / factor[j][j]
    forward = []
    for row in range(KRYLOV):
        value = hessen[0][row] * beta
        for other in range(row):
            value = value - factor[row][other] * forward[other]
        forward.append(value / factor[row][row])
    y = [None] * KRYLOV
    for row in reversed(range(KRYLOV)):
        value = forward[row]
        for other in range(row + 1, KRYLOV):
            value = value - factor[other][row] * y[other]
        y[row] = value / factor[row][row]
    weights = []
    for i in range(KRYLOV):
        terms = [y[j] * basis[j][i] for j in range(KRYLOV) if basis[j][i] is not None]
        weights.append(functools.reduce(lambda a, b: a + b, terms))
    return weights


def kernel(
    sizes,
    head_in,
    soil_in,
    table_in,
    forcing_in,
    canopy_in,
    slot_in,
    out_ref,
    flux_ref,
    table_ref,
    soil_ref,
    forcing_ref,
    canopy_ref,
    slot_ref,
    send_c,
    recv_c,
    split,
    hot,
    records,
    head,
    soil,
    conduct,
    slope,
    ksat,
    steep,
    cap,
    coef,
    basis,
    wet,
    theta_old,
    source,
    mask,
    send_x,
    recv_x,
    send_y,
    recv_y,
    recv_k,
    part,
    gather,
    sem_in,
    sem_c,
    sem_e,
    sem_g,
):
    size_x, size_y = sizes
    devices = size_x * size_y
    layers = out_ref.shape[0]
    gx, gy = lax.axis_index("gx"), lax.axis_index("gy")
    me = gx * size_y + gy

    loads = [
        pltpu.make_async_copy(src, dst, sem_in.at[i])
        for i, (src, dst) in enumerate(
            (
                (canopy_in, canopy_ref),
                (head_in, head.at[:, 0:16, 0:512]),
                (soil_in, soil_ref),
                (slot_in, slot_ref),
                (forcing_in, forcing_ref),
                (table_in, table_ref),
            )
        )
    ]
    for load in loads:
        load.start()

    def wrap(value, size):
        return lax.rem(value + size, size)

    def others(visit):
        for dy in range(1, size_y):
            visit(gx, lax.rem(gy + dy, size_y))

        def ring(i, carry):
            far = (i + 1) // 2
            x = wrap(gx + jnp.where(lax.rem(i, 2) == 1, far, -far), size_x)
            for dy in range(size_y):
                visit(x, lax.rem(gy + dy, size_y))
            return carry

        lax.fori_loop(1, size_x, ring, 0)

    barrier = pltpu.get_barrier_semaphore()
    others(lambda x, y: pl.semaphore_signal(barrier, inc=1, device_id=(x, y), device_id_type=MESH))

    row = lax.broadcasted_iota(jnp.int32, (ROWS, LANES), 0)
    col = lax.broadcasted_iota(jnp.int32, (ROWS, LANES), 1)
    one, zero = jnp.float32(1.0), jnp.float32(0.0)
    in_x, in_y = (gx < size_x - 1, gx > 0), (gy < size_y - 1, gy > 0)
    has_next_x, has_prev_x = (jnp.where(there, one, zero) for there in in_x)
    has_next_y, has_prev_y = (jnp.where(there, one, zero) for there in in_y)
    inside_x = jnp.where(
        row < 16,
        1.0,
        jnp.where(row < 16 + HALO, has_next_x, jnp.where(row >= ROWS - HALO, has_prev_x, 0.0)),
    )
    inside_y = jnp.where(
        col < 512,
        1.0,
        jnp.where(col < 512 + HALO, has_next_y, jnp.where(col >= LANES - HALO, has_prev_y, 0.0)),
    )
    mask[...] = inside_x * inside_y

    def own(ref, k):
        return ref[k, 0:16, 0:512]

    def clear(k, carry):
        for ref in (head, soil, basis.at[0]):
            ref[k, 16:24, 0:512] = jnp.zeros((8, 512), jnp.float32)
            ref[k, 0:24, 512:640] = jnp.zeros((24, 128), jnp.float32)
        return carry

    lax.fori_loop(0, layers, clear, 0)
    for side in range(2):
        for slot in range(5):
            send_x[side, slot, 24:32, :] = jnp.zeros((8, 512), jnp.float32)

    low7 = lax.broadcasted_iota(jnp.int32, (7, 128), 1) < CAP

    def pack(q, carry):
        lanes = pl.ds(pl.multiple_of(q * 128, 128), 128)
        first, second = canopy_ref[0:7, lanes], canopy_ref[6:13, lanes]
        send_c[2 * q, 0:7] = jnp.where(low7, first, pltpu.roll(second, CAP, 1))
        send_c[2 * q + 1, 0:7] = jnp.where(low7, pltpu.roll(first, CAP, 1), second)
        return carry

    loads[0].wait()
    lax.fori_loop(0, devices // 2, pack, 0, unroll=4)
    quarter = size_x // 4

    def seat(x):
        return lax.rem(gx - x + quarter + size_x, size_x)

    def slab(x):
        return pl.ds(pl.multiple_of((seat(x) * size_y + gy) * 8, 8), 7)

    recv_c[slab(gx), :] = send_c[me, 0:7]

    next_x, prev_x = wrap(gx + 1, size_x), wrap(gx - 1, size_x)
    next_y, prev_y = wrap(gy + 1, size_y), wrap(gy - 1, size_y)
    lane16 = lax.broadcasted_iota(jnp.int32, (16, 128), 1)
    group16 = lane16 // 4
    lane24 = lax.broadcasted_iota(jnp.int32, (ROWS, 128), 1)
    early8 = lax.broadcasted_iota(jnp.int32, (8, 128), 0) < 4

    def start(number, slot, fields):
        for f, (ref, index) in enumerate(fields):
            up = jnp.zeros((16, 128), jnp.float32)
            down = jnp.zeros((16, 128), jnp.float32)
            for k in range(layers):
                rows = slice(HALO * k, HALO * (k + 1))
                send_x[0, slot + f, rows, :] = ref[index + (k, slice(16 - HALO, 16), slice(0, 512))]
                send_x[1, slot + f, rows, :] = ref[index + (k, slice(0, HALO), slice(0, 512))]
                last = ref[index + (k, slice(0, 16), slice(384, 512))]
                first = ref[index + (k, slice(0, 16), slice(0, 128))]
                here = group16 == k
                up = jnp.where(here, pltpu.roll(last, 4 * k + 4, 1), up)
                down = jnp.where(here, pltpu.roll(first, 4 * k, 1) if k else first, down)
            send_y[0, slot + f] = up
            send_y[1, slot + f] = down
        slots = pl.ds(slot, len(fields))
        plan = []
        for side, y in enumerate((next_y, prev_y)):
            for turn, x in enumerate((next_x, prev_x)):
                edge = pl.ds(8 * (1 - turn), 8)
                plan.append(
                    (
                        send_y.at[side, slots, edge],
                        recv_k.at[side, turn, slots],
                        (x, y),
                        in_x[turn] & in_y[side],
                        in_x[1 - turn] & in_y[1 - side],
                    )
                )
        for side, x in enumerate((next_x, prev_x)):
            plan.append(
                (send_x.at[side, slots], recv_x.at[side, slots], (x, gy), in_x[side], in_x[1 - side])
            )
        for side, y in enumerate((next_y, prev_y)):
            plan.append(
                (send_y.at[side, slots], recv_y.at[side, slots], (gx, y), in_y[side], in_y[1 - side])
            )
        moves = []
        for i, (src, dst, target, sends, receives) in enumerate(plan):
            move = pltpu.make_async_remote_copy(
                src_ref=src,
                dst_ref=dst,
                send_sem=sem_e.at[0, number, i],
                recv_sem=sem_e.at[1, number, i],
                device_id=target,
                device_id_type=MESH,
            )
            moves.append((move, sends, receives))
        for i in (4, 5, 0, 1, 2, 3, 6, 7):
            move, sends, _ = moves[i]
            pl.when(sends)(move.start)
        return moves

    def await_all(moves):
        for move, _, receives in moves:
            pl.when(receives)(move.wait_recv)

    def drain(moves):
        for move, sends, _ in moves:
            pl.when(sends)(move.wait_send)

    def finish(moves, slot, fields):
        await_all(moves[6:] + moves[:4])
        edge = mask[:, 512:640]
        for f, (ref, index) in enumerate(fields):
            sides = [
                jnp.concatenate(
                    [
                        recv_y[side, slot + f],
                        jnp.where(early8, recv_k[side, 1, slot + f], recv_k[side, 0, slot + f]),
                    ],
                    axis=0,
                )
                for side in range(2)
            ]
            for k in range(layers):
                left = pltpu.roll(sides[0], 128 - (4 * k + 4), 1)
                right = pltpu.roll(sides[1], 128 - 4 * k, 1) if k else sides[1]
                both = jnp.where(lane24 < 64, right, left)
                ref[index + (k, slice(0, ROWS), slice(512, 640))] = jnp.where(edge > 0.0, both, 0.0)
        await_all(moves[4:6])
        for f, (ref, index) in enumerate(fields):
            for k in range(layers):
                rows = slice(HALO * k, HALO * (k + 1))
                after = jnp.where(in_x[0], recv_x[1, slot + f, rows, :], 0.0)
                before = jnp.where(in_x[1], recv_x[0, slot + f, rows, :], 0.0)
                ref[index + (k, slice(16, 16 + HALO), slice(0, 512))] = after
                ref[index + (k, slice(ROWS - HALO, ROWS), slice(0, 512))] = before

    loads[1].wait()
    loads[2].wait()

    def convert(k, carry):
        soil[k, 0:16, 0:512] = soil_ref[k].astype(jnp.float32)
        return carry

    lax.fori_loop(0, layers, convert, 0)

    pl.semaphore_wait(barrier, devices - 1)

    def scatter(x, y):
        pltpu.make_async_remote_copy(
            src_ref=send_c.at[x * size_y + y, pl.ds(0, 7)],
            dst_ref=recv_c.at[slab(x)],
            send_sem=sem_c.at[0],
            recv_sem=sem_c.at[1],
            device_id=(x, y),
            device_id_type=MESH,
        ).start()

    opening = [(head, ()), (soil, ())]
    moves = start(0, 0, opening)
    started = [moves]
    others(scatter)

    def look_up(rows, lanes):
        def layer(k, carry):
            kind = soil[k, rows, lanes]
            values = [jnp.zeros(kind.shape, jnp.float32) for _ in range(3)]
            for c in range(table_ref.shape[1]):
                match = kind == float(c)
                values = [jnp.where(match, table_ref[p, c], v) for p, v in enumerate(values)]
            ksat[k, rows, lanes] = values[0] * mask[rows, lanes]
            steep[k, rows, lanes] = values[1]
            cap[k, rows, lanes] = values[2]
            return carry

        lax.fori_loop(0, layers, layer, 0)

    loads[5].wait()
    look_up(*OWN)

    def saturate(rows, lanes, keep):
        def layer(k, carry):
            a, ks, c = (ref[k, rows, lanes] for ref in (steep, ksat, cap))
            s = logistic(a * head[k, rows, lanes])
            rise = a * s * (1.0 - s)
            conduct[k, rows, lanes] = ks * (0.1 + 0.9 * s * s)
            slope[k, rows, lanes] = 0.9 * ks * s * rise
            coef[0, k, rows, lanes] = STORAGE * c * rise
            keep(k, s, c)
            return carry

        lax.fori_loop(0, layers, layer, 0, unroll=2)

    def keep_old(k, s, c):
        wet[k] = s
        theta_old[k] = c * s

    def keep_residual(k, s, c):
        basis[0, k, 0:16, 0:512] = STORAGE * (c * s - theta_old[k]) - source[k]

    def keep_none(k, s, c):
        pass

    saturate(*OWN, keep_old)

    loads[3].wait()
    within = lax.broadcasted_iota(jnp.int32, (256, 512), 0)

    def seats_of(x):
        slot = jnp.maximum(slot_ref[pl.ds(x, 1), :], 0)
        shift = (size_y * CAP).bit_length() - 1
        seat = ((slot >> shift) - gx + quarter) & (size_x - 1)
        return (seat << shift) + (slot & (size_y * CAP - 1))

    def spot(x, carry):
        slot = seats_of(x)
        hot[x] = jnp.where(within == (slot & 255), 1.0, 0.0).astype(jnp.bfloat16)
        return carry

    lax.fori_loop(0, 16, spot, 0)

    finish(moves, 0, opening)
    for region in RIM:
        look_up(*region)

    def around(k):
        return jnp.minimum(k + 1, layers - 1), jnp.maximum(k - 1, 0)

    def balance(added):
        def layer(k, carry):
            h, kk = head[k], conduct[k]
            total = basis[0, k, 0:16, 0:512] if added else 0.0
            for axis in range(2):
                flow = 0.5 * (kk + ahead(kk, axis)) * (h - ahead(h, axis))
                total = total + (flow - behind(flow, axis))[0:16, 0:512]
            below, above = around(k)
            h, kk = own(head, k), own(conduct, k)
            flow = 0.5 * (kk + own(conduct, below)) * (h - own(head, below) + 1.0)
            total = total + jnp.where(k == layers - 1, kk, flow)
            flow = 0.5 * (own(conduct, above) + kk) * (own(head, above) - h + 1.0)
            basis[0, k, 0:16, 0:512] = total - jnp.where(k == 0, 0.0, flow)
            return carry

        lax.fori_loop(0, layers, layer, 0, unroll=2)

    def linearize():
        def layer(k, carry):
            scaled = mask[...] * (1.0 / SCALE)
            h, kk, dk = head[k], conduct[k], slope[k]
            diagonal = coef[0, k] - SHIFT
            for axis, at in ((0, 1), (1, 3)):
                drop = h - ahead(h, axis)
                mean = 0.5 * (kk + ahead(kk, axis))
                mine = dk * drop + mean
                other = ahead(dk, axis) * drop - mean
                diagonal = diagonal + mine - behind(other, axis)
                coef[at, k] = other * scaled
                coef[at + 1, k] = -behind(mine, axis) * scaled
            below, above = around(k)
            bottom, top = k == layers - 1, k == 0
            drop = h - head[below] + 1.0
            mean = 0.5 * (kk + conduct[below])
            diagonal = diagonal + jnp.where(bottom, 2.0 * dk, dk * drop + mean)
            coef[5, k] = jnp.where(bottom, 0.0, slope[below] * drop - mean) * scaled
            drop = head[above] - h + 1.0
            mean = 0.5 * (kk + conduct[above])
            diagonal = diagonal - jnp.where(top, 0.0, dk * drop - mean)
            coef[6, k] = -jnp.where(top, 0.0, slope[above] * drop + mean) * scaled
            coef[0, k] = diagonal * scaled
            return carry

        lax.fori_loop(0, layers, layer, 0)

    for region in RIM:
        saturate(*region, keep_none)
    balance(False)

    blocks = devices // 4
    low = lax.broadcasted_iota(jnp.int32, (blocks, 128), 1) < CAP
    which = lax.broadcasted_iota(jnp.int32, (blocks, 512), 0)

    def choose():
        arrived = send_c.at[pl.ds(0, devices - 1), pl.ds(0, 7)]
        pltpu.make_async_copy(arrived, arrived, sem_c.at[1]).wait()

        def put(r, left, right):
            value = jnp.concatenate([left, right], axis=1)
            high = value.astype(jnp.bfloat16)
            rows = slice(blocks * r, blocks * (r + 1))
            split[rows, 0:256] = high
            split[rows, 256:512] = (value - high.astype(jnp.float32)).astype(jnp.bfloat16)

        for r in range(7):
            plain = [recv_c[pl.ds(r + 8 * c, blocks, stride=32), :] for c in range(4)]
            moved = [pltpu.roll(x, CAP, 1) for x in plain]
            put(r, jnp.where(low, plain[0], moved[1]), jnp.where(low, plain[2], moved[3]))
            if r >= 1:
                put(r + 6, jnp.where(low, moved[0], plain[1]), jnp.where(low, moved[2], plain[3]))

        def select(x, carry):
            found = jnp.dot(
                split[...], jnp.concatenate([hot[x], hot[x]], axis=0), preferred_element_type=jnp.float32
            )
            match = which == seats_of(x) >> 8
            for r in range(13):
                piece = jnp.where(match, found[blocks * r : blocks * (r + 1)], 0.0)
                records[r, pl.ds(x, 1), :] = jnp.sum(piece, axis=0, keepdims=True)
            return carry

        lax.fori_loop(0, 16, select, 0, unroll=16)

    choose()
    loads[4].wait()
    sunlight, air, humidity, rainfall = (forcing_ref[i] for i in range(4))
    leaf, albedo, resist = (records[i] for i in range(3))
    total, roots = jnp.zeros_like(leaf), jnp.zeros_like(leaf)
    for k in range(layers):
        total = total + records[3 + k] * wet[k]
        roots = roots + records[3 + k]
    conductance = total / roots * leaf / (leaf + resist)
    exchange_coef = 0.5 + 0.3 * leaf
    radiation = (1.0 - albedo) * sunlight + 0.3
    surface = air
    for _ in range(2):
        vapour = 0.5 * jnp.exp(2.0 * (surface - air))
        square = surface * surface
        excess = (
            radiation
            - 0.3 * square * square
            - exchange_coef * (surface - air)
            - conductance * (vapour - humidity)
        )
        tangent = -1.2 * square * surface - exchange_coef - 2.0 * conductance * vapour
        surface = surface - excess / tangent
    evaporation = conductance * (0.5 * jnp.exp(2.0 * (surface - air)) - humidity)
    ks_top = own(ksat, 0)
    infiltration = rainfall * ks_top / (rainfall + ks_top)
    land = slot_ref[...] >= 0
    evaporation = jnp.where(land, evaporation, 0.0)
    infiltration = jnp.where(land, infiltration, 0.0)
    flux_ref[0] = evaporation
    flux_ref[1] = infiltration
    share = evaporation / total
    for k in range(layers):
        gain = -jnp.where(land, share * records[3 + k] * wet[k], 0.0)
        if k == 0:
            gain = gain + infiltration
        source[k] = gain
        basis[0, k, 0:16, 0:512] -= gain

    def fold(product):
        tall = product[0:8] + product[8:16]
        return (tall[:, 0:128] + tall[:, 128:256]) + (tall[:, 256:384] + tall[:, 384:512])

    lane1 = lax.broadcasted_iota(jnp.int32, (1, 128), 1)

    def place(partial, at, sums):
        for i, value in enumerate(sums):
            line = jnp.sum(value, axis=0, keepdims=True)
            partial = jnp.where(lane1 == at + i, jnp.sum(line, axis=1, keepdims=True), partial)
        return partial

    def matvec(j):
        rows, lanes = (slice(0, ROWS), slice(0, LANES)) if j + 1 < KRYLOV else (slice(0, 16), slice(0, 512))

        def layer(k, carry):
            v = basis[j, k]
            below, above = around(k)

            def term(i, value):
                return coef[i, k, rows, lanes] * value[rows, lanes]

            w = term(0, v)
            w = w + term(1, ahead(v, 0)) + term(2, behind(v, 0))
            w = w + term(3, ahead(v, 1)) + term(4, behind(v, 1))
            w = w + coef[5, k, rows, lanes] * basis[j, below, rows, lanes]
            w = w + coef[6, k, rows, lanes] * basis[j, above, rows, lanes]
            if j + 1 < KRYLOV:
                basis[j + 1, k] = w
            mine = w[0:16, 0:512]
            sums = [fold(mine * basis[i, k, 0:16, 0:512]) for i in range(j + 1)]
            sums.append(fold(mine * mine))
            return tuple(a + b for a, b in zip(carry, sums))

        zeros = tuple(jnp.zeros((8, 128), jnp.float32) for _ in range(j + 2))
        return lax.fori_loop(0, layers, layer, zeros, unroll=2)

    def square_of_start():
        def layer(k, carry):
            value = basis[0, k, 0:16, 0:512]
            return carry + fold(value * value)

        return [lax.fori_loop(0, layers, layer, jnp.zeros((8, 128), jnp.float32))]

    def reduce_all(n, partial):
        mine = part.at[n]
        mine[...] = partial
        gather[n, me] = partial

        def send(x, y):
            pltpu.make_async_remote_copy(
                src_ref=mine,
                dst_ref=gather.at[n, me],
                send_sem=sem_g.at[0, n],
                recv_sem=sem_g.at[1, n],
                device_id=(x, y),
                device_id_type=MESH,
            ).start()

        others(send)
        rest = gather.at[n, pl.ds(0, devices - 1)]
        pltpu.make_async_copy(rest, rest, sem_g.at[1, n]).wait()
        sums = [gather[n, i] for i in range(4)]
        for i in range(4, devices, 4):
            sums = [a + gather[n, i + k] for k, a in enumerate(sums)]
        return (sums[0] + sums[1]) + (sums[2] + sums[3])

    for n in range(NEWTON):
        field = [(basis, (0,))]
        moves = start(1 + n, 2 + n, field)
        started.append(moves)
        partial = place(jnp.zeros((1, 128), jnp.float32), 0, square_of_start())
        if not n:
            linearize()
        else:
            finish(head_moves, 4, [(head, ())])
            for region in RIM:
                saturate(*region, keep_none)
            linearize()
        finish(moves, 2 + n, field)
        for j, at in ((0, 1), (1, 3), (2, 6)):
            partial = place(partial, at, matvec(j))
        sums = reduce_all(n, partial)
        gram = [[None] * 4 for _ in range(4)]
        at = 0
        for i in range(4):
            for j in range(i + 1):
                gram[i][j] = gram[j][i] = jnp.broadcast_to(sums[:, at : at + 1], (1, 128))
                at += 1
        weights = [w[:, 0:1] for w in krylov_weights(gram)]
        last = n + 1 == NEWTON
        rows, lanes = (slice(0, 16), slice(0, 512)) if last else (slice(0, ROWS), slice(0, LANES))

        def update(k, carry):
            value = head[k, rows, lanes]
            for i in range(KRYLOV):
                value = value - weights[i] * basis[i, k, rows, lanes]
            if last:
                out_ref[k] = value
            else:
                head[k] = value
            return carry

        lax.fori_loop(0, layers, update, 0)
        if not last:
            head_moves = start(3, 4, [(head, ())])
            started.append(head_moves)
            saturate(*OWN, keep_residual)
            for region in RIM:
                saturate(*region, keep_none)
            balance(True)

    for moves in started:
        drain(moves)
    sent = send_c.at[pl.ds(0, devices - 1), pl.ds(0, 7)]
    pltpu.make_async_copy(sent, sent, sem_c.at[0]).wait()
    for n in range(NEWTON):
        sent = gather.at[n, pl.ds(0, devices - 1)]
        pltpu.make_async_copy(sent, sent, sem_g.at[0, n]).wait()


def shards(sizes, head_old, soil_type, soil_table, forcing, canopy, column_slot):
    layers = head_old.shape[0]
    devices = sizes[0] * sizes[1]
    f32 = jnp.float32
    wide = (layers, ROWS, LANES)
    tile = (layers, 16, 512)
    vmem, anywhere = pl.BlockSpec(memory_space=pltpu.VMEM), pl.BlockSpec(memory_space=pl.ANY)
    return pl.pallas_call(
        functools.partial(kernel, sizes),
        out_shape=(
            jax.ShapeDtypeStruct(head_old.shape, f32),
            jax.ShapeDtypeStruct((2, 16, 512), f32),
        ),
        in_specs=[anywhere] * 6,
        out_specs=(vmem, vmem),
        scratch_shapes=[
            pltpu.SMEM(soil_table.shape, f32),
            pltpu.VMEM(tile, jnp.int32),
            pltpu.VMEM(forcing.shape, f32),
            pltpu.VMEM(canopy.shape, f32),
            pltpu.VMEM(column_slot.shape, jnp.int32),
            pltpu.VMEM((devices, 8, 128), f32),
            pltpu.VMEM((devices * 8, 128), f32),
            pltpu.VMEM((13 * (devices // 4), 512), jnp.bfloat16),
            pltpu.VMEM((16, 256, 512), jnp.bfloat16),
            pltpu.VMEM((13, 16, 512), f32),
            pltpu.VMEM(wide, f32),
            pltpu.VMEM(wide, f32),
            pltpu.VMEM(wide, f32),
            pltpu.VMEM(wide, f32),
            pltpu.VMEM(wide, f32),
            pltpu.VMEM(wide, f32),
            pltpu.VMEM(wide, f32),
            pltpu.VMEM((7,) + wide, f32),
            pltpu.VMEM((KRYLOV,) + wide, f32),
            pltpu.VMEM(tile, f32),
            pltpu.VMEM(tile, f32),
            pltpu.VMEM(tile, f32),
            pltpu.VMEM((ROWS, LANES), f32),
            pltpu.VMEM((2, 5, 32, 512), f32),
            pltpu.VMEM((2, 5, 32, 512), f32),
            pltpu.VMEM((2, 5, 16, 128), f32),
            pltpu.VMEM((2, 5, 16, 128), f32),
            pltpu.VMEM((2, 2, 5, 8, 128), f32),
            pltpu.VMEM((NEWTON, 1, 128), f32),
            pltpu.VMEM((NEWTON, devices, 1, 128), f32),
            pltpu.SemaphoreType.DMA((6,)),
            pltpu.SemaphoreType.DMA((3,)),
            pltpu.SemaphoreType.DMA((2, 4, 8)),
            pltpu.SemaphoreType.DMA((2, NEWTON)),
        ],
        compiler_params=pltpu.CompilerParams(collective_id=0, has_side_effects=True),
        name="coupled_step",
    )(head_old, soil_type, soil_table, forcing, canopy, column_slot)


def solution(mesh):
    sizes = (mesh.shape["gx"], mesh.shape["gy"])
    return jax.shard_map(
        functools.partial(shards, sizes),
        mesh=mesh,
        in_specs=(
            P(None, "gx", "gy"),
            P(None, "gx", "gy"),
            P(),
            P(None, "gx", "gy"),
            P(None, ("gx", "gy")),
            P("gx", "gy"),
        ),
        out_specs=(P(None, "gx", "gy"), P(None, "gx", "gy")),
        check_vma=False,
    )
```

```python
import functools

import jax
import jax.numpy as jnp
from jax import lax
from jax.experimental import pallas as pl
from jax.experimental.pallas import tpu as pltpu
from jax.sharding import PartitionSpec as P

NEWTON = 2
KRYLOV = 3
CAP = 64

STORAGE = 4.0
EPSILON = 1e-06

SHIFT = 3.0
SCALE = 3.0

MESH = pl.DeviceIdType.MESH
OWN = (slice(0, 16), slice(0, 512))
RIM = ((slice(16, 24), slice(0, 512)), (slice(0, 24), slice(512, 640)))
HALO = 3
ROWS = 24
LANES = 640


def logistic(u):
    return 1.0 / (1.0 + jnp.exp(-u))


def ahead(x, axis):
    return pltpu.roll(x, x.shape[axis] - 1, axis)


def behind(x, axis):
    return pltpu.roll(x, 1, axis)


def krylov_weights(gram):
    def inner(vector, image):
        terms = [a * b for a, b in zip(vector, image) if a is not None]
        return functools.reduce(lambda a, b: a + b, terms)

    def image_of(vector):
        return [inner(vector, [gram[i][k] for i in range(4)]) for k in range(4)]

    beta = jnp.sqrt(gram[0][0] + EPSILON)
    basis = [[1.0 / beta, None, None, None]]
    images = [image_of(basis[0])]
    hessen = [[None] * KRYLOV for _ in range(KRYLOV + 1)]
    for j in range(KRYLOV):
        v = basis[j]
        w = [None] * 4
        for i in range(j + 2):
            if i <= j:
                w[i] = SHIFT * v[i]
            if i >= 1:
                term = SCALE * v[i - 1]
                w[i] = term if w[i] is None else w[i] + term
        for i in range(j + 1):
            product = inner(w, images[i])
            hessen[i][j] = product
            w = [a if b is None else a - product * b for a, b in zip(w, basis[i])]
        square = jnp.maximum(inner(w, image_of(w)), 0.0)
        length = jnp.sqrt(square + EPSILON)
        hessen[j + 1][j] = length
        if j + 1 < KRYLOV:
            basis.append([None if a is None else a / length for a in w])
            images.append(image_of(basis[-1]))

    def column(a, b):
        pairs = [(hessen[i][a], hessen[i][b]) for i in range(KRYLOV + 1)]
        terms = [x * y for x, y in pairs if x is not None and y is not None]
        return functools.reduce(lambda x, y: x + y, terms)

    factor = [[None] * KRYLOV for _ in range(KRYLOV)]
    for i in range(KRYLOV):
        for j in range(i + 1):
            value = column(i, j)
            for k in range(j):
                value = value - factor[i][k] * factor[j][k]
            factor[i][j] = jnp.sqrt(value) if i == j else value / factor[j][j]
    forward = []
    for row in range(KRYLOV):
        value = hessen[0][row] * beta
        for other in range(row):
            value = value - factor[row][other] * forward[other]
        forward.append(value / factor[row][row])
    y = [None] * KRYLOV
    for row in reversed(range(KRYLOV)):
        value = forward[row]
        for other in range(row + 1, KRYLOV):
            value = value - factor[other][row] * y[other]
        y[row] = value / factor[row][row]
    weights = []
    for i in range(KRYLOV):
        terms = [y[j] * basis[j][i] for j in range(KRYLOV) if basis[j][i] is not None]
        weights.append(functools.reduce(lambda a, b: a + b, terms))
    return weights


def kernel(
    sizes,
    head_in,
    soil_in,
    table_in,
    forcing_in,
    canopy_in,
    slot_in,
    out_ref,
    flux_ref,
    table_ref,
    soil_ref,
    forcing_ref,
    canopy_ref,
    slot_ref,
    send_c,
    recv_c,
    split,
    hot,
    records,
    head,
    soil,
    conduct,
    slope,
    ksat,
    steep,
    cap,
    coef,
    basis,
    wet,
    theta_old,
    source,
    mask,
    send_x,
    recv_x,
    send_y,
    recv_y,
    recv_k,
    part,
    gather,
    sem_in,
    sem_c,
    sem_e,
    sem_g,
):
    size_x, size_y = sizes
    devices = size_x * size_y
    layers = out_ref.shape[0]
    gx, gy = lax.axis_index("gx"), lax.axis_index("gy")
    me = gx * size_y + gy

    loads = [
        pltpu.make_async_copy(src, dst, sem_in.at[i])
        for i, (src, dst) in enumerate(
            (
                (canopy_in, canopy_ref),
                (head_in, head.at[:, 0:16, 0:512]),
                (soil_in, soil_ref),
                (slot_in, slot_ref),
                (forcing_in, forcing_ref),
                (table_in, table_ref),
            )
        )
    ]
    for load in loads:
        load.start()

    def wrap(value, size):
        return lax.rem(value + size, size)

    def others(visit):
        for dy in range(1, size_y):
            visit(gx, lax.rem(gy + dy, size_y))

        def ring(i, carry):
            far = (i + 1) // 2
            x = wrap(gx + jnp.where(lax.rem(i, 2) == 1, far, -far), size_x)
            for dy in range(size_y):
                visit(x, lax.rem(gy + dy, size_y))
            return carry

        lax.fori_loop(1, size_x, ring, 0)

    barrier = pltpu.get_barrier_semaphore()
    others(lambda x, y: pl.semaphore_signal(barrier, inc=1, device_id=(x, y), device_id_type=MESH))

    row = lax.broadcasted_iota(jnp.int32, (ROWS, LANES), 0)
    col = lax.broadcasted_iota(jnp.int32, (ROWS, LANES), 1)
    one, zero = jnp.float32(1.0), jnp.float32(0.0)
    in_x, in_y = (gx < size_x - 1, gx > 0), (gy < size_y - 1, gy > 0)
    has_next_x, has_prev_x = (jnp.where(there, one, zero) for there in in_x)
    has_next_y, has_prev_y = (jnp.where(there, one, zero) for there in in_y)
    inside_x = jnp.where(
        row < 16,
        1.0,
        jnp.where(row < 16 + HALO, has_next_x, jnp.where(row >= ROWS - HALO, has_prev_x, 0.0)),
    )
    inside_y = jnp.where(
        col < 512,
        1.0,
        jnp.where(col < 512 + HALO, has_next_y, jnp.where(col >= LANES - HALO, has_prev_y, 0.0)),
    )
    mask[...] = inside_x * inside_y

    def own(ref, k):
        return ref[k, 0:16, 0:512]

    def clear(k, carry):
        for ref in (head, soil, basis.at[0]):
            ref[k, 16:24, 0:512] = jnp.zeros((8, 512), jnp.float32)
            ref[k, 0:24, 512:640] = jnp.zeros((24, 128), jnp.float32)
        return carry

    lax.fori_loop(0, layers, clear, 0)
    for side in range(2):
        for slot in range(5):
            send_x[side, slot, 24:32, :] = jnp.zeros((8, 512), jnp.float32)

    low7 = lax.broadcasted_iota(jnp.int32, (7, 128), 1) < CAP

    def pack(q, carry):
        lanes = pl.ds(pl.multiple_of(q * 128, 128), 128)
        first, second = canopy_ref[0:7, lanes], canopy_ref[6:13, lanes]
        send_c[2 * q, 0:7] = jnp.where(low7, first, pltpu.roll(second, CAP, 1))
        send_c[2 * q + 1, 0:7] = jnp.where(low7, pltpu.roll(first, CAP, 1), second)
        return carry

    loads[0].wait()
    lax.fori_loop(0, devices // 2, pack, 0, unroll=4)
    quarter = size_x // 4

    def seat(x):
        return lax.rem(gx - x + quarter + size_x, size_x)

    def slab(x):
        return pl.ds(pl.multiple_of((seat(x) * size_y + gy) * 8, 8), 7)

    recv_c[slab(gx), :] = send_c[me, 0:7]

    next_x, prev_x = wrap(gx + 1, size_x), wrap(gx - 1, size_x)
    next_y, prev_y = wrap(gy + 1, size_y), wrap(gy - 1, size_y)
    lane16 = lax.broadcasted_iota(jnp.int32, (16, 128), 1)
    group16 = lane16 // 4
    lane24 = lax.broadcasted_iota(jnp.int32, (ROWS, 128), 1)
    early8 = lax.broadcasted_iota(jnp.int32, (8, 128), 0) < 4

    def start(number, slot, fields):
        for f, (ref, index) in enumerate(fields):
            up = jnp.zeros((16, 128), jnp.float32)
            down = jnp.zeros((16, 128), jnp.float32)
            for k in range(layers):
                rows = slice(HALO * k, HALO * (k + 1))
                send_x[0, slot + f, rows, :] = ref[index + (k, slice(16 - HALO, 16), slice(0, 512))]
                send_x[1, slot + f, rows, :] = ref[index + (k, slice(0, HALO), slice(0, 512))]
                last = ref[index + (k, slice(0, 16), slice(384, 512))]
                first = ref[index + (k, slice(0, 16), slice(0, 128))]
                here = group16 == k
                up = jnp.where(here, pltpu.roll(last, 4 * k + 4, 1), up)
                down = jnp.where(here, pltpu.roll(first, 4 * k, 1) if k else first, down)
            send_y[0, slot + f] = up
            send_y[1, slot + f] = down
        slots = pl.ds(slot, len(fields))
        plan = []
        for side, y in enumerate((next_y, prev_y)):
            for turn, x in enumerate((next_x, prev_x)):
                edge = pl.ds(8 * (1 - turn), 8)
                plan.append(
                    (
                        send_y.at[side, slots, edge],
                        recv_k.at[side, turn, slots],
                        (x, y),
                        in_x[turn] & in_y[side],
                        in_x[1 - turn] & in_y[1 - side],
                    )
                )
        for side, x in enumerate((next_x, prev_x)):
            plan.append(
                (send_x.at[side, slots], recv_x.at[side, slots], (x, gy), in_x[side], in_x[1 - side])
            )
        for side, y in enumerate((next_y, prev_y)):
            plan.append(
                (send_y.at[side, slots], recv_y.at[side, slots], (gx, y), in_y[side], in_y[1 - side])
            )
        moves = []
        for i, (src, dst, target, sends, receives) in enumerate(plan):
            move = pltpu.make_async_remote_copy(
                src_ref=src,
                dst_ref=dst,
                send_sem=sem_e.at[0, number, i],
                recv_sem=sem_e.at[1, number, i],
                device_id=target,
                device_id_type=MESH,
            )
            moves.append((move, sends, receives))
        for i in (4, 5, 0, 1, 2, 3, 6, 7):
            move, sends, _ = moves[i]
            pl.when(sends)(move.start)
        return moves

    def await_all(moves):
        for move, _, receives in moves:
            pl.when(receives)(move.wait_recv)

    def drain(moves):
        for move, sends, _ in moves:
            pl.when(sends)(move.wait_send)

    def finish(moves, slot, fields):
        await_all(moves[6:] + moves[:4])
        edge = mask[:, 512:640]
        for f, (ref, index) in enumerate(fields):
            sides = [
                jnp.concatenate(
                    [
                        recv_y[side, slot + f],
                        jnp.where(early8, recv_k[side, 1, slot + f], recv_k[side, 0, slot + f]),
                    ],
                    axis=0,
                )
                for side in range(2)
            ]
            for k in range(layers):
                left = pltpu.roll(sides[0], 128 - (4 * k + 4), 1)
                right = pltpu.roll(sides[1], 128 - 4 * k, 1) if k else sides[1]
                both = jnp.where(lane24 < 64, right, left)
                ref[index + (k, slice(0, ROWS), slice(512, 640))] = jnp.where(edge > 0.0, both, 0.0)
        await_all(moves[4:6])
        for f, (ref, index) in enumerate(fields):
            for k in range(layers):
                rows = slice(HALO * k, HALO * (k + 1))
                after = jnp.where(in_x[0], recv_x[1, slot + f, rows, :], 0.0)
                before = jnp.where(in_x[1], recv_x[0, slot + f, rows, :], 0.0)
                ref[index + (k, slice(16, 16 + HALO), slice(0, 512))] = after
                ref[index + (k, slice(ROWS - HALO, ROWS), slice(0, 512))] = before

    loads[1].wait()
    loads[2].wait()

    def convert(k, carry):
        soil[k, 0:16, 0:512] = soil_ref[k].astype(jnp.float32)
        return carry

    lax.fori_loop(0, layers, convert, 0)

    pl.semaphore_wait(barrier, devices - 1)

    def scatter(x, y):
        pltpu.make_async_remote_copy(
            src_ref=send_c.at[x * size_y + y, pl.ds(0, 7)],
            dst_ref=recv_c.at[slab(x)],
            send_sem=sem_c.at[0],
            recv_sem=sem_c.at[1],
            device_id=(x, y),
            device_id_type=MESH,
        ).start()

    opening = [(head, ()), (soil, ())]
    moves = start(0, 0, opening)
    started = [moves]
    others(scatter)

    def look_up(rows, lanes):
        def layer(k, carry):
            kind = soil[k, rows, lanes]
            values = [jnp.zeros(kind.shape, jnp.float32) for _ in range(3)]
            for c in range(table_ref.shape[1]):
                match = kind == float(c)
                values = [jnp.where(match, table_ref[p, c], v) for p, v in enumerate(values)]
            ksat[k, rows, lanes] = values[0] * mask[rows, lanes]
            steep[k, rows, lanes] = values[1]
            cap[k, rows, lanes] = values[2]
            return carry

        lax.fori_loop(0, layers, layer, 0, unroll=2)

    loads[5].wait()
    look_up(*OWN)

    def saturate(rows, lanes, keep):
        def layer(k, carry):
            a, ks, c = (ref[k, rows, lanes] for ref in (steep, ksat, cap))
            s = logistic(a * head[k, rows, lanes])
            rise = a * s * (1.0 - s)
            conduct[k, rows, lanes] = ks * (0.1 + 0.9 * s * s)
            slope[k, rows, lanes] = 0.9 * ks * s * rise
            coef[0, k, rows, lanes] = STORAGE * c * rise
            keep(k, s, c)
            return carry

        lax.fori_loop(0, layers, layer, 0, unroll=2)

    def keep_old(k, s, c):
        wet[k] = s
        theta_old[k] = c * s

    def keep_residual(k, s, c):
        basis[0, k, 0:16, 0:512] = STORAGE * (c * s - theta_old[k]) - source[k]

    def keep_none(k, s, c):
        pass

    saturate(*OWN, keep_old)

    loads[3].wait()
    within = lax.broadcasted_iota(jnp.int32, (256, 512), 0)

    def seats_of(x):
        slot = jnp.maximum(slot_ref[pl.ds(x, 1), :], 0)
        shift = (size_y * CAP).bit_length() - 1
        seat = ((slot >> shift) - gx + quarter) & (size_x - 1)
        return (seat << shift) + (slot & (size_y * CAP - 1))

    def spot(x, carry):
        slot = seats_of(x)
        hot[x] = jnp.where(within == (slot & 255), 1.0, 0.0).astype(jnp.bfloat16)
        return carry

    lax.fori_loop(0, 16, spot, 0)

    finish(moves, 0, opening)
    for region in RIM:
        look_up(*region)

    def around(k):
        return jnp.minimum(k + 1, layers - 1), jnp.maximum(k - 1, 0)

    def balance(added):
        def layer(k, carry):
            h, kk = head[k], conduct[k]
            total = basis[0, k, 0:16, 0:512] if added else 0.0
            for axis in range(2):
                flow = 0.5 * (kk + ahead(kk, axis)) * (h - ahead(h, axis))
                total = total + (flow - behind(flow, axis))[0:16, 0:512]
            below, above = around(k)
            h, kk = own(head, k), own(conduct, k)
            flow = 0.5 * (kk + own(conduct, below)) * (h - own(head, below) + 1.0)
            total = total + jnp.where(k == layers - 1, kk, flow)
            flow = 0.5 * (own(conduct, above) + kk) * (own(head, above) - h + 1.0)
            basis[0, k, 0:16, 0:512] = total - jnp.where(k == 0, 0.0, flow)
            return carry

        lax.fori_loop(0, layers, layer, 0, unroll=2)

    def linearize():
        def layer(k, carry):
            scaled = mask[...] * (1.0 / SCALE)
            h, kk, dk = head[k], conduct[k], slope[k]
            diagonal = coef[0, k] - SHIFT
            for axis, at in ((0, 1), (1, 3)):
                drop = h - ahead(h, axis)
                mean = 0.5 * (kk + ahead(kk, axis))
                mine = dk * drop + mean
                other = ahead(dk, axis) * drop - mean
                diagonal = diagonal + mine - behind(other, axis)
                coef[at, k] = other * scaled
                coef[at + 1, k] = -behind(mine, axis) * scaled
            below, above = around(k)
            bottom, top = k == layers - 1, k == 0
            drop = h - head[below] + 1.0
            mean = 0.5 * (kk + conduct[below])
            diagonal = diagonal + jnp.where(bottom, 2.0 * dk, dk * drop + mean)
            coef[5, k] = jnp.where(bottom, 0.0, slope[below] * drop - mean) * scaled
            drop = head[above] - h + 1.0
            mean = 0.5 * (kk + conduct[above])
            diagonal = diagonal - jnp.where(top, 0.0, dk * drop - mean)
            coef[6, k] = -jnp.where(top, 0.0, slope[above] * drop + mean) * scaled
            coef[0, k] = diagonal * scaled
            return carry

        lax.fori_loop(0, layers, layer, 0, unroll=2)

    for region in RIM:
        saturate(*region, keep_none)
    balance(False)

    blocks = devices // 4
    low = lax.broadcasted_iota(jnp.int32, (blocks, 128), 1) < CAP
    which = lax.broadcasted_iota(jnp.int32, (blocks, 512), 0)

    def choose():
        arrived = send_c.at[pl.ds(0, devices - 1), pl.ds(0, 7)]
        pltpu.make_async_copy(arrived, arrived, sem_c.at[1]).wait()

        def put(r, left, right):
            value = jnp.concatenate([left, right], axis=1)
            high = value.astype(jnp.bfloat16)
            rows = slice(blocks * r, blocks * (r + 1))
            split[rows, 0:256] = high
            split[rows, 256:512] = (value - high.astype(jnp.float32)).astype(jnp.bfloat16)

        for r in range(7):
            plain = [recv_c[pl.ds(r + 8 * c, blocks, stride=32), :] for c in range(4)]
            moved = [pltpu.roll(x, CAP, 1) for x in plain]
            put(r, jnp.where(low, plain[0], moved[1]), jnp.where(low, plain[2], moved[3]))
            if r >= 1:
                put(r + 6, jnp.where(low, moved[0], plain[1]), jnp.where(low, moved[2], plain[3]))

        def select(x, carry):
            found = jnp.dot(
                split[...], jnp.concatenate([hot[x], hot[x]], axis=0), preferred_element_type=jnp.float32
            )
            match = which == seats_of(x) >> 8
            for r in range(13):
                piece = jnp.where(match, found[blocks * r : blocks * (r + 1)], 0.0)
                records[r, pl.ds(x, 1), :] = jnp.sum(piece, axis=0, keepdims=True)
            return carry

        lax.fori_loop(0, 16, select, 0, unroll=16)

    choose()
    loads[4].wait()
    sunlight, air, humidity, rainfall = (forcing_ref[i] for i in range(4))
    leaf, albedo, resist = (records[i] for i in range(3))
    total, roots = jnp.zeros_like(leaf), jnp.zeros_like(leaf)
    for k in range(layers):
        total = total + records[3 + k] * wet[k]
        roots = roots + records[3 + k]
    conductance = total / roots * leaf / (leaf + resist)
    exchange_coef = 0.5 + 0.3 * leaf
    radiation = (1.0 - albedo) * sunlight + 0.3
    surface = air
    for _ in range(2):
        vapour = 0.5 * jnp.exp(2.0 * (surface - air))
        square = surface * surface
        excess = (
            radiation
            - 0.3 * square * square
            - exchange_coef * (surface - air)
            - conductance * (vapour - humidity)
        )
        tangent = -1.2 * square * surface - exchange_coef - 2.0 * conductance * vapour
        surface = surface - excess / tangent
    evaporation = conductance * (0.5 * jnp.exp(2.0 * (surface - air)) - humidity)
    ks_top = own(ksat, 0)
    infiltration = rainfall * ks_top / (rainfall + ks_top)
    land = slot_ref[...] >= 0
    evaporation = jnp.where(land, evaporation, 0.0)
    infiltration = jnp.where(land, infiltration, 0.0)
    flux_ref[0] = evaporation
    flux_ref[1] = infiltration
    share = evaporation / total
    for k in range(layers):
        gain = -jnp.where(land, share * records[3 + k] * wet[k], 0.0)
        if k == 0:
            gain = gain + infiltration
        source[k] = gain
        basis[0, k, 0:16, 0:512] -= gain

    def fold(product):
        tall = product[0:8] + product[8:16]
        return (tall[:, 0:128] + tall[:, 128:256]) + (tall[:, 256:384] + tall[:, 384:512])

    lane1 = lax.broadcasted_iota(jnp.int32, (1, 128), 1)

    def place(partial, at, sums):
        for i, value in enumerate(sums):
            line = jnp.sum(value, axis=0, keepdims=True)
            partial = jnp.where(lane1 == at + i, jnp.sum(line, axis=1, keepdims=True), partial)
        return partial

    def matvec(j):
        rows, lanes = (slice(0, ROWS), slice(0, LANES)) if j + 1 < KRYLOV else (slice(0, 16), slice(0, 512))

        def layer(k, carry):
            v = basis[j, k]
            below, above = around(k)

            def term(i, value):
                return coef[i, k, rows, lanes] * value[rows, lanes]

            w = term(0, v)
            w = w + term(1, ahead(v, 0)) + term(2, behind(v, 0))
            w = w + term(3, ahead(v, 1)) + term(4, behind(v, 1))
            w = w + coef[5, k, rows, lanes] * basis[j, below, rows, lanes]
            w = w + coef[6, k, rows, lanes] * basis[j, above, rows, lanes]
            if j + 1 < KRYLOV:
                basis[j + 1, k] = w
            mine = w[0:16, 0:512]
            sums = [fold(mine * basis[i, k, 0:16, 0:512]) for i in range(j + 1)]
            sums.append(fold(mine * mine))
            return tuple(a + b for a, b in zip(carry, sums))

        zeros = tuple(jnp.zeros((8, 128), jnp.float32) for _ in range(j + 2))
        return lax.fori_loop(0, layers, layer, zeros, unroll=5)

    def square_of_start():
        def layer(k, carry):
            value = basis[0, k, 0:16, 0:512]
            return carry + fold(value * value)

        return [lax.fori_loop(0, layers, layer, jnp.zeros((8, 128), jnp.float32))]

    def reduce_all(n, partial):
        mine = part.at[n]
        mine[...] = partial
        gather[n, me] = partial

        def send(x, y):
            pltpu.make_async_remote_copy(
                src_ref=mine,
                dst_ref=gather.at[n, me],
                send_sem=sem_g.at[0, n],
                recv_sem=sem_g.at[1, n],
                device_id=(x, y),
                device_id_type=MESH,
            ).start()

        others(send)
        rest = gather.at[n, pl.ds(0, devices - 1)]
        pltpu.make_async_copy(rest, rest, sem_g.at[1, n]).wait()
        sums = [gather[n, i] for i in range(4)]
        for i in range(4, devices, 4):
            sums = [a + gather[n, i + k] for k, a in enumerate(sums)]
        return (sums[0] + sums[1]) + (sums[2] + sums[3])

    for n in range(NEWTON):
        field = [(basis, (0,))]
        moves = start(1 + n, 2 + n, field)
        started.append(moves)
        partial = place(jnp.zeros((1, 128), jnp.float32), 0, square_of_start())
        if not n:
            linearize()
        else:
            finish(head_moves, 4, [(head, ())])
            for region in RIM:
                saturate(*region, keep_none)
            linearize()
        finish(moves, 2 + n, field)
        for j, at in ((0, 1), (1, 3), (2, 6)):
            partial = place(partial, at, matvec(j))
        sums = reduce_all(n, partial)
        gram = [[None] * 4 for _ in range(4)]
        at = 0
        for i in range(4):
            for j in range(i + 1):
                gram[i][j] = gram[j][i] = jnp.broadcast_to(sums[:, at : at + 1], (1, 128))
                at += 1
        weights = [w[:, 0:1] for w in krylov_weights(gram)]
        last = n + 1 == NEWTON
        rows, lanes = (slice(0, 16), slice(0, 512)) if last else (slice(0, ROWS), slice(0, LANES))

        def update(k, carry):
            value = head[k, rows, lanes]
            for i in range(KRYLOV):
                value = value - weights[i] * basis[i, k, rows, lanes]
            if last:
                out_ref[k] = value
            else:
                head[k] = value
            return carry

        lax.fori_loop(0, layers, update, 0)
        if not last:
            head_moves = start(3, 4, [(head, ())])
            started.append(head_moves)
            saturate(*OWN, keep_residual)
            for region in RIM:
                saturate(*region, keep_none)
            balance(True)

    for moves in started:
        drain(moves)
    sent = send_c.at[pl.ds(0, devices - 1), pl.ds(0, 7)]
    pltpu.make_async_copy(sent, sent, sem_c.at[0]).wait()
    for n in range(NEWTON):
        sent = gather.at[n, pl.ds(0, devices - 1)]
        pltpu.make_async_copy(sent, sent, sem_g.at[0, n]).wait()


def shards(sizes, head_old, soil_type, soil_table, forcing, canopy, column_slot):
    inputs = (head_old, soil_type, soil_table, forcing, canopy, column_slot)
    layers = head_old.shape[0]
    devices = sizes[0] * sizes[1]
    f32 = jnp.float32
    wide = (layers, ROWS, LANES)
    tile = (layers, 16, 512)
    vmem, anywhere = pl.BlockSpec(memory_space=pltpu.VMEM), pl.BlockSpec(memory_space=pl.ANY)
    return pl.pallas_call(
        functools.partial(kernel, sizes),
        out_shape=(
            jax.ShapeDtypeStruct(head_old.shape, f32),
            jax.ShapeDtypeStruct((2, 16, 512), f32),
        ),
        in_specs=[anywhere] * 6,
        out_specs=(vmem, vmem),
        scratch_shapes=[
            pltpu.SMEM(soil_table.shape, f32),
            pltpu.VMEM(tile, jnp.int32),
            pltpu.VMEM(forcing.shape, f32),
            pltpu.VMEM(canopy.shape, f32),
            pltpu.VMEM(column_slot.shape, jnp.int32),
            pltpu.VMEM((devices, 8, 128), f32),
            pltpu.VMEM((devices * 8, 128), f32),
            pltpu.VMEM((13 * (devices // 4), 512), jnp.bfloat16),
            pltpu.VMEM((16, 256, 512), jnp.bfloat16),
            pltpu.VMEM((13, 16, 512), f32),
            pltpu.VMEM(wide, f32),
            pltpu.VMEM(wide, f32),
            pltpu.VMEM(wide, f32),
            pltpu.VMEM(wide, f32),
            pltpu.VMEM(wide, f32),
            pltpu.VMEM(wide, f32),
            pltpu.VMEM(wide, f32),
            pltpu.VMEM((7,) + wide, f32),
            pltpu.VMEM((KRYLOV,) + wide, f32),
            pltpu.VMEM(tile, f32),
            pltpu.VMEM(tile, f32),
            pltpu.VMEM(tile, f32),
            pltpu.VMEM((ROWS, LANES), f32),
            pltpu.VMEM((2, 5, 32, 512), f32),
            pltpu.VMEM((2, 5, 32, 512), f32),
            pltpu.VMEM((2, 5, 16, 128), f32),
            pltpu.VMEM((2, 5, 16, 128), f32),
            pltpu.VMEM((2, 2, 5, 8, 128), f32),
            pltpu.VMEM((NEWTON, 1, 128), f32),
            pltpu.VMEM((NEWTON, devices, 1, 128), f32),
            pltpu.SemaphoreType.DMA((6,)),
            pltpu.SemaphoreType.DMA((3,)),
            pltpu.SemaphoreType.DMA((2, 4, 8)),
            pltpu.SemaphoreType.DMA((2, NEWTON)),
        ],
        compiler_params=pltpu.CompilerParams(
            collective_id=0, has_side_effects=True, vmem_limit_bytes=48 * 1024 * 1024
        ),
        name="coupled_step",
    )(*(pltpu.with_memory_space_constraint(x, pltpu.HBM) for x in inputs))


def solution(mesh):
    sizes = (mesh.shape["gx"], mesh.shape["gy"])
    return jax.shard_map(
        functools.partial(shards, sizes),
        mesh=mesh,
        in_specs=(
            P(None, "gx", "gy"),
            P(None, "gx", "gy"),
            P(),
            P(None, "gx", "gy"),
            P(None, ("gx", "gy")),
            P("gx", "gy"),
        ),
        out_specs=(P(None, "gx", "gy"), P(None, "gx", "gy")),
        check_vma=False,
    )
```

```python
import functools

import jax
import jax.numpy as jnp
from jax import lax
from jax.experimental import pallas as pl
from jax.experimental.pallas import tpu as pltpu
from jax.sharding import PartitionSpec as P

NEWTON = 2
KRYLOV = 3
CAP = 64

STORAGE = 4.0
EPSILON = 1e-06

SHIFT = 3.0
SCALE = 3.0

MESH = pl.DeviceIdType.MESH
OWN = (slice(0, 16), slice(0, 512))
RIM = ((slice(16, 24), slice(0, 512)), (slice(0, 24), slice(512, 640)))
HALO = 3
ROWS = 24
LANES = 640


def logistic(u):
    return 1.0 / (1.0 + jnp.exp(-u))


def ahead(x, axis):
    return pltpu.roll(x, x.shape[axis] - 1, axis)


def behind(x, axis):
    return pltpu.roll(x, 1, axis)


def krylov_weights(gram):
    def inner(vector, image):
        terms = [a * b for a, b in zip(vector, image) if a is not None]
        return functools.reduce(lambda a, b: a + b, terms)

    def image_of(vector):
        return [inner(vector, [gram[i][k] for i in range(4)]) for k in range(4)]

    beta = jnp.sqrt(gram[0][0] + EPSILON)
    basis = [[1.0 / beta, None, None, None]]
    images = [image_of(basis[0])]
    hessen = [[None] * KRYLOV for _ in range(KRYLOV + 1)]
    for j in range(KRYLOV):
        v = basis[j]
        w = [None] * 4
        for i in range(j + 2):
            if i <= j:
                w[i] = SHIFT * v[i]
            if i >= 1:
                term = SCALE * v[i - 1]
                w[i] = term if w[i] is None else w[i] + term
        for i in range(j + 1):
            product = inner(w, images[i])
            hessen[i][j] = product
            w = [a if b is None else a - product * b for a, b in zip(w, basis[i])]
        square = jnp.maximum(inner(w, image_of(w)), 0.0)
        length = jnp.sqrt(square + EPSILON)
        hessen[j + 1][j] = length
        if j + 1 < KRYLOV:
            basis.append([None if a is None else a / length for a in w])
            images.append(image_of(basis[-1]))

    def column(a, b):
        pairs = [(hessen[i][a], hessen[i][b]) for i in range(KRYLOV + 1)]
        terms = [x * y for x, y in pairs if x is not None and y is not None]
        return functools.reduce(lambda x, y: x + y, terms)

    factor = [[None] * KRYLOV for _ in range(KRYLOV)]
    for i in range(KRYLOV):
        for j in range(i + 1):
            value = column(i, j)
            for k in range(j):
                value = value - factor[i][k] * factor[j][k]
            factor[i][j] = jnp.sqrt(value) if i == j else value / factor[j][j]
    forward = []
    for row in range(KRYLOV):
        value = hessen[0][row] * beta
        for other in range(row):
            value = value - factor[row][other] * forward[other]
        forward.append(value / factor[row][row])
    y = [None] * KRYLOV
    for row in reversed(range(KRYLOV)):
        value = forward[row]
        for other in range(row + 1, KRYLOV):
            value = value - factor[other][row] * y[other]
        y[row] = value / factor[row][row]
    weights = []
    for i in range(KRYLOV):
        terms = [y[j] * basis[j][i] for j in range(KRYLOV) if basis[j][i] is not None]
        weights.append(functools.reduce(lambda a, b: a + b, terms))
    return weights


def kernel(
    sizes,
    head_in,
    soil_in,
    table_in,
    forcing_in,
    canopy_in,
    slot_in,
    out_ref,
    flux_ref,
    table_ref,
    soil_ref,
    forcing_ref,
    canopy_ref,
    slot_ref,
    send_c,
    recv_c,
    split,
    hot,
    records,
    head,
    soil,
    conduct,
    slope,
    ksat,
    steep,
    cap,
    coef,
    basis,
    wet,
    theta_old,
    source,
    mask,
    send_x,
    recv_x,
    send_w,
    recv_w,
    send_y,
    recv_y,
    recv_k,
    part,
    gather,
    sem_in,
    sem_c,
    sem_e,
    sem_g,
):
    size_x, size_y = sizes
    devices = size_x * size_y
    layers = out_ref.shape[0]
    gx, gy = lax.axis_index("gx"), lax.axis_index("gy")
    me = gx * size_y + gy

    loads = [
        pltpu.make_async_copy(src, dst, sem_in.at[i])
        for i, (src, dst) in enumerate(
            (
                (canopy_in, canopy_ref),
                (head_in, head.at[:, 0:16, 0:512]),
                (soil_in, soil_ref),
                (slot_in, slot_ref),
                (forcing_in, forcing_ref),
                (table_in, table_ref),
            )
        )
    ]
    for load in loads:
        load.start()

    def wrap(value, size):
        return lax.rem(value + size, size)

    def others(visit):
        for dy in range(1, size_y):
            visit(gx, lax.rem(gy + dy, size_y))

        def ring(i, carry):
            far = (i + 1) // 2
            x = wrap(gx + jnp.where(lax.rem(i, 2) == 1, far, -far), size_x)
            for dy in range(size_y):
                visit(x, lax.rem(gy + dy, size_y))
            return carry

        lax.fori_loop(1, size_x, ring, 0)

    barrier = pltpu.get_barrier_semaphore()
    others(lambda x, y: pl.semaphore_signal(barrier, inc=1, device_id=(x, y), device_id_type=MESH))

    row = lax.broadcasted_iota(jnp.int32, (ROWS, LANES), 0)
    col = lax.broadcasted_iota(jnp.int32, (ROWS, LANES), 1)
    one, zero = jnp.float32(1.0), jnp.float32(0.0)
    in_x, in_y = (gx < size_x - 1, gx > 0), (gy < size_y - 1, gy > 0)
    has_next_x, has_prev_x = (jnp.where(there, one, zero) for there in in_x)
    has_next_y, has_prev_y = (jnp.where(there, one, zero) for there in in_y)
    inside_x = jnp.where(
        row < 16,
        1.0,
        jnp.where(row < 16 + HALO, has_next_x, jnp.where(row >= ROWS - HALO, has_prev_x, 0.0)),
    )
    inside_y = jnp.where(
        col < 512,
        1.0,
        jnp.where(col < 512 + HALO, has_next_y, jnp.where(col >= LANES - HALO, has_prev_y, 0.0)),
    )
    mask[...] = inside_x * inside_y

    def own(ref, k):
        return ref[k, 0:16, 0:512]

    def clear(k, carry):
        for ref in (head, soil, basis.at[0]):
            ref[k, 16:24, 0:512] = jnp.zeros((8, 512), jnp.float32)
            ref[k, 0:24, 512:640] = jnp.zeros((24, 128), jnp.float32)
        return carry

    lax.fori_loop(0, layers, clear, 0)
    for side in range(2):
        for slot in range(5):
            send_x[side, slot, 24:32, :] = jnp.zeros((8, 512), jnp.float32)
        for slot in range(2):
            send_w[side, slot, 8:16, :] = jnp.zeros((8, 512), jnp.float32)

    low7 = lax.broadcasted_iota(jnp.int32, (7, 128), 1) < CAP

    def pack(q, carry):
        lanes = pl.ds(pl.multiple_of(q * 128, 128), 128)
        first, second = canopy_ref[0:7, lanes], canopy_ref[6:13, lanes]
        send_c[2 * q, 0:7] = jnp.where(low7, first, pltpu.roll(second, CAP, 1))
        send_c[2 * q + 1, 0:7] = jnp.where(low7, pltpu.roll(first, CAP, 1), second)
        return carry

    loads[0].wait()
    lax.fori_loop(0, devices // 2, pack, 0, unroll=4)
    quarter = size_x // 4

    def seat(x):
        return lax.rem(gx - x + quarter + size_x, size_x)

    def slab(x):
        return pl.ds(pl.multiple_of((seat(x) * size_y + gy) * 8, 8), 7)

    recv_c[slab(gx), :] = send_c[me, 0:7]

    next_x, prev_x = wrap(gx + 1, size_x), wrap(gx - 1, size_x)
    next_y, prev_y = wrap(gy + 1, size_y), wrap(gy - 1, size_y)
    lane16 = lax.broadcasted_iota(jnp.int32, (16, 128), 1)
    group16 = lane16 // 4
    lane24 = lax.broadcasted_iota(jnp.int32, (ROWS, 128), 1)
    early8 = lax.broadcasted_iota(jnp.int32, (8, 128), 0) < 4

    def send_all(number, plan):
        moves = []
        for i, src, dst, target, sends, receives in plan:
            move = pltpu.make_async_remote_copy(
                src_ref=src,
                dst_ref=dst,
                send_sem=sem_e.at[0, number, i],
                recv_sem=sem_e.at[1, number, i],
                device_id=target,
                device_id_type=MESH,
            )
            moves.append((move, sends, receives))
        for move, sends, _ in moves:
            pl.when(sends)(move.start)
        return moves

    def start_x(number, slot, fields, depth):
        send, recv = (send_x, recv_x) if depth == HALO else (send_w, recv_w)
        for f, (ref, index) in enumerate(fields):
            for k in range(layers):
                rows = slice(depth * k, depth * (k + 1))
                send[0, slot + f, rows, :] = ref[index + (k, slice(16 - depth, 16), slice(0, 512))]
                send[1, slot + f, rows, :] = ref[index + (k, slice(0, depth), slice(0, 512))]
        slots = pl.ds(slot, len(fields))
        return send_all(
            number,
            [
                (side, send.at[side, slots], recv.at[side, slots], (x, gy), in_x[side], in_x[1 - side])
                for side, x in enumerate((next_x, prev_x))
            ],
        )

    def start_y(number, slot, fields):
        for f, (ref, index) in enumerate(fields):
            up = jnp.zeros((16, 128), jnp.float32)
            down = jnp.zeros((16, 128), jnp.float32)
            for k in range(layers):
                last = ref[index + (k, slice(0, 16), slice(384, 512))]
                first = ref[index + (k, slice(0, 16), slice(0, 128))]
                here = group16 == k
                up = jnp.where(here, pltpu.roll(last, 4 * k + 4, 1), up)
                down = jnp.where(here, pltpu.roll(first, 4 * k, 1) if k else first, down)
            send_y[0, slot + f] = up
            send_y[1, slot + f] = down
        slots = pl.ds(slot, len(fields))
        plan = []
        for side, y in enumerate((next_y, prev_y)):
            for turn, x in enumerate((next_x, prev_x)):
                plan.append(
                    (
                        2 + 2 * side + turn,
                        send_y.at[side, slots, pl.ds(8 * (1 - turn), 8)],
                        recv_k.at[side, turn, slots],
                        (x, y),
                        in_x[turn] & in_y[side],
                        in_x[1 - turn] & in_y[1 - side],
                    )
                )
        for side, y in enumerate((next_y, prev_y)):
            plan.append(
                (
                    6 + side,
                    send_y.at[side, slots],
                    recv_y.at[side, slots],
                    (gx, y),
                    in_y[side],
                    in_y[1 - side],
                )
            )
        return send_all(number, plan)

    def start(number, slot, fields):
        moves = start_x(number, slot, fields, HALO)
        return moves, start_y(number, slot, fields)

    def await_all(moves):
        for move, _, receives in moves:
            pl.when(receives)(move.wait_recv)

    def drain(moves):
        for move, sends, _ in moves:
            pl.when(sends)(move.wait_send)

    def finish_y(moves, slot, fields):
        await_all(moves)
        edge = mask[:, 512:640]
        for f, (ref, index) in enumerate(fields):
            sides = [
                jnp.concatenate(
                    [
                        recv_y[side, slot + f],
                        jnp.where(early8, recv_k[side, 1, slot + f], recv_k[side, 0, slot + f]),
                    ],
                    axis=0,
                )
                for side in range(2)
            ]
            for k in range(layers):
                left = pltpu.roll(sides[0], 128 - (4 * k + 4), 1)
                right = pltpu.roll(sides[1], 128 - 4 * k, 1) if k else sides[1]
                both = jnp.where(lane24 < 64, right, left)
                ref[index + (k, slice(0, ROWS), slice(512, 640))] = jnp.where(edge > 0.0, both, 0.0)

    def finish_x(moves, slot, fields, depth):
        recv = recv_x if depth == HALO else recv_w
        await_all(moves)
        for f, (ref, index) in enumerate(fields):
            for k in range(layers):
                rows = slice(depth * k, depth * (k + 1))
                after = jnp.where(in_x[0], recv[1, slot + f, rows, :], 0.0)
                before = jnp.where(in_x[1], recv[0, slot + f, rows, :], 0.0)
                ref[index + (k, slice(16, 16 + depth), slice(0, 512))] = after
                ref[index + (k, slice(ROWS - depth, ROWS), slice(0, 512))] = before

    def finish(moves, slot, fields):
        finish_y(moves[1], slot, fields)
        finish_x(moves[0], slot, fields, HALO)

    loads[1].wait()
    loads[2].wait()

    def convert(k, carry):
        soil[k, 0:16, 0:512] = soil_ref[k].astype(jnp.float32)
        return carry

    lax.fori_loop(0, layers, convert, 0)

    pl.semaphore_wait(barrier, devices - 1)

    def scatter(x, y):
        pltpu.make_async_remote_copy(
            src_ref=send_c.at[x * size_y + y, pl.ds(0, 7)],
            dst_ref=recv_c.at[slab(x)],
            send_sem=sem_c.at[0],
            recv_sem=sem_c.at[1],
            device_id=(x, y),
            device_id_type=MESH,
        ).start()

    opening = [(head, ()), (soil, ())]
    near = start_x(0, 0, opening, 1), start_y(0, 0, opening)
    started = [*near]
    others(scatter)

    def look_up(rows, lanes):
        def layer(k, carry):
            kind = soil[k, rows, lanes]
            values = [jnp.zeros(kind.shape, jnp.float32) for _ in range(3)]
            for c in range(table_ref.shape[1]):
                match = kind == float(c)
                values = [jnp.where(match, table_ref[p, c], v) for p, v in enumerate(values)]
            ksat[k, rows, lanes] = values[0] * mask[rows, lanes]
            steep[k, rows, lanes] = values[1]
            cap[k, rows, lanes] = values[2]
            return carry

        lax.fori_loop(0, layers, layer, 0, unroll=2)

    loads[5].wait()
    look_up(*OWN)

    def saturate(rows, lanes, keep):
        def layer(k, carry):
            a, ks, c = (ref[k, rows, lanes] for ref in (steep, ksat, cap))
            s = logistic(a * head[k, rows, lanes])
            rise = a * s * (1.0 - s)
            conduct[k, rows, lanes] = ks * (0.1 + 0.9 * s * s)
            slope[k, rows, lanes] = 0.9 * ks * s * rise
            coef[0, k, rows, lanes] = STORAGE * c * rise
            keep(k, s, c)
            return carry

        lax.fori_loop(0, layers, layer, 0, unroll=2)

    def keep_old(k, s, c):
        wet[k] = s
        theta_old[k] = c * s

    def keep_residual(k, s, c):
        basis[0, k, 0:16, 0:512] = STORAGE * (c * s - theta_old[k]) - source[k]

    def keep_none(k, s, c):
        pass

    saturate(*OWN, keep_old)

    loads[3].wait()
    within = lax.broadcasted_iota(jnp.int32, (256, 512), 0)

    def seats_of(x):
        slot = jnp.maximum(slot_ref[pl.ds(x, 1), :], 0)
        shift = (size_y * CAP).bit_length() - 1
        seat = ((slot >> shift) - gx + quarter) & (size_x - 1)
        return (seat << shift) + (slot & (size_y * CAP - 1))

    def spot(x, carry):
        slot = seats_of(x)
        hot[x] = jnp.where(within == (slot & 255), 1.0, 0.0).astype(jnp.bfloat16)
        return carry

    lax.fori_loop(0, 16, spot, 0)

    finish_y(near[1], 0, opening)
    finish_x(near[0], 0, opening, 1)
    for region in RIM:
        look_up(*region)

    def around(k):
        return jnp.minimum(k + 1, layers - 1), jnp.maximum(k - 1, 0)

    def balance(added):
        def layer(k, carry):
            h, kk = head[k], conduct[k]
            total = basis[0, k, 0:16, 0:512] if added else 0.0
            for axis in range(2):
                flow = 0.5 * (kk + ahead(kk, axis)) * (h - ahead(h, axis))
                total = total + (flow - behind(flow, axis))[0:16, 0:512]
            below, above = around(k)
            h, kk = own(head, k), own(conduct, k)
            flow = 0.5 * (kk + own(conduct, below)) * (h - own(head, below) + 1.0)
            total = total + jnp.where(k == layers - 1, kk, flow)
            flow = 0.5 * (own(conduct, above) + kk) * (own(head, above) - h + 1.0)
            basis[0, k, 0:16, 0:512] = total - jnp.where(k == 0, 0.0, flow)
            return carry

        lax.fori_loop(0, layers, layer, 0, unroll=2)

    def linearize():
        def layer(k, carry):
            scaled = mask[...] * (1.0 / SCALE)
            h, kk, dk = head[k], conduct[k], slope[k]
            diagonal = coef[0, k] - SHIFT
            for axis, at in ((0, 1), (1, 3)):
                drop = h - ahead(h, axis)
                mean = 0.5 * (kk + ahead(kk, axis))
                mine = dk * drop + mean
                other = ahead(dk, axis) * drop - mean
                diagonal = diagonal + mine - behind(other, axis)
                coef[at, k] = other * scaled
                coef[at + 1, k] = -behind(mine, axis) * scaled
            below, above = around(k)
            bottom, top = k == layers - 1, k == 0
            drop = h - head[below] + 1.0
            mean = 0.5 * (kk + conduct[below])
            diagonal = diagonal + jnp.where(bottom, 2.0 * dk, dk * drop + mean)
            coef[5, k] = jnp.where(bottom, 0.0, slope[below] * drop - mean) * scaled
            drop = head[above] - h + 1.0
            mean = 0.5 * (kk + conduct[above])
            diagonal = diagonal - jnp.where(top, 0.0, dk * drop - mean)
            coef[6, k] = -jnp.where(top, 0.0, slope[above] * drop + mean) * scaled
            coef[0, k] = diagonal * scaled
            return carry

        lax.fori_loop(0, layers, layer, 0, unroll=2)

    for region in RIM:
        saturate(*region, keep_none)
    balance(False)
    deep = start_x(4, 0, opening, HALO)
    started.append(deep)

    blocks = devices // 4
    low = lax.broadcasted_iota(jnp.int32, (blocks, 128), 1) < CAP
    which = lax.broadcasted_iota(jnp.int32, (blocks, 512), 0)

    def choose():
        arrived = send_c.at[pl.ds(0, devices - 1), pl.ds(0, 7)]
        pltpu.make_async_copy(arrived, arrived, sem_c.at[1]).wait()

        def put(r, left, right):
            value = jnp.concatenate([left, right], axis=1)
            high = value.astype(jnp.bfloat16)
            rows = slice(blocks * r, blocks * (r + 1))
            split[rows, 0:256] = high
            split[rows, 256:512] = (value - high.astype(jnp.float32)).astype(jnp.bfloat16)

        for r in range(7):
            plain = [recv_c[pl.ds(r + 8 * c, blocks, stride=32), :] for c in range(4)]
            moved = [pltpu.roll(x, CAP, 1) for x in plain]
            put(r, jnp.where(low, plain[0], moved[1]), jnp.where(low, plain[2], moved[3]))
            if r >= 1:
                put(r + 6, jnp.where(low, moved[0], plain[1]), jnp.where(low, moved[2], plain[3]))

        def select(x, carry):
            found = jnp.dot(
                split[...], jnp.concatenate([hot[x], hot[x]], axis=0), preferred_element_type=jnp.float32
            )
            match = which == seats_of(x) >> 8
            for r in range(13):
                piece = jnp.where(match, found[blocks * r : blocks * (r + 1)], 0.0)
                records[r, pl.ds(x, 1), :] = jnp.sum(piece, axis=0, keepdims=True)
            return carry

        lax.fori_loop(0, 16, select, 0, unroll=16)

    choose()
    loads[4].wait()
    sunlight, air, humidity, rainfall = (forcing_ref[i] for i in range(4))
    leaf, albedo, resist = (records[i] for i in range(3))
    total, roots = jnp.zeros_like(leaf), jnp.zeros_like(leaf)
    for k in range(layers):
        total = total + records[3 + k] * wet[k]
        roots = roots + records[3 + k]
    conductance = total / roots * leaf / (leaf + resist)
    exchange_coef = 0.5 + 0.3 * leaf
    radiation = (1.0 - albedo) * sunlight + 0.3
    surface = air
    for _ in range(2):
        vapour = 0.5 * jnp.exp(2.0 * (surface - air))
        square = surface * surface
        excess = (
            radiation
            - 0.3 * square * square
            - exchange_coef * (surface - air)
            - conductance * (vapour - humidity)
        )
        tangent = -1.2 * square * surface - exchange_coef - 2.0 * conductance * vapour
        surface = surface - excess / tangent
    evaporation = conductance * (0.5 * jnp.exp(2.0 * (surface - air)) - humidity)
    ks_top = own(ksat, 0)
    infiltration = rainfall * ks_top / (rainfall + ks_top)
    land = slot_ref[...] >= 0
    evaporation = jnp.where(land, evaporation, 0.0)
    infiltration = jnp.where(land, infiltration, 0.0)
    flux_ref[0] = evaporation
    flux_ref[1] = infiltration
    share = evaporation / total
    for k in range(layers):
        gain = -jnp.where(land, share * records[3 + k] * wet[k], 0.0)
        if k == 0:
            gain = gain + infiltration
        source[k] = gain
        basis[0, k, 0:16, 0:512] -= gain

    def fold(product):
        tall = product[0:8] + product[8:16]
        return (tall[:, 0:128] + tall[:, 128:256]) + (tall[:, 256:384] + tall[:, 384:512])

    lane1 = lax.broadcasted_iota(jnp.int32, (1, 128), 1)

    def place(partial, at, sums):
        for i, value in enumerate(sums):
            line = jnp.sum(value, axis=0, keepdims=True)
            partial = jnp.where(lane1 == at + i, jnp.sum(line, axis=1, keepdims=True), partial)
        return partial

    def matvec(j):
        rows, lanes = (slice(0, ROWS), slice(0, LANES)) if j + 1 < KRYLOV else (slice(0, 16), slice(0, 512))

        def layer(k, carry):
            v = basis[j, k]
            below, above = around(k)

            def term(i, value):
                return coef[i, k, rows, lanes] * value[rows, lanes]

            w = term(0, v)
            w = w + term(1, ahead(v, 0)) + term(2, behind(v, 0))
            w = w + term(3, ahead(v, 1)) + term(4, behind(v, 1))
            w = w + coef[5, k, rows, lanes] * basis[j, below, rows, lanes]
            w = w + coef[6, k, rows, lanes] * basis[j, above, rows, lanes]
            if j + 1 < KRYLOV:
                basis[j + 1, k] = w
            mine = w[0:16, 0:512]
            sums = [fold(mine * basis[i, k, 0:16, 0:512]) for i in range(j + 1)]
            sums.append(fold(mine * mine))
            return tuple(a + b for a, b in zip(carry, sums))

        zeros = tuple(jnp.zeros((8, 128), jnp.float32) for _ in range(j + 2))
        return lax.fori_loop(0, layers, layer, zeros, unroll=5)

    def square_of_start():
        def layer(k, carry):
            value = basis[0, k, 0:16, 0:512]
            return carry + fold(value * value)

        return [lax.fori_loop(0, layers, layer, jnp.zeros((8, 128), jnp.float32))]

    def hops(step):
        x, y = step
        return sum((0, 1, 2, 1)[i % 4] for i in (x, x // 4, y // 2))

    steps = [(x, y) for x in range(size_x) for y in range(size_y) if x or y]
    farthest = sorted(steps, key=hops, reverse=True)

    def reduce_all(n, partial):
        mine = part.at[n]
        mine[...] = partial
        gather[n, me] = partial

        def send(x, y):
            pltpu.make_async_remote_copy(
                src_ref=mine,
                dst_ref=gather.at[n, me],
                send_sem=sem_g.at[0, n],
                recv_sem=sem_g.at[1, n],
                device_id=(x, y),
                device_id_type=MESH,
            ).start()

        for x, y in farthest:
            send(lax.rem(gx + x, size_x), lax.rem(gy + y, size_y))
        rest = gather.at[n, pl.ds(0, devices - 1)]
        pltpu.make_async_copy(rest, rest, sem_g.at[1, n]).wait()
        sums = [gather[n, i] for i in range(4)]
        for i in range(4, devices, 4):
            sums = [a + gather[n, i + k] for k, a in enumerate(sums)]
        return (sums[0] + sums[1]) + (sums[2] + sums[3])

    for n in range(NEWTON):
        field = [(basis, (0,))]
        moves = start(1 + n, 2 + n, field)
        started.extend(moves)
        partial = place(jnp.zeros((1, 128), jnp.float32), 0, square_of_start())
        if not n:
            finish_x(deep, 0, opening, HALO)
            look_up(*RIM[0])
            saturate(*RIM[0], keep_none)
            linearize()
        else:
            finish(head_moves, 4, [(head, ())])
            for region in RIM:
                saturate(*region, keep_none)
            linearize()
        finish(moves, 2 + n, field)
        for j, at in ((0, 1), (1, 3), (2, 6)):
            partial = place(partial, at, matvec(j))
        sums = reduce_all(n, partial)
        gram = [[None] * 4 for _ in range(4)]
        at = 0
        for i in range(4):
            for j in range(i + 1):
                gram[i][j] = gram[j][i] = jnp.broadcast_to(sums[:, at : at + 1], (1, 128))
                at += 1
        weights = [w[:, 0:1] for w in krylov_weights(gram)]
        last = n + 1 == NEWTON
        rows, lanes = (slice(0, 16), slice(0, 512)) if last else (slice(0, ROWS), slice(0, LANES))

        def update(k, carry):
            value = head[k, rows, lanes]
            for i in range(KRYLOV):
                value = value - weights[i] * basis[i, k, rows, lanes]
            if last:
                out_ref[k] = value
            else:
                head[k] = value
            return carry

        lax.fori_loop(0, layers, update, 0)
        if not last:
            head_moves = start(3, 4, [(head, ())])
            started.extend(head_moves)
            saturate(*OWN, keep_residual)
            for region in RIM:
                saturate(*region, keep_none)
            balance(True)

    for moves in started:
        drain(moves)
    sent = send_c.at[pl.ds(0, devices - 1), pl.ds(0, 7)]
    pltpu.make_async_copy(sent, sent, sem_c.at[0]).wait()
    for n in range(NEWTON):
        sent = gather.at[n, pl.ds(0, devices - 1)]
        pltpu.make_async_copy(sent, sent, sem_g.at[0, n]).wait()


def shards(sizes, head_old, soil_type, soil_table, forcing, canopy, column_slot):
    inputs = (head_old, soil_type, soil_table, forcing, canopy, column_slot)
    layers = head_old.shape[0]
    devices = sizes[0] * sizes[1]
    f32 = jnp.float32
    wide = (layers, ROWS, LANES)
    tile = (layers, 16, 512)
    vmem, anywhere = pl.BlockSpec(memory_space=pltpu.VMEM), pl.BlockSpec(memory_space=pl.ANY)
    return pl.pallas_call(
        functools.partial(kernel, sizes),
        out_shape=(
            jax.ShapeDtypeStruct(head_old.shape, f32),
            jax.ShapeDtypeStruct((2, 16, 512), f32),
        ),
        in_specs=[anywhere] * 6,
        out_specs=(vmem, vmem),
        scratch_shapes=[
            pltpu.SMEM(soil_table.shape, f32),
            pltpu.VMEM(tile, jnp.int32),
            pltpu.VMEM(forcing.shape, f32),
            pltpu.VMEM(canopy.shape, f32),
            pltpu.VMEM(column_slot.shape, jnp.int32),
            pltpu.VMEM((devices, 8, 128), f32),
            pltpu.VMEM((devices * 8, 128), f32),
            pltpu.VMEM((13 * (devices // 4), 512), jnp.bfloat16),
            pltpu.VMEM((16, 256, 512), jnp.bfloat16),
            pltpu.VMEM((13, 16, 512), f32),
            pltpu.VMEM(wide, f32),
            pltpu.VMEM(wide, f32),
            pltpu.VMEM(wide, f32),
            pltpu.VMEM(wide, f32),
            pltpu.VMEM(wide, f32),
            pltpu.VMEM(wide, f32),
            pltpu.VMEM(wide, f32),
            pltpu.VMEM((7,) + wide, f32),
            pltpu.VMEM((KRYLOV,) + wide, f32),
            pltpu.VMEM(tile, f32),
            pltpu.VMEM(tile, f32),
            pltpu.VMEM(tile, f32),
            pltpu.VMEM((ROWS, LANES), f32),
            pltpu.VMEM((2, 5, 32, 512), f32),
            pltpu.VMEM((2, 5, 32, 512), f32),
            pltpu.VMEM((2, 2, 16, 512), f32),
            pltpu.VMEM((2, 2, 16, 512), f32),
            pltpu.VMEM((2, 5, 16, 128), f32),
            pltpu.VMEM((2, 5, 16, 128), f32),
            pltpu.VMEM((2, 2, 5, 8, 128), f32),
            pltpu.VMEM((NEWTON, 1, 128), f32),
            pltpu.VMEM((NEWTON, devices, 1, 128), f32),
            pltpu.SemaphoreType.DMA((6,)),
            pltpu.SemaphoreType.DMA((3,)),
            pltpu.SemaphoreType.DMA((2, 5, 8)),
            pltpu.SemaphoreType.DMA((2, NEWTON)),
        ],
        compiler_params=pltpu.CompilerParams(
            collective_id=0, has_side_effects=True, vmem_limit_bytes=48 * 1024 * 1024
        ),
        name="coupled_step",
    )(*(pltpu.with_memory_space_constraint(x, pltpu.HBM) for x in inputs))


def solution(mesh):
    sizes = (mesh.shape["gx"], mesh.shape["gy"])
    return jax.shard_map(
        functools.partial(shards, sizes),
        mesh=mesh,
        in_specs=(
            P(None, "gx", "gy"),
            P(None, "gx", "gy"),
            P(),
            P(None, "gx", "gy"),
            P(None, ("gx", "gy")),
            P("gx", "gy"),
        ),
        out_specs=(P(None, "gx", "gy"), P(None, "gx", "gy")),
        check_vma=False,
    )
```

```python
import functools

import jax
import jax.numpy as jnp
from jax import lax
from jax.experimental import pallas as pl
from jax.experimental.pallas import tpu as pltpu
from jax.sharding import PartitionSpec as P

NEWTON = 2
KRYLOV = 3
CAP = 64

STORAGE = 4.0
EPSILON = 1e-06

SHIFT = 3.0
SCALE = 3.0

MESH = pl.DeviceIdType.MESH
OWN = (slice(0, 16), slice(0, 512))
RIM = ((slice(16, 24), slice(0, 512)), (slice(0, 24), slice(512, 640)))
HALO = 3
ROWS = 24
LANES = 640


def logistic(u):
    return 1.0 / (1.0 + jnp.exp(-u))


def ahead(x, axis):
    return pltpu.roll(x, x.shape[axis] - 1, axis)


def behind(x, axis):
    return pltpu.roll(x, 1, axis)


def krylov_weights(gram):
    def inner(vector, image):
        terms = [a * b for a, b in zip(vector, image) if a is not None]
        return functools.reduce(lambda a, b: a + b, terms)

    def image_of(vector):
        return [inner(vector, [gram[i][k] for i in range(4)]) for k in range(4)]

    beta = jnp.sqrt(gram[0][0] + EPSILON)
    basis = [[1.0 / beta, None, None, None]]
    images = [image_of(basis[0])]
    hessen = [[None] * KRYLOV for _ in range(KRYLOV + 1)]
    for j in range(KRYLOV):
        v = basis[j]
        w = [None] * 4
        for i in range(j + 2):
            if i <= j:
                w[i] = SHIFT * v[i]
            if i >= 1:
                term = SCALE * v[i - 1]
                w[i] = term if w[i] is None else w[i] + term
        for i in range(j + 1):
            product = inner(w, images[i])
            hessen[i][j] = product
            w = [a if b is None else a - product * b for a, b in zip(w, basis[i])]
        square = jnp.maximum(inner(w, image_of(w)), 0.0)
        length = jnp.sqrt(square + EPSILON)
        hessen[j + 1][j] = length
        if j + 1 < KRYLOV:
            basis.append([None if a is None else a / length for a in w])
            images.append(image_of(basis[-1]))

    def column(a, b):
        pairs = [(hessen[i][a], hessen[i][b]) for i in range(KRYLOV + 1)]
        terms = [x * y for x, y in pairs if x is not None and y is not None]
        return functools.reduce(lambda x, y: x + y, terms)

    factor = [[None] * KRYLOV for _ in range(KRYLOV)]
    for i in range(KRYLOV):
        for j in range(i + 1):
            value = column(i, j)
            for k in range(j):
                value = value - factor[i][k] * factor[j][k]
            factor[i][j] = jnp.sqrt(value) if i == j else value / factor[j][j]
    forward = []
    for row in range(KRYLOV):
        value = hessen[0][row] * beta
        for other in range(row):
            value = value - factor[row][other] * forward[other]
        forward.append(value / factor[row][row])
    y = [None] * KRYLOV
    for row in reversed(range(KRYLOV)):
        value = forward[row]
        for other in range(row + 1, KRYLOV):
            value = value - factor[other][row] * y[other]
        y[row] = value / factor[row][row]
    weights = []
    for i in range(KRYLOV):
        terms = [y[j] * basis[j][i] for j in range(KRYLOV) if basis[j][i] is not None]
        weights.append(functools.reduce(lambda a, b: a + b, terms))
    return weights


def kernel(
    sizes,
    head_in,
    soil_in,
    table_in,
    forcing_in,
    canopy_in,
    slot_in,
    out_ref,
    flux_ref,
    table_ref,
    soil_ref,
    forcing_ref,
    canopy_ref,
    slot_ref,
    send_c,
    recv_c,
    split,
    hot,
    records,
    head,
    soil,
    conduct,
    slope,
    ksat,
    steep,
    cap,
    coef,
    basis,
    wet,
    theta_old,
    source,
    mask,
    send_x,
    recv_x,
    send_w,
    recv_w,
    send_y,
    recv_y,
    recv_k,
    part,
    gather,
    sem_in,
    sem_c,
    sem_e,
    sem_g,
):
    size_x, size_y = sizes
    devices = size_x * size_y
    layers = out_ref.shape[0]
    gx, gy = lax.axis_index("gx"), lax.axis_index("gy")
    me = gx * size_y + gy

    loads = [
        pltpu.make_async_copy(src, dst, sem_in.at[i])
        for i, (src, dst) in enumerate(
            (
                (canopy_in, canopy_ref),
                (head_in, head.at[:, 0:16, 0:512]),
                (soil_in, soil_ref),
                (slot_in, slot_ref),
                (forcing_in, forcing_ref),
                (table_in, table_ref),
            )
        )
    ]
    for load in loads:
        load.start()

    def wrap(value, size):
        return lax.rem(value + size, size)

    def hops(step):
        x, y = step
        return sum((0, 1, 2, 1)[i % 4] for i in (x, x // 4, y // 2))

    steps = [(x, y) for x in range(size_x) for y in range(size_y) if x or y]
    farthest = sorted(steps, key=hops, reverse=True)

    def others(visit):
        for x, y in farthest:
            visit(lax.rem(gx + x, size_x), lax.rem(gy + y, size_y))

    def ringwise(visit):
        for dy in range(1, size_y):
            visit(gx, lax.rem(gy + dy, size_y))

        def ring(i, carry):
            far = (i + 1) // 2
            x = wrap(gx + jnp.where(lax.rem(i, 2) == 1, far, -far), size_x)
            for dy in range(size_y):
                visit(x, lax.rem(gy + dy, size_y))
            return carry

        lax.fori_loop(1, size_x, ring, 0)

    barrier = pltpu.get_barrier_semaphore()
    others(lambda x, y: pl.semaphore_signal(barrier, inc=1, device_id=(x, y), device_id_type=MESH))

    row = lax.broadcasted_iota(jnp.int32, (ROWS, LANES), 0)
    col = lax.broadcasted_iota(jnp.int32, (ROWS, LANES), 1)
    one, zero = jnp.float32(1.0), jnp.float32(0.0)
    in_x, in_y = (gx < size_x - 1, gx > 0), (gy < size_y - 1, gy > 0)
    has_next_x, has_prev_x = (jnp.where(there, one, zero) for there in in_x)
    has_next_y, has_prev_y = (jnp.where(there, one, zero) for there in in_y)
    inside_x = jnp.where(
        row < 16,
        1.0,
        jnp.where(row < 16 + HALO, has_next_x, jnp.where(row >= ROWS - HALO, has_prev_x, 0.0)),
    )
    inside_y = jnp.where(
        col < 512,
        1.0,
        jnp.where(col < 512 + HALO, has_next_y, jnp.where(col >= LANES - HALO, has_prev_y, 0.0)),
    )
    mask[...] = inside_x * inside_y

    def own(ref, k):
        return ref[k, 0:16, 0:512]

    def clear(k, carry):
        for ref in (head, soil, basis.at[0]):
            ref[k, 16:24, 0:512] = jnp.zeros((8, 512), jnp.float32)
            ref[k, 0:24, 512:640] = jnp.zeros((24, 128), jnp.float32)
        return carry

    lax.fori_loop(0, layers, clear, 0)
    for side in range(2):
        for slot in range(5):
            send_x[side, slot, 16:32, :] = jnp.zeros((16, 512), jnp.float32)
        for slot in range(2):
            send_w[side, slot, 8:16, :] = jnp.zeros((8, 512), jnp.float32)

    low7 = lax.broadcasted_iota(jnp.int32, (7, 128), 1) < CAP

    def pack(q, carry):
        lanes = pl.ds(pl.multiple_of(q * 128, 128), 128)
        first, second = canopy_ref[0:7, lanes], canopy_ref[6:13, lanes]
        send_c[2 * q, 0:7] = jnp.where(low7, first, pltpu.roll(second, CAP, 1))
        send_c[2 * q + 1, 0:7] = jnp.where(low7, pltpu.roll(first, CAP, 1), second)
        return carry

    loads[0].wait()
    lax.fori_loop(0, devices // 2, pack, 0, unroll=4)
    quarter = size_x // 4

    def seat(x):
        return lax.rem(gx - x + quarter + size_x, size_x)

    def slab(x):
        return pl.ds(pl.multiple_of((seat(x) * size_y + gy) * 8, 8), 7)

    recv_c[slab(gx), :] = send_c[me, 0:7]

    next_x, prev_x = wrap(gx + 1, size_x), wrap(gx - 1, size_x)
    next_y, prev_y = wrap(gy + 1, size_y), wrap(gy - 1, size_y)
    lane16 = lax.broadcasted_iota(jnp.int32, (16, 128), 1)
    group16 = lane16 // 4
    lane24 = lax.broadcasted_iota(jnp.int32, (ROWS, 128), 1)
    early8 = lax.broadcasted_iota(jnp.int32, (8, 128), 0) < 4

    def send_all(number, plan):
        moves = []
        for i, src, dst, target, sends, receives in plan:
            move = pltpu.make_async_remote_copy(
                src_ref=src,
                dst_ref=dst,
                send_sem=sem_e.at[0, number, i],
                recv_sem=sem_e.at[1, number, i],
                device_id=target,
                device_id_type=MESH,
            )
            moves.append((move, sends, receives))
        for move, sends, _ in moves:
            pl.when(sends)(move.start)
        return moves

    def start_x(number, slot, fields, depth, skip=0):
        send, recv = (send_x, recv_x) if depth == HALO else (send_w, recv_w)
        count = depth - skip
        height = -(-layers * count // 8) * 8
        for f, (ref, index) in enumerate(fields):
            for k in range(layers):
                rows = slice(count * k, count * (k + 1))
                send[0, slot + f, rows, :] = ref[
                    index + (k, slice(16 - depth, 16 - skip), slice(0, 512))
                ]
                send[1, slot + f, rows, :] = ref[index + (k, slice(skip, depth), slice(0, 512))]
        block = (pl.ds(slot, len(fields)), pl.ds(0, height))
        return send_all(
            number,
            [
                (
                    side,
                    send.at[(side, *block)],
                    recv.at[(side, *block)],
                    (x, gy),
                    in_x[side],
                    in_x[1 - side],
                )
                for side, x in enumerate((next_x, prev_x))
            ],
        )

    def start_y(number, slot, fields):
        for f, (ref, index) in enumerate(fields):
            up = jnp.zeros((16, 128), jnp.float32)
            down = jnp.zeros((16, 128), jnp.float32)
            for k in range(layers):
                last = ref[index + (k, slice(0, 16), slice(384, 512))]
                first = ref[index + (k, slice(0, 16), slice(0, 128))]
                here = group16 == k
                up = jnp.where(here, pltpu.roll(last, 4 * k + 4, 1), up)
                down = jnp.where(here, pltpu.roll(first, 4 * k, 1) if k else first, down)
            send_y[0, slot + f] = up
            send_y[1, slot + f] = down
        slots = pl.ds(slot, len(fields))
        plan = []
        for side, y in enumerate((next_y, prev_y)):
            for turn, x in enumerate((next_x, prev_x)):
                plan.append(
                    (
                        2 + 2 * side + turn,
                        send_y.at[side, slots, pl.ds(8 * (1 - turn), 8)],
                        recv_k.at[side, turn, slots],
                        (x, y),
                        in_x[turn] & in_y[side],
                        in_x[1 - turn] & in_y[1 - side],
                    )
                )
        for side, y in enumerate((next_y, prev_y)):
            plan.append(
                (
                    6 + side,
                    send_y.at[side, slots],
                    recv_y.at[side, slots],
                    (gx, y),
                    in_y[side],
                    in_y[1 - side],
                )
            )
        return send_all(number, plan)

    def start(number, slot, fields, skip=0):
        moves = start_x(number, slot, fields, HALO, skip)
        return moves, start_y(number, slot, fields)

    def await_all(moves):
        for move, _, receives in moves:
            pl.when(receives)(move.wait_recv)

    def drain(moves):
        for move, sends, _ in moves:
            pl.when(sends)(move.wait_send)

    def finish_y(moves, slot, fields):
        await_all(moves)
        edge = mask[:, 512:640]
        for f, (ref, index) in enumerate(fields):
            sides = [
                jnp.concatenate(
                    [
                        recv_y[side, slot + f],
                        jnp.where(early8, recv_k[side, 1, slot + f], recv_k[side, 0, slot + f]),
                    ],
                    axis=0,
                )
                for side in range(2)
            ]
            for k in range(layers):
                left = pltpu.roll(sides[0], 128 - (4 * k + 4), 1)
                right = pltpu.roll(sides[1], 128 - 4 * k, 1) if k else sides[1]
                both = jnp.where(lane24 < 64, right, left)
                ref[index + (k, slice(0, ROWS), slice(512, 640))] = jnp.where(edge > 0.0, both, 0.0)

    def finish_x(moves, slot, fields, depth, skip=0):
        recv = recv_x if depth == HALO else recv_w
        await_all(moves)
        for f, (ref, index) in enumerate(fields):
            for k in range(layers):
                rows = slice((depth - skip) * k, (depth - skip) * (k + 1))
                after = jnp.where(in_x[0], recv[1, slot + f, rows, :], 0.0)
                before = jnp.where(in_x[1], recv[0, slot + f, rows, :], 0.0)
                ref[index + (k, slice(16 + skip, 16 + depth), slice(0, 512))] = after
                ref[index + (k, slice(ROWS - depth, ROWS - skip), slice(0, 512))] = before

    def finish(moves, slot, fields, skip=0):
        finish_y(moves[1], slot, fields)
        finish_x(moves[0], slot, fields, HALO, skip)

    loads[1].wait()
    loads[2].wait()

    def convert(k, carry):
        soil[k, 0:16, 0:512] = soil_ref[k].astype(jnp.float32)
        return carry

    lax.fori_loop(0, layers, convert, 0)

    pl.semaphore_wait(barrier, devices - 1)

    def scatter(x, y):
        pltpu.make_async_remote_copy(
            src_ref=send_c.at[x * size_y + y, pl.ds(0, 7)],
            dst_ref=recv_c.at[slab(x)],
            send_sem=sem_c.at[0],
            recv_sem=sem_c.at[1],
            device_id=(x, y),
            device_id_type=MESH,
        ).start()

    opening = [(head, ()), (soil, ())]
    near = start_x(0, 0, opening, 1), start_y(0, 0, opening)
    started = [*near]
    ringwise(scatter)

    def look_up(rows, lanes):
        def layer(k, carry):
            kind = soil[k, rows, lanes]
            values = [jnp.zeros(kind.shape, jnp.float32) for _ in range(3)]
            for c in range(table_ref.shape[1]):
                match = kind == float(c)
                values = [jnp.where(match, table_ref[p, c], v) for p, v in enumerate(values)]
            ksat[k, rows, lanes] = values[0] * mask[rows, lanes]
            steep[k, rows, lanes] = values[1]
            cap[k, rows, lanes] = values[2]
            return carry

        lax.fori_loop(0, layers, layer, 0, unroll=2)

    loads[5].wait()
    look_up(*OWN)

    def saturate(rows, lanes, keep):
        def layer(k, carry):
            a, ks, c = (ref[k, rows, lanes] for ref in (steep, ksat, cap))
            s = logistic(a * head[k, rows, lanes])
            rise = a * s * (1.0 - s)
            conduct[k, rows, lanes] = ks * (0.1 + 0.9 * s * s)
            slope[k, rows, lanes] = 0.9 * ks * s * rise
            coef[0, k, rows, lanes] = STORAGE * c * rise
            keep(k, s, c)
            return carry

        lax.fori_loop(0, layers, layer, 0, unroll=2)

    def keep_old(k, s, c):
        wet[k] = s
        theta_old[k] = c * s

    def keep_residual(k, s, c):
        basis[0, k, 0:16, 0:512] = STORAGE * (c * s - theta_old[k]) - source[k]

    def keep_none(k, s, c):
        pass

    saturate(*OWN, keep_old)

    loads[3].wait()
    within = lax.broadcasted_iota(jnp.int32, (256, 512), 0)

    def seats_of(x):
        slot = jnp.maximum(slot_ref[pl.ds(x, 1), :], 0)
        shift = (size_y * CAP).bit_length() - 1
        seat = ((slot >> shift) - gx + quarter) & (size_x - 1)
        return (seat << shift) + (slot & (size_y * CAP - 1))

    def spot(x, carry):
        slot = seats_of(x)
        hot[x] = jnp.where(within == (slot & 255), 1.0, 0.0).astype(jnp.bfloat16)
        return carry

    lax.fori_loop(0, 16, spot, 0)

    finish_y(near[1], 0, opening)
    finish_x(near[0], 0, opening, 1)
    for region in RIM:
        look_up(*region)

    def around(k):
        return jnp.minimum(k + 1, layers - 1), jnp.maximum(k - 1, 0)

    def balance(added):
        def layer(k, carry):
            h, kk = head[k], conduct[k]
            total = basis[0, k, 0:16, 0:512] if added else 0.0
            for axis in range(2):
                flow = 0.5 * (kk + ahead(kk, axis)) * (h - ahead(h, axis))
                total = total + (flow - behind(flow, axis))[0:16, 0:512]
            below, above = around(k)
            h, kk = own(head, k), own(conduct, k)
            flow = 0.5 * (kk + own(conduct, below)) * (h - own(head, below) + 1.0)
            total = total + jnp.where(k == layers - 1, kk, flow)
            flow = 0.5 * (own(conduct, above) + kk) * (own(head, above) - h + 1.0)
            basis[0, k, 0:16, 0:512] = total - jnp.where(k == 0, 0.0, flow)
            return carry

        lax.fori_loop(0, layers, layer, 0, unroll=2)

    def linearize():
        def layer(k, carry):
            scaled = mask[...] * (1.0 / SCALE)
            h, kk, dk = head[k], conduct[k], slope[k]
            diagonal = coef[0, k] - SHIFT
            for axis, at in ((0, 1), (1, 3)):
                drop = h - ahead(h, axis)
                mean = 0.5 * (kk + ahead(kk, axis))
                mine = dk * drop + mean
                other = ahead(dk, axis) * drop - mean
                diagonal = diagonal + mine - behind(other, axis)
                coef[at, k] = other * scaled
                coef[at + 1, k] = -behind(mine, axis) * scaled
            below, above = around(k)
            bottom, top = k == layers - 1, k == 0
            drop = h - head[below] + 1.0
            mean = 0.5 * (kk + conduct[below])
            diagonal = diagonal + jnp.where(bottom, 2.0 * dk, dk * drop + mean)
            coef[5, k] = jnp.where(bottom, 0.0, slope[below] * drop - mean) * scaled
            drop = head[above] - h + 1.0
            mean = 0.5 * (kk + conduct[above])
            diagonal = diagonal - jnp.where(top, 0.0, dk * drop - mean)
            coef[6, k] = -jnp.where(top, 0.0, slope[above] * drop + mean) * scaled
            coef[0, k] = diagonal * scaled
            return carry

        lax.fori_loop(0, layers, layer, 0, unroll=2)

    for region in RIM:
        saturate(*region, keep_none)
    balance(False)
    deep = start_x(4, 0, opening, HALO)
    started.append(deep)

    blocks = devices // 4
    low = lax.broadcasted_iota(jnp.int32, (blocks, 128), 1) < CAP
    which = lax.broadcasted_iota(jnp.int32, (blocks, 512), 0)

    def choose():
        arrived = send_c.at[pl.ds(0, devices - 1), pl.ds(0, 7)]
        pltpu.make_async_copy(arrived, arrived, sem_c.at[1]).wait()

        def put(r, left, right):
            value = jnp.concatenate([left, right], axis=1)
            high = value.astype(jnp.bfloat16)
            rows = slice(blocks * r, blocks * (r + 1))
            split[rows, 0:256] = high
            split[rows, 256:512] = (value - high.astype(jnp.float32)).astype(jnp.bfloat16)

        for r in range(7):
            plain = [recv_c[pl.ds(r + 8 * c, blocks, stride=32), :] for c in range(4)]
            moved = [pltpu.roll(x, CAP, 1) for x in plain]
            put(r, jnp.where(low, plain[0], moved[1]), jnp.where(low, plain[2], moved[3]))
            if r >= 1:
                put(r + 6, jnp.where(low, moved[0], plain[1]), jnp.where(low, moved[2], plain[3]))

        def select(x, carry):
            found = jnp.dot(
                split[...], jnp.concatenate([hot[x], hot[x]], axis=0), preferred_element_type=jnp.float32
            )
            match = which == seats_of(x) >> 8
            for r in range(13):
                piece = jnp.where(match, found[blocks * r : blocks * (r + 1)], 0.0)
                records[r, pl.ds(x, 1), :] = jnp.sum(piece, axis=0, keepdims=True)
            return carry

        lax.fori_loop(0, 16, select, 0, unroll=16)

    choose()
    loads[4].wait()
    sunlight, air, humidity, rainfall = (forcing_ref[i] for i in range(4))
    leaf, albedo, resist = (records[i] for i in range(3))
    total, roots = jnp.zeros_like(leaf), jnp.zeros_like(leaf)
    for k in range(layers):
        total = total + records[3 + k] * wet[k]
        roots = roots + records[3 + k]
    conductance = total / roots * leaf / (leaf + resist)
    exchange_coef = 0.5 + 0.3 * leaf
    radiation = (1.0 - albedo) * sunlight + 0.3
    surface = air
    for _ in range(2):
        vapour = 0.5 * jnp.exp(2.0 * (surface - air))
        square = surface * surface
        excess = (
            radiation
            - 0.3 * square * square
            - exchange_coef * (surface - air)
            - conductance * (vapour - humidity)
        )
        tangent = -1.2 * square * surface - exchange_coef - 2.0 * conductance * vapour
        surface = surface - excess / tangent
    evaporation = conductance * (0.5 * jnp.exp(2.0 * (surface - air)) - humidity)
    ks_top = own(ksat, 0)
    infiltration = rainfall * ks_top / (rainfall + ks_top)
    land = slot_ref[...] >= 0
    evaporation = jnp.where(land, evaporation, 0.0)
    infiltration = jnp.where(land, infiltration, 0.0)
    flux_ref[0] = evaporation
    flux_ref[1] = infiltration
    share = evaporation / total
    for k in range(layers):
        gain = -jnp.where(land, share * records[3 + k] * wet[k], 0.0)
        if k == 0:
            gain = gain + infiltration
        source[k] = gain
        basis[0, k, 0:16, 0:512] -= gain

    def fold(product):
        tall = product[0:8] + product[8:16]
        return (tall[:, 0:128] + tall[:, 128:256]) + (tall[:, 256:384] + tall[:, 384:512])

    lane1 = lax.broadcasted_iota(jnp.int32, (1, 128), 1)

    def place(partial, at, sums):
        for i, value in enumerate(sums):
            line = jnp.sum(value, axis=0, keepdims=True)
            partial = jnp.where(lane1 == at + i, jnp.sum(line, axis=1, keepdims=True), partial)
        return partial

    def matvec(j):
        rows, lanes = (slice(0, ROWS), slice(0, LANES)) if j + 1 < KRYLOV else (slice(0, 16), slice(0, 512))

        def layer(k, carry):
            v = basis[j, k]
            below, above = around(k)

            def term(i, value):
                return coef[i, k, rows, lanes] * value[rows, lanes]

            w = term(0, v)
            w = w + term(1, ahead(v, 0)) + term(2, behind(v, 0))
            w = w + term(3, ahead(v, 1)) + term(4, behind(v, 1))
            w = w + coef[5, k, rows, lanes] * basis[j, below, rows, lanes]
            w = w + coef[6, k, rows, lanes] * basis[j, above, rows, lanes]
            if j + 1 < KRYLOV:
                basis[j + 1, k] = w
            mine = w[0:16, 0:512]
            sums = [fold(mine * basis[i, k, 0:16, 0:512]) for i in range(j + 1)]
            sums.append(fold(mine * mine))
            return tuple(a + b for a, b in zip(carry, sums))

        zeros = tuple(jnp.zeros((8, 128), jnp.float32) for _ in range(j + 2))
        return lax.fori_loop(0, layers, layer, zeros, unroll=5)

    def square_of_start():
        def layer(k, carry):
            value = basis[0, k, 0:16, 0:512]
            return carry + fold(value * value)

        return [lax.fori_loop(0, layers, layer, jnp.zeros((8, 128), jnp.float32))]

    def reduce_all(n, partial):
        mine = part.at[n]
        mine[...] = partial
        gather[n, me] = partial

        def send(x, y):
            pltpu.make_async_remote_copy(
                src_ref=mine,
                dst_ref=gather.at[n, me],
                send_sem=sem_g.at[0, n],
                recv_sem=sem_g.at[1, n],
                device_id=(x, y),
                device_id_type=MESH,
            ).start()

        others(send)
        rest = gather.at[n, pl.ds(0, devices - 1)]
        pltpu.make_async_copy(rest, rest, sem_g.at[1, n]).wait()
        sums = [gather[n, i] for i in range(4)]
        for i in range(4, devices, 4):
            sums = [a + gather[n, i + k] for k, a in enumerate(sums)]
        return (sums[0] + sums[1]) + (sums[2] + sums[3])

    for n in range(NEWTON):
        field = [(basis, (0,))]
        moves = start(1 + n, 2 + n, field)
        started.extend(moves)
        partial = place(jnp.zeros((1, 128), jnp.float32), 0, square_of_start())
        if not n:
            finish_x(deep, 0, opening, HALO)
            look_up(*RIM[0])
            saturate(*RIM[0], keep_none)
            linearize()
        else:
            finish(head_moves, 4, [(head, ())], skip=1)
            for region in RIM:
                saturate(*region, keep_none)
            linearize()
        finish(moves, 2 + n, field)
        for j, at in ((0, 1), (1, 3), (2, 6)):
            partial = place(partial, at, matvec(j))
        sums = reduce_all(n, partial)
        gram = [[None] * 4 for _ in range(4)]
        at = 0
        for i in range(4):
            for j in range(i + 1):
                gram[i][j] = gram[j][i] = jnp.broadcast_to(sums[:, at : at + 1], (1, 128))
                at += 1
        weights = [w[:, 0:1] for w in krylov_weights(gram)]
        last = n + 1 == NEWTON
        rows, lanes = (slice(0, 16), slice(0, 512)) if last else (slice(0, ROWS), slice(0, LANES))

        def update(k, carry):
            value = head[k, rows, lanes]
            for i in range(KRYLOV):
                value = value - weights[i] * basis[i, k, rows, lanes]
            if last:
                out_ref[k] = value
            else:
                head[k] = value
            return carry

        lax.fori_loop(0, layers, update, 0)
        if not last:
            head_moves = start(3, 4, [(head, ())], skip=1)
            started.extend(head_moves)
            saturate(*OWN, keep_residual)
            for region in RIM:
                saturate(*region, keep_none)
            balance(True)

    for moves in started:
        drain(moves)
    sent = send_c.at[pl.ds(0, devices - 1), pl.ds(0, 7)]
    pltpu.make_async_copy(sent, sent, sem_c.at[0]).wait()
    for n in range(NEWTON):
        sent = gather.at[n, pl.ds(0, devices - 1)]
        pltpu.make_async_copy(sent, sent, sem_g.at[0, n]).wait()


def shards(sizes, head_old, soil_type, soil_table, forcing, canopy, column_slot):
    inputs = (head_old, soil_type, soil_table, forcing, canopy, column_slot)
    layers = head_old.shape[0]
    devices = sizes[0] * sizes[1]
    f32 = jnp.float32
    wide = (layers, ROWS, LANES)
    tile = (layers, 16, 512)
    vmem, anywhere = pl.BlockSpec(memory_space=pltpu.VMEM), pl.BlockSpec(memory_space=pl.ANY)
    return pl.pallas_call(
        functools.partial(kernel, sizes),
        out_shape=(
            jax.ShapeDtypeStruct(head_old.shape, f32),
            jax.ShapeDtypeStruct((2, 16, 512), f32),
        ),
        in_specs=[anywhere] * 6,
        out_specs=(vmem, vmem),
        scratch_shapes=[
            pltpu.SMEM(soil_table.shape, f32),
            pltpu.VMEM(tile, jnp.int32),
            pltpu.VMEM(forcing.shape, f32),
            pltpu.VMEM(canopy.shape, f32),
            pltpu.VMEM(column_slot.shape, jnp.int32),
            pltpu.VMEM((devices, 8, 128), f32),
            pltpu.VMEM((devices * 8, 128), f32),
            pltpu.VMEM((13 * (devices // 4), 512), jnp.bfloat16),
            pltpu.VMEM((16, 256, 512), jnp.bfloat16),
            pltpu.VMEM((13, 16, 512), f32),
            pltpu.VMEM(wide, f32),
            pltpu.VMEM(wide, f32),
            pltpu.VMEM(wide, f32),
            pltpu.VMEM(wide, f32),
            pltpu.VMEM(wide, f32),
            pltpu.VMEM(wide, f32),
            pltpu.VMEM(wide, f32),
            pltpu.VMEM((7,) + wide, f32),
            pltpu.VMEM((KRYLOV,) + wide, f32),
            pltpu.VMEM(tile, f32),
            pltpu.VMEM(tile, f32),
            pltpu.VMEM(tile, f32),
            pltpu.VMEM((ROWS, LANES), f32),
            pltpu.VMEM((2, 5, 32, 512), f32),
            pltpu.VMEM((2, 5, 32, 512), f32),
            pltpu.VMEM((2, 2, 16, 512), f32),
            pltpu.VMEM((2, 2, 16, 512), f32),
            pltpu.VMEM((2, 5, 16, 128), f32),
            pltpu.VMEM((2, 5, 16, 128), f32),
            pltpu.VMEM((2, 2, 5, 8, 128), f32),
            pltpu.VMEM((NEWTON, 1, 128), f32),
            pltpu.VMEM((NEWTON, devices, 1, 128), f32),
            pltpu.SemaphoreType.DMA((6,)),
            pltpu.SemaphoreType.DMA((3,)),
            pltpu.SemaphoreType.DMA((2, 5, 8)),
            pltpu.SemaphoreType.DMA((2, NEWTON)),
        ],
        compiler_params=pltpu.CompilerParams(
            collective_id=0, has_side_effects=True, vmem_limit_bytes=48 * 1024 * 1024
        ),
        name="coupled_step",
    )(*(pltpu.with_memory_space_constraint(x, pltpu.HBM) for x in inputs))


def solution(mesh):
    sizes = (mesh.shape["gx"], mesh.shape["gy"])
    return jax.shard_map(
        functools.partial(shards, sizes),
        mesh=mesh,
        in_specs=(
            P(None, "gx", "gy"),
            P(None, "gx", "gy"),
            P(),
            P(None, "gx", "gy"),
            P(None, ("gx", "gy")),
            P("gx", "gy"),
        ),
        out_specs=(P(None, "gx", "gy"), P(None, "gx", "gy")),
        check_vma=False,
    )
```

```python
import functools

import jax
import jax.numpy as jnp
from jax import lax
from jax.experimental import pallas as pl
from jax.experimental.pallas import tpu as pltpu
from jax.sharding import PartitionSpec as P

NEWTON = 2
KRYLOV = 3
CAP = 64

STORAGE = 4.0
EPSILON = 1e-06

SHIFT = 3.0
SCALE = 3.0

MESH = pl.DeviceIdType.MESH
OWN = (slice(0, 16), slice(0, 512))
RIM = ((slice(16, 24), slice(0, 512)), (slice(0, 24), slice(512, 640)))
HALO = 3
ROWS = 24
LANES = 640


def logistic(u):
    return 1.0 / (1.0 + jnp.exp(-u))


def ahead(x, axis):
    return pltpu.roll(x, x.shape[axis] - 1, axis)


def behind(x, axis):
    return pltpu.roll(x, 1, axis)


def krylov_weights(gram):
    def inner(vector, image):
        terms = [a * b for a, b in zip(vector, image) if a is not None]
        return functools.reduce(lambda a, b: a + b, terms)

    def image_of(vector):
        return [inner(vector, [gram[i][k] for i in range(4)]) for k in range(4)]

    beta = jnp.sqrt(gram[0][0] + EPSILON)
    basis = [[1.0 / beta, None, None, None]]
    images = [image_of(basis[0])]
    hessen = [[None] * KRYLOV for _ in range(KRYLOV + 1)]
    for j in range(KRYLOV):
        v = basis[j]
        w = [None] * 4
        for i in range(j + 2):
            if i <= j:
                w[i] = SHIFT * v[i]
            if i >= 1:
                term = SCALE * v[i - 1]
                w[i] = term if w[i] is None else w[i] + term
        for i in range(j + 1):
            product = inner(w, images[i])
            hessen[i][j] = product
            w = [a if b is None else a - product * b for a, b in zip(w, basis[i])]
        square = jnp.maximum(inner(w, image_of(w)), 0.0)
        length = jnp.sqrt(square + EPSILON)
        hessen[j + 1][j] = length
        if j + 1 < KRYLOV:
            basis.append([None if a is None else a / length for a in w])
            images.append(image_of(basis[-1]))

    def column(a, b):
        pairs = [(hessen[i][a], hessen[i][b]) for i in range(KRYLOV + 1)]
        terms = [x * y for x, y in pairs if x is not None and y is not None]
        return functools.reduce(lambda x, y: x + y, terms)

    factor = [[None] * KRYLOV for _ in range(KRYLOV)]
    for i in range(KRYLOV):
        for j in range(i + 1):
            value = column(i, j)
            for k in range(j):
                value = value - factor[i][k] * factor[j][k]
            factor[i][j] = jnp.sqrt(value) if i == j else value / factor[j][j]
    forward = []
    for row in range(KRYLOV):
        value = hessen[0][row] * beta
        for other in range(row):
            value = value - factor[row][other] * forward[other]
        forward.append(value / factor[row][row])
    y = [None] * KRYLOV
    for row in reversed(range(KRYLOV)):
        value = forward[row]
        for other in range(row + 1, KRYLOV):
            value = value - factor[other][row] * y[other]
        y[row] = value / factor[row][row]
    weights = []
    for i in range(KRYLOV):
        terms = [y[j] * basis[j][i] for j in range(KRYLOV) if basis[j][i] is not None]
        weights.append(functools.reduce(lambda a, b: a + b, terms))
    return weights


def kernel(
    sizes,
    head_in,
    soil_in,
    table_in,
    forcing_in,
    canopy_in,
    slot_in,
    out_ref,
    flux_ref,
    table_ref,
    soil_ref,
    forcing_ref,
    canopy_ref,
    slot_ref,
    send_c,
    recv_c,
    split,
    hot,
    records,
    head,
    soil,
    conduct,
    slope,
    ksat,
    steep,
    cap,
    coef,
    basis,
    wet,
    theta_old,
    source,
    mask,
    send_x,
    recv_x,
    send_w,
    recv_w,
    send_y,
    recv_y,
    recv_k,
    part,
    gather,
    sem_in,
    sem_c,
    sem_e,
    sem_g,
):
    size_x, size_y = sizes
    devices = size_x * size_y
    layers = out_ref.shape[0]
    gx, gy = lax.axis_index("gx"), lax.axis_index("gy")
    me = gx * size_y + gy

    loads = [
        pltpu.make_async_copy(src, dst, sem_in.at[i])
        for i, (src, dst) in enumerate(
            (
                (canopy_in, canopy_ref.at[0]),
                (head_in, head.at[:, 0:16, 0:512]),
                (soil_in, soil_ref),
                (slot_in, slot_ref.at[0:16]),
                (forcing_in, forcing_ref),
                (table_in, table_ref),
            )
        )
    ]
    for load in loads:
        load.start()

    def wrap(value, size):
        return lax.rem(value + size, size)

    def hops(step):
        x, y = step
        return sum((0, 1, 2, 1)[i % 4] for i in (x, x // 4, y // 2))

    steps = [(x, y) for x in range(size_x) for y in range(size_y) if x or y]
    farthest = sorted(steps, key=hops, reverse=True)

    def others(visit):
        for x, y in farthest:
            visit(lax.rem(gx + x, size_x), lax.rem(gy + y, size_y))

    def ringwise(visit):
        for dy in range(1, size_y):
            visit(gx, lax.rem(gy + dy, size_y))

        def ring(i, carry):
            far = (i + 1) // 2
            x = wrap(gx + jnp.where(lax.rem(i, 2) == 1, far, -far), size_x)
            for dy in range(size_y):
                visit(x, lax.rem(gy + dy, size_y))
            return carry

        lax.fori_loop(1, size_x, ring, 0)

    barrier = pltpu.get_barrier_semaphore()
    others(lambda x, y: pl.semaphore_signal(barrier, inc=1, device_id=(x, y), device_id_type=MESH))

    row = lax.broadcasted_iota(jnp.int32, (ROWS, LANES), 0)
    col = lax.broadcasted_iota(jnp.int32, (ROWS, LANES), 1)
    one, zero = jnp.float32(1.0), jnp.float32(0.0)
    in_x, in_y = (gx < size_x - 1, gx > 0), (gy < size_y - 1, gy > 0)
    has_next_x, has_prev_x = (jnp.where(there, one, zero) for there in in_x)
    has_next_y, has_prev_y = (jnp.where(there, one, zero) for there in in_y)
    inside_x = jnp.where(
        row < 16,
        1.0,
        jnp.where(row < 16 + HALO, has_next_x, jnp.where(row >= ROWS - HALO, has_prev_x, 0.0)),
    )
    inside_y = jnp.where(
        col < 512,
        1.0,
        jnp.where(col < 512 + HALO, has_next_y, jnp.where(col >= LANES - HALO, has_prev_y, 0.0)),
    )
    mask[...] = inside_x * inside_y

    def own(ref, k):
        return ref[k, 0:16, 0:512]

    def clear(k, carry):
        for ref in (head, soil, basis.at[0]):
            ref[k, 16:24, 0:512] = jnp.zeros((8, 512), jnp.float32)
            ref[k, 0:24, 512:640] = jnp.zeros((24, 128), jnp.float32)
        return carry

    lax.fori_loop(0, layers, clear, 0)
    for side in range(2):
        for slot in range(5):
            send_x[side, slot, 16:32, :] = jnp.zeros((16, 512), jnp.float32)
        for slot in range(2):
            send_w[side, slot, 8:16, :] = jnp.zeros((8, 512), jnp.float32)

    low7 = lax.broadcasted_iota(jnp.int32, (7, 128), 1) < CAP

    def pack(q, carry):
        lanes = pl.ds(pl.multiple_of(q * 128, 128), 128)
        first, second = canopy_ref[0, 0:7, lanes], canopy_ref[0, 6:13, lanes]
        send_c[2 * q, 0:7] = jnp.where(low7, first, pltpu.roll(second, CAP, 1))
        send_c[2 * q + 1, 0:7] = jnp.where(low7, pltpu.roll(first, CAP, 1), second)
        return carry

    loads[0].wait()
    lax.fori_loop(0, devices // 2, pack, 0, unroll=4)
    quarter = size_x // 4

    def seat(x):
        return lax.rem(gx - x + quarter + size_x, size_x)

    def slab(x):
        return pl.ds(pl.multiple_of((seat(x) * size_y + gy) * 8, 8), 7)

    recv_c[slab(gx), :] = send_c[me, 0:7]

    next_x, prev_x = wrap(gx + 1, size_x), wrap(gx - 1, size_x)
    next_y, prev_y = wrap(gy + 1, size_y), wrap(gy - 1, size_y)
    lane16 = lax.broadcasted_iota(jnp.int32, (16, 128), 1)
    group16 = lane16 // 4
    lane24 = lax.broadcasted_iota(jnp.int32, (ROWS, 128), 1)
    early8 = lax.broadcasted_iota(jnp.int32, (8, 128), 0) < 4

    def send_all(number, plan):
        moves = []
        for i, src, dst, target, sends, receives in plan:
            move = pltpu.make_async_remote_copy(
                src_ref=src,
                dst_ref=dst,
                send_sem=sem_e.at[0, number, i],
                recv_sem=sem_e.at[1, number, i],
                device_id=target,
                device_id_type=MESH,
            )
            moves.append((move, sends, receives))
        for move, sends, _ in moves:
            pl.when(sends)(move.start)
        return moves

    def start_x(number, slot, fields, depth, skip=0):
        send, recv = (send_x, recv_x) if depth == HALO else (send_w, recv_w)
        count = depth - skip
        height = -(-layers * count // 8) * 8
        for f, (ref, index) in enumerate(fields):
            for k in range(layers):
                rows = slice(count * k, count * (k + 1))
                send[0, slot + f, rows, :] = ref[
                    index + (k, slice(16 - depth, 16 - skip), slice(0, 512))
                ]
                send[1, slot + f, rows, :] = ref[index + (k, slice(skip, depth), slice(0, 512))]
        block = (pl.ds(slot, len(fields)), pl.ds(0, height))
        return send_all(
            number,
            [
                (
                    side,
                    send.at[(side, *block)],
                    recv.at[(side, *block)],
                    (x, gy),
                    in_x[side],
                    in_x[1 - side],
                )
                for side, x in enumerate((next_x, prev_x))
            ],
        )

    def start_y(number, slot, fields):
        for f, (ref, index) in enumerate(fields):
            up = jnp.zeros((16, 128), jnp.float32)
            down = jnp.zeros((16, 128), jnp.float32)
            for k in range(layers):
                last = ref[index + (k, slice(0, 16), slice(384, 512))]
                first = ref[index + (k, slice(0, 16), slice(0, 128))]
                here = group16 == k
                up = jnp.where(here, pltpu.roll(last, 4 * k + 4, 1), up)
                down = jnp.where(here, pltpu.roll(first, 4 * k, 1) if k else first, down)
            send_y[0, slot + f] = up
            send_y[1, slot + f] = down
        slots = pl.ds(slot, len(fields))
        plan = []
        for side, y in enumerate((next_y, prev_y)):
            for turn, x in enumerate((next_x, prev_x)):
                plan.append(
                    (
                        2 + 2 * side + turn,
                        send_y.at[side, slots, pl.ds(8 * (1 - turn), 8)],
                        recv_k.at[side, turn, slots],
                        (x, y),
                        in_x[turn] & in_y[side],
                        in_x[1 - turn] & in_y[1 - side],
                    )
                )
        for side, y in enumerate((next_y, prev_y)):
            plan.append(
                (
                    6 + side,
                    send_y.at[side, slots],
                    recv_y.at[side, slots],
                    (gx, y),
                    in_y[side],
                    in_y[1 - side],
                )
            )
        return send_all(number, plan)

    def start(number, slot, fields, skip=0):
        moves = start_x(number, slot, fields, HALO, skip)
        return moves, start_y(number, slot, fields)

    def await_all(moves):
        for move, _, receives in moves:
            pl.when(receives)(move.wait_recv)

    def drain(moves):
        for move, sends, _ in moves:
            pl.when(sends)(move.wait_send)

    def finish_y(moves, slot, fields):
        await_all(moves)
        edge = mask[:, 512:640]
        for f, (ref, index) in enumerate(fields):
            sides = [
                jnp.concatenate(
                    [
                        recv_y[side, slot + f],
                        jnp.where(early8, recv_k[side, 1, slot + f], recv_k[side, 0, slot + f]),
                    ],
                    axis=0,
                )
                for side in range(2)
            ]
            for k in range(layers):
                left = pltpu.roll(sides[0], 128 - (4 * k + 4), 1)
                right = pltpu.roll(sides[1], 128 - 4 * k, 1) if k else sides[1]
                both = jnp.where(lane24 < 64, right, left)
                ref[index + (k, slice(0, ROWS), slice(512, 640))] = jnp.where(edge > 0.0, both, 0.0)

    def finish_x(moves, slot, fields, depth, skip=0):
        recv = recv_x if depth == HALO else recv_w
        await_all(moves)
        for f, (ref, index) in enumerate(fields):
            for k in range(layers):
                rows = slice((depth - skip) * k, (depth - skip) * (k + 1))
                after = jnp.where(in_x[0], recv[1, slot + f, rows, :], 0.0)
                before = jnp.where(in_x[1], recv[0, slot + f, rows, :], 0.0)
                ref[index + (k, slice(16 + skip, 16 + depth), slice(0, 512))] = after
                ref[index + (k, slice(ROWS - depth, ROWS - skip), slice(0, 512))] = before

    def finish(moves, slot, fields, skip=0):
        finish_y(moves[1], slot, fields)
        finish_x(moves[0], slot, fields, HALO, skip)

    loads[1].wait()
    loads[2].wait()

    def convert(k, carry):
        soil[k, 0:16, 0:512] = soil_ref[k].astype(jnp.float32)
        return carry

    lax.fori_loop(0, layers, convert, 0)

    pl.semaphore_wait(barrier, devices - 1)

    def scatter(x, y):
        pltpu.make_async_remote_copy(
            src_ref=send_c.at[x * size_y + y, pl.ds(0, 7)],
            dst_ref=recv_c.at[slab(x)],
            send_sem=sem_c.at[0],
            recv_sem=sem_c.at[1],
            device_id=(x, y),
            device_id_type=MESH,
        ).start()

    opening = [(head, ()), (soil, ())]
    near = start_x(0, 0, opening, 1), start_y(0, 0, opening)
    started = [*near]
    ringwise(scatter)

    def look_up(rows, lanes):
        def layer(k, carry):
            kind = soil[k, rows, lanes]
            values = [jnp.zeros(kind.shape, jnp.float32) for _ in range(3)]
            for c in range(table_ref.shape[1]):
                match = kind == float(c)
                values = [jnp.where(match, table_ref[p, c], v) for p, v in enumerate(values)]
            ksat[k, rows, lanes] = values[0] * mask[rows, lanes]
            steep[k, rows, lanes] = values[1]
            cap[k, rows, lanes] = values[2]
            return carry

        lax.fori_loop(0, layers, layer, 0, unroll=2)

    loads[5].wait()
    look_up(*OWN)

    def saturate(rows, lanes, keep):
        def layer(k, carry):
            a, ks, c = (ref[k, rows, lanes] for ref in (steep, ksat, cap))
            s = logistic(a * head[k, rows, lanes])
            rise = a * s * (1.0 - s)
            conduct[k, rows, lanes] = ks * (0.1 + 0.9 * s * s)
            slope[k, rows, lanes] = 0.9 * ks * s * rise
            coef[0, k, rows, lanes] = STORAGE * c * rise
            keep(k, s, c)
            return carry

        lax.fori_loop(0, layers, layer, 0, unroll=2)

    def keep_old(k, s, c):
        wet[k] = s
        theta_old[k] = c * s

    def keep_residual(k, s, c):
        basis[0, k, 0:16, 0:512] = STORAGE * (c * s - theta_old[k]) - source[k]

    def keep_none(k, s, c):
        pass

    saturate(*OWN, keep_old)

    loads[3].wait()
    within = lax.broadcasted_iota(jnp.int32, (256, 512), 0)

    def seats_of(x):
        slot = jnp.maximum(slot_ref[pl.ds(x, 1), :], 0)
        shift = (size_y * CAP).bit_length() - 1
        seat = ((slot >> shift) - gx + quarter) & (size_x - 1)
        return (seat << shift) + (slot & (size_y * CAP - 1))

    def spot(x, carry):
        slot = seats_of(x)
        hot[x] = jnp.where(within == (slot & 255), 1.0, 0.0).astype(jnp.bfloat16)
        return carry

    lax.fori_loop(0, 16, spot, 0)

    finish_y(near[1], 0, opening)
    finish_x(near[0], 0, opening, 1)
    for region in RIM:
        look_up(*region)

    def around(k):
        return jnp.minimum(k + 1, layers - 1), jnp.maximum(k - 1, 0)

    def balance(added):
        def layer(k, carry):
            h, kk = head[k], conduct[k]
            total = basis[0, k, 0:16, 0:512] if added else 0.0
            for axis in range(2):
                flow = 0.5 * (kk + ahead(kk, axis)) * (h - ahead(h, axis))
                total = total + (flow - behind(flow, axis))[0:16, 0:512]
            below, above = around(k)
            h, kk = own(head, k), own(conduct, k)
            flow = 0.5 * (kk + own(conduct, below)) * (h - own(head, below) + 1.0)
            total = total + jnp.where(k == layers - 1, kk, flow)
            flow = 0.5 * (own(conduct, above) + kk) * (own(head, above) - h + 1.0)
            basis[0, k, 0:16, 0:512] = total - jnp.where(k == 0, 0.0, flow)
            return carry

        lax.fori_loop(0, layers, layer, 0, unroll=2)

    def linearize():
        def layer(k, carry):
            scaled = mask[...] * (1.0 / SCALE)
            h, kk, dk = head[k], conduct[k], slope[k]
            diagonal = coef[0, k] - SHIFT
            for axis, at in ((0, 1), (1, 3)):
                drop = h - ahead(h, axis)
                mean = 0.5 * (kk + ahead(kk, axis))
                mine = dk * drop + mean
                other = ahead(dk, axis) * drop - mean
                diagonal = diagonal + mine - behind(other, axis)
                coef[at, k] = other * scaled
                coef[at + 1, k] = -behind(mine, axis) * scaled
            below, above = around(k)
            bottom, top = k == layers - 1, k == 0
            drop = h - head[below] + 1.0
            mean = 0.5 * (kk + conduct[below])
            diagonal = diagonal + jnp.where(bottom, 2.0 * dk, dk * drop + mean)
            coef[5, k] = jnp.where(bottom, 0.0, slope[below] * drop - mean) * scaled
            drop = head[above] - h + 1.0
            mean = 0.5 * (kk + conduct[above])
            diagonal = diagonal - jnp.where(top, 0.0, dk * drop - mean)
            coef[6, k] = -jnp.where(top, 0.0, slope[above] * drop + mean) * scaled
            coef[0, k] = diagonal * scaled
            return carry

        lax.fori_loop(0, layers, layer, 0, unroll=2)

    for region in RIM:
        saturate(*region, keep_none)
    balance(False)
    deep = start_x(4, 0, opening, HALO)
    started.append(deep)

    blocks = devices // 4
    low = lax.broadcasted_iota(jnp.int32, (blocks, 128), 1) < CAP
    which = lax.broadcasted_iota(jnp.int32, (blocks, 512), 0)

    def choose():
        arrived = send_c.at[pl.ds(0, devices - 1), pl.ds(0, 7)]
        pltpu.make_async_copy(arrived, arrived, sem_c.at[1]).wait()

        def put(r, left, right):
            value = jnp.concatenate([left, right], axis=1)
            high = value.astype(jnp.bfloat16)
            rows = slice(blocks * r, blocks * (r + 1))
            split[rows, 0:256] = high
            split[rows, 256:512] = (value - high.astype(jnp.float32)).astype(jnp.bfloat16)

        for r in range(7):
            plain = [recv_c[pl.ds(r + 8 * c, blocks, stride=32), :] for c in range(4)]
            moved = [pltpu.roll(x, CAP, 1) for x in plain]
            put(r, jnp.where(low, plain[0], moved[1]), jnp.where(low, plain[2], moved[3]))
            if r >= 1:
                put(r + 6, jnp.where(low, moved[0], plain[1]), jnp.where(low, moved[2], plain[3]))

        def select(x, carry):
            found = jnp.dot(
                split[...], jnp.concatenate([hot[x], hot[x]], axis=0), preferred_element_type=jnp.float32
            )
            match = which == seats_of(x) >> 8
            for r in range(13):
                piece = jnp.where(match, found[blocks * r : blocks * (r + 1)], 0.0)
                records[r, pl.ds(x, 1), :] = jnp.sum(piece, axis=0, keepdims=True)
            return carry

        lax.fori_loop(0, 16, select, 0, unroll=16)

    choose()
    loads[4].wait()
    sunlight, air, humidity, rainfall = (forcing_ref[i] for i in range(4))
    leaf, albedo, resist = (records[i] for i in range(3))
    total, roots = jnp.zeros_like(leaf), jnp.zeros_like(leaf)
    for k in range(layers):
        total = total + records[3 + k] * wet[k]
        roots = roots + records[3 + k]
    conductance = total / roots * leaf / (leaf + resist)
    exchange_coef = 0.5 + 0.3 * leaf
    radiation = (1.0 - albedo) * sunlight + 0.3
    surface = air
    for _ in range(2):
        vapour = 0.5 * jnp.exp(2.0 * (surface - air))
        square = surface * surface
        excess = (
            radiation
            - 0.3 * square * square
            - exchange_coef * (surface - air)
            - conductance * (vapour - humidity)
        )
        tangent = -1.2 * square * surface - exchange_coef - 2.0 * conductance * vapour
        surface = surface - excess / tangent
    evaporation = conductance * (0.5 * jnp.exp(2.0 * (surface - air)) - humidity)
    ks_top = own(ksat, 0)
    infiltration = rainfall * ks_top / (rainfall + ks_top)
    land = slot_ref[0:16, :] >= 0
    evaporation = jnp.where(land, evaporation, 0.0)
    infiltration = jnp.where(land, infiltration, 0.0)
    flux_ref[0] = evaporation
    flux_ref[1] = infiltration
    share = evaporation / total
    for k in range(layers):
        gain = -jnp.where(land, share * records[3 + k] * wet[k], 0.0)
        if k == 0:
            gain = gain + infiltration
        source[k] = gain
        basis[0, k, 0:16, 0:512] -= gain

    def fold(product):
        tall = product[0:8] + product[8:16]
        return (tall[:, 0:128] + tall[:, 128:256]) + (tall[:, 256:384] + tall[:, 384:512])

    lane1 = lax.broadcasted_iota(jnp.int32, (1, 128), 1)

    def place(partial, at, sums):
        for i, value in enumerate(sums):
            line = jnp.sum(value, axis=0, keepdims=True)
            partial = jnp.where(lane1 == at + i, jnp.sum(line, axis=1, keepdims=True), partial)
        return partial

    def matvec(j):
        rows, lanes = (slice(0, ROWS), slice(0, LANES)) if j + 1 < KRYLOV else (slice(0, 16), slice(0, 512))

        def layer(k, carry):
            v = basis[j, k]
            below, above = around(k)

            def term(i, value):
                return coef[i, k, rows, lanes] * value[rows, lanes]

            w = term(0, v)
            w = w + term(1, ahead(v, 0)) + term(2, behind(v, 0))
            w = w + term(3, ahead(v, 1)) + term(4, behind(v, 1))
            w = w + coef[5, k, rows, lanes] * basis[j, below, rows, lanes]
            w = w + coef[6, k, rows, lanes] * basis[j, above, rows, lanes]
            if j + 1 < KRYLOV:
                basis[j + 1, k] = w
            mine = w[0:16, 0:512]
            sums = [fold(mine * basis[i, k, 0:16, 0:512]) for i in range(j + 1)]
            sums.append(fold(mine * mine))
            return tuple(a + b for a, b in zip(carry, sums))

        zeros = tuple(jnp.zeros((8, 128), jnp.float32) for _ in range(j + 2))
        return lax.fori_loop(0, layers, layer, zeros, unroll=5)

    def square_of_start():
        def layer(k, carry):
            value = basis[0, k, 0:16, 0:512]
            return carry + fold(value * value)

        return [lax.fori_loop(0, layers, layer, jnp.zeros((8, 128), jnp.float32))]

    def reduce_all(n, partial):
        mine = part.at[n]
        mine[...] = partial
        gather[n, me] = partial

        def send(x, y):
            pltpu.make_async_remote_copy(
                src_ref=mine,
                dst_ref=gather.at[n, me],
                send_sem=sem_g.at[0, n],
                recv_sem=sem_g.at[1, n],
                device_id=(x, y),
                device_id_type=MESH,
            ).start()

        others(send)
        rest = gather.at[n, pl.ds(0, devices - 1)]
        pltpu.make_async_copy(rest, rest, sem_g.at[1, n]).wait()
        sums = [gather[n, i] for i in range(4)]
        for i in range(4, devices, 4):
            sums = [a + gather[n, i + k] for k, a in enumerate(sums)]
        return (sums[0] + sums[1]) + (sums[2] + sums[3])

    for n in range(NEWTON):
        field = [(basis, (0,))]
        moves = start(1 + n, 2 + n, field)
        started.extend(moves)
        partial = place(jnp.zeros((1, 128), jnp.float32), 0, square_of_start())
        if not n:
            finish_x(deep, 0, opening, HALO)
            look_up(*RIM[0])
            saturate(*RIM[0], keep_none)
            linearize()
        else:
            finish(head_moves, 4, [(head, ())], skip=1)
            for region in RIM:
                saturate(*region, keep_none)
            linearize()
        finish(moves, 2 + n, field)
        for j, at in ((0, 1), (1, 3), (2, 6)):
            partial = place(partial, at, matvec(j))
        sums = reduce_all(n, partial)
        gram = [[None] * 4 for _ in range(4)]
        at = 0
        for i in range(4):
            for j in range(i + 1):
                gram[i][j] = gram[j][i] = jnp.broadcast_to(sums[:, at : at + 1], (1, 128))
                at += 1
        weights = [w[:, 0:1] for w in krylov_weights(gram)]
        last = n + 1 == NEWTON
        rows, lanes = (slice(0, 16), slice(0, 512)) if last else (slice(0, ROWS), slice(0, LANES))

        def update(k, carry):
            value = head[k, rows, lanes]
            for i in range(KRYLOV):
                value = value - weights[i] * basis[i, k, rows, lanes]
            if last:
                out_ref[k] = value
            else:
                head[k] = value
            return carry

        lax.fori_loop(0, layers, update, 0)
        if not last:
            head_moves = start(3, 4, [(head, ())], skip=1)
            started.extend(head_moves)
            saturate(*OWN, keep_residual)
            for region in RIM:
                saturate(*region, keep_none)
            balance(True)

    for moves in started:
        drain(moves)
    sent = send_c.at[pl.ds(0, devices - 1), pl.ds(0, 7)]
    pltpu.make_async_copy(sent, sent, sem_c.at[0]).wait()
    for n in range(NEWTON):
        sent = gather.at[n, pl.ds(0, devices - 1)]
        pltpu.make_async_copy(sent, sent, sem_g.at[0, n]).wait()


def shards(sizes, head_old, soil_type, soil_table, forcing, canopy, column_slot):
    inputs = (head_old, soil_type, soil_table, forcing, canopy, column_slot)
    layers = head_old.shape[0]
    devices = sizes[0] * sizes[1]
    f32 = jnp.float32
    wide = (layers, ROWS, LANES)
    tile = (layers, 16, 512)
    vmem, anywhere = pl.BlockSpec(memory_space=pltpu.VMEM), pl.BlockSpec(memory_space=pl.ANY)
    return pl.pallas_call(
        functools.partial(kernel, sizes),
        out_shape=(
            jax.ShapeDtypeStruct(head_old.shape, f32),
            jax.ShapeDtypeStruct((2, 16, 512), f32),
        ),
        in_specs=[anywhere] * 6,
        out_specs=(vmem, vmem),
        scratch_shapes=[
            pltpu.SMEM(soil_table.shape, f32),
            pltpu.VMEM(tile, jnp.int32),
            pltpu.VMEM(forcing.shape, f32),
            pltpu.VMEM((2,) + canopy.shape, f32),
            pltpu.VMEM((24, 512), jnp.int32),
            pltpu.VMEM((devices, 8, 128), f32),
            pltpu.VMEM((devices * 8, 128), f32),
            pltpu.VMEM((13 * (devices // 4), 512), jnp.bfloat16),
            pltpu.VMEM((16, 256, 512), jnp.bfloat16),
            pltpu.VMEM((14, 16, 512), f32),
            pltpu.VMEM(wide, f32),
            pltpu.VMEM(wide, f32),
            pltpu.VMEM(wide, f32),
            pltpu.VMEM(wide, f32),
            pltpu.VMEM(wide, f32),
            pltpu.VMEM(wide, f32),
            pltpu.VMEM(wide, f32),
            pltpu.VMEM((7,) + wide, f32),
            pltpu.VMEM((KRYLOV,) + wide, f32),
            pltpu.VMEM(tile, f32),
            pltpu.VMEM(tile, f32),
            pltpu.VMEM(tile, f32),
            pltpu.VMEM((ROWS, LANES), f32),
            pltpu.VMEM((2, 6, 32, 512), f32),
            pltpu.VMEM((2, 6, 32, 512), f32),
            pltpu.VMEM((2, 3, 16, 512), f32),
            pltpu.VMEM((2, 3, 16, 512), f32),
            pltpu.VMEM((2, 5, 16, 128), f32),
            pltpu.VMEM((2, 5, 16, 128), f32),
            pltpu.VMEM((2, 2, 5, 8, 128), f32),
            pltpu.VMEM((NEWTON + 8, 1, 128), f32),
            pltpu.VMEM((NEWTON + 1, devices, 1, 128), f32),
            pltpu.SemaphoreType.DMA((6,)),
            pltpu.SemaphoreType.DMA((3,)),
            pltpu.SemaphoreType.DMA((2, 5, 8)),
            pltpu.SemaphoreType.DMA((2, NEWTON)),
        ],
        compiler_params=pltpu.CompilerParams(
            collective_id=0, has_side_effects=True, vmem_limit_bytes=48 * 1024 * 1024
        ),
        name="coupled_step",
    )(*(pltpu.with_memory_space_constraint(x, pltpu.HBM) for x in inputs))


def solution(mesh):
    sizes = (mesh.shape["gx"], mesh.shape["gy"])
    return jax.shard_map(
        functools.partial(shards, sizes),
        mesh=mesh,
        in_specs=(
            P(None, "gx", "gy"),
            P(None, "gx", "gy"),
            P(),
            P(None, "gx", "gy"),
            P(None, ("gx", "gy")),
            P("gx", "gy"),
        ),
        out_specs=(P(None, "gx", "gy"), P(None, "gx", "gy")),
        check_vma=False,
    )
```

```python
import functools

import jax
import jax.numpy as jnp
from jax import lax
from jax.experimental import pallas as pl
from jax.experimental.pallas import tpu as pltpu
from jax.sharding import PartitionSpec as P

NEWTON = 2
KRYLOV = 3
CAP = 64

STORAGE = 4.0
EPSILON = 1e-06

SHIFT = 3.0
SCALE = 3.0

MESH = pl.DeviceIdType.MESH
OWN = (slice(0, 16), slice(0, 512))
RIM = ((slice(16, 24), slice(0, 512)), (slice(0, 24), slice(512, 640)))
HALO = 3
ROWS = 24
LANES = 640


def logistic(u):
    return 1.0 / (1.0 + jnp.exp(-u))


def ahead(x, axis):
    return pltpu.roll(x, x.shape[axis] - 1, axis)


def behind(x, axis):
    return pltpu.roll(x, 1, axis)


def krylov_weights(gram):
    def inner(vector, image):
        terms = [a * b for a, b in zip(vector, image) if a is not None]
        return functools.reduce(lambda a, b: a + b, terms)

    def image_of(vector):
        return [inner(vector, [gram[i][k] for i in range(4)]) for k in range(4)]

    beta = jnp.sqrt(gram[0][0] + EPSILON)
    basis = [[1.0 / beta, None, None, None]]
    images = [image_of(basis[0])]
    hessen = [[None] * KRYLOV for _ in range(KRYLOV + 1)]
    for j in range(KRYLOV):
        v = basis[j]
        w = [None] * 4
        for i in range(j + 2):
            if i <= j:
                w[i] = SHIFT * v[i]
            if i >= 1:
                term = SCALE * v[i - 1]
                w[i] = term if w[i] is None else w[i] + term
        for i in range(j + 1):
            product = inner(w, images[i])
            hessen[i][j] = product
            w = [a if b is None else a - product * b for a, b in zip(w, basis[i])]
        square = jnp.maximum(inner(w, image_of(w)), 0.0)
        length = jnp.sqrt(square + EPSILON)
        hessen[j + 1][j] = length
        if j + 1 < KRYLOV:
            basis.append([None if a is None else a / length for a in w])
            images.append(image_of(basis[-1]))

    def column(a, b):
        pairs = [(hessen[i][a], hessen[i][b]) for i in range(KRYLOV + 1)]
        terms = [x * y for x, y in pairs if x is not None and y is not None]
        return functools.reduce(lambda x, y: x + y, terms)

    factor = [[None] * KRYLOV for _ in range(KRYLOV)]
    for i in range(KRYLOV):
        for j in range(i + 1):
            value = column(i, j)
            for k in range(j):
                value = value - factor[i][k] * factor[j][k]
            factor[i][j] = jnp.sqrt(value) if i == j else value / factor[j][j]
    forward = []
    for row in range(KRYLOV):
        value = hessen[0][row] * beta
        for other in range(row):
            value = value - factor[row][other] * forward[other]
        forward.append(value / factor[row][row])
    y = [None] * KRYLOV
    for row in reversed(range(KRYLOV)):
        value = forward[row]
        for other in range(row + 1, KRYLOV):
            value = value - factor[other][row] * y[other]
        y[row] = value / factor[row][row]
    weights = []
    for i in range(KRYLOV):
        terms = [y[j] * basis[j][i] for j in range(KRYLOV) if basis[j][i] is not None]
        weights.append(functools.reduce(lambda a, b: a + b, terms))
    return weights


def kernel(
    sizes,
    head_in,
    soil_in,
    table_in,
    forcing_in,
    canopy_in,
    slot_in,
    out_ref,
    flux_ref,
    table_ref,
    soil_ref,
    forcing_ref,
    canopy_ref,
    slot_ref,
    send_c,
    recv_c,
    split,
    hot,
    records,
    head,
    soil,
    conduct,
    slope,
    ksat,
    steep,
    cap,
    coef,
    basis,
    wet,
    theta_old,
    source,
    mask,
    send_x,
    recv_x,
    send_w,
    recv_w,
    send_y,
    recv_y,
    recv_k,
    part,
    gather,
    sem_in,
    sem_c,
    sem_e,
    sem_g,
):
    size_x, size_y = sizes
    devices = size_x * size_y
    layers = out_ref.shape[0]
    gx, gy = lax.axis_index("gx"), lax.axis_index("gy")
    me = gx * size_y + gy

    loads = [
        pltpu.make_async_copy(src, dst, sem_in.at[i])
        for i, (src, dst) in enumerate(
            (
                (canopy_in, canopy_ref.at[0]),
                (head_in, head.at[:, 0:16, 0:512]),
                (soil_in, soil_ref),
                (slot_in, slot_ref.at[0:16]),
                (forcing_in, forcing_ref),
                (table_in, table_ref),
            )
        )
    ]
    for load in loads:
        load.start()

    def wrap(value, size):
        return lax.rem(value + size, size)

    def hops(step):
        x, y = step
        return sum((0, 1, 2, 1)[i % 4] for i in (x, x // 4, y // 2))

    steps = [(x, y) for x in range(size_x) for y in range(size_y) if x or y]
    farthest = sorted(steps, key=hops, reverse=True)

    def others(visit):
        for x, y in farthest:
            visit(lax.rem(gx + x, size_x), lax.rem(gy + y, size_y))

    def ringwise(visit):
        for dy in range(1, size_y):
            visit(gx, lax.rem(gy + dy, size_y))

        def ring(i, carry):
            far = (i + 1) // 2
            x = wrap(gx + jnp.where(lax.rem(i, 2) == 1, far, -far), size_x)
            for dy in range(size_y):
                visit(x, lax.rem(gy + dy, size_y))
            return carry

        lax.fori_loop(1, size_x, ring, 0)

    barrier = pltpu.get_barrier_semaphore()
    others(lambda x, y: pl.semaphore_signal(barrier, inc=1, device_id=(x, y), device_id_type=MESH))

    row = lax.broadcasted_iota(jnp.int32, (ROWS, LANES), 0)
    col = lax.broadcasted_iota(jnp.int32, (ROWS, LANES), 1)
    one, zero = jnp.float32(1.0), jnp.float32(0.0)
    in_x, in_y = (gx < size_x - 1, gx > 0), (gy < size_y - 1, gy > 0)
    has_next_x, has_prev_x = (jnp.where(there, one, zero) for there in in_x)
    has_next_y, has_prev_y = (jnp.where(there, one, zero) for there in in_y)
    inside_x = jnp.where(
        row < 16,
        1.0,
        jnp.where(row < 16 + HALO, has_next_x, jnp.where(row >= ROWS - HALO, has_prev_x, 0.0)),
    )
    inside_y = jnp.where(
        col < 512,
        1.0,
        jnp.where(col < 512 + HALO, has_next_y, jnp.where(col >= LANES - HALO, has_prev_y, 0.0)),
    )
    mask[...] = inside_x * inside_y

    def own(ref, k):
        return ref[k, 0:16, 0:512]

    def clear(k, carry):
        for ref in (head, soil, basis.at[0]):
            ref[k, 16:24, 0:512] = jnp.zeros((8, 512), jnp.float32)
            ref[k, 0:24, 512:640] = jnp.zeros((24, 128), jnp.float32)
        return carry

    lax.fori_loop(0, layers, clear, 0)
    for side in range(2):
        for slot in range(5):
            send_x[side, slot, 16:32, :] = jnp.zeros((16, 512), jnp.float32)
        for slot in range(2):
            send_w[side, slot, 8:16, :] = jnp.zeros((8, 512), jnp.float32)

    low7 = lax.broadcasted_iota(jnp.int32, (7, 128), 1) < CAP

    def pack(q, carry):
        lanes = pl.ds(pl.multiple_of(q * 128, 128), 128)
        first, second = canopy_ref[0, 0:7, lanes], canopy_ref[0, 6:13, lanes]
        send_c[2 * q, 0:7] = jnp.where(low7, first, pltpu.roll(second, CAP, 1))
        send_c[2 * q + 1, 0:7] = jnp.where(low7, pltpu.roll(first, CAP, 1), second)
        return carry

    loads[0].wait()
    lax.fori_loop(0, devices // 2, pack, 0, unroll=4)
    quarter = size_x // 4

    def seat(x):
        return lax.rem(gx - x + quarter + size_x, size_x)

    def slab(x):
        return pl.ds(pl.multiple_of((seat(x) * size_y + gy) * 8, 8), 7)

    recv_c[slab(gx), :] = send_c[me, 0:7]

    next_x, prev_x = wrap(gx + 1, size_x), wrap(gx - 1, size_x)
    next_y, prev_y = wrap(gy + 1, size_y), wrap(gy - 1, size_y)
    lane16 = lax.broadcasted_iota(jnp.int32, (16, 128), 1)
    group16 = lane16 // 4
    lane24 = lax.broadcasted_iota(jnp.int32, (ROWS, 128), 1)
    early8 = lax.broadcasted_iota(jnp.int32, (8, 128), 0) < 4

    def send_all(number, plan):
        moves = []
        for i, src, dst, target, sends, receives in plan:
            move = pltpu.make_async_remote_copy(
                src_ref=src,
                dst_ref=dst,
                send_sem=sem_e.at[0, number, i],
                recv_sem=sem_e.at[1, number, i],
                device_id=target,
                device_id_type=MESH,
            )
            moves.append((move, sends, receives))
        for move, sends, _ in moves:
            pl.when(sends)(move.start)
        return moves

    def start_x(number, slot, fields, depth, skip=0):
        send, recv = (send_x, recv_x) if depth == HALO else (send_w, recv_w)
        count = depth - skip
        height = -(-layers * count // 8) * 8
        for f, (ref, index) in enumerate(fields):
            for k in range(layers):
                rows = slice(count * k, count * (k + 1))
                send[0, slot + f, rows, :] = ref[
                    index + (k, slice(16 - depth, 16 - skip), slice(0, 512))
                ]
                send[1, slot + f, rows, :] = ref[index + (k, slice(skip, depth), slice(0, 512))]
        block = (pl.ds(slot, len(fields)), pl.ds(0, height))
        return send_all(
            number,
            [
                (
                    side,
                    send.at[(side, *block)],
                    recv.at[(side, *block)],
                    (x, gy),
                    in_x[side],
                    in_x[1 - side],
                )
                for side, x in enumerate((next_x, prev_x))
            ],
        )

    def start_y(number, slot, fields):
        for f, (ref, index) in enumerate(fields):
            up = jnp.zeros((16, 128), jnp.float32)
            down = jnp.zeros((16, 128), jnp.float32)
            for k in range(layers):
                last = ref[index + (k, slice(0, 16), slice(384, 512))]
                first = ref[index + (k, slice(0, 16), slice(0, 128))]
                here = group16 == k
                up = jnp.where(here, pltpu.roll(last, 4 * k + 4, 1), up)
                down = jnp.where(here, pltpu.roll(first, 4 * k, 1) if k else first, down)
            send_y[0, slot + f] = up
            send_y[1, slot + f] = down
        slots = pl.ds(slot, len(fields))
        plan = []
        for side, y in enumerate((next_y, prev_y)):
            for turn, x in enumerate((next_x, prev_x)):
                plan.append(
                    (
                        2 + 2 * side + turn,
                        send_y.at[side, slots, pl.ds(8 * (1 - turn), 8)],
                        recv_k.at[side, turn, slots],
                        (x, y),
                        in_x[turn] & in_y[side],
                        in_x[1 - turn] & in_y[1 - side],
                    )
                )
        for side, y in enumerate((next_y, prev_y)):
            plan.append(
                (
                    6 + side,
                    send_y.at[side, slots],
                    recv_y.at[side, slots],
                    (gx, y),
                    in_y[side],
                    in_y[1 - side],
                )
            )
        return send_all(number, plan)

    def start(number, slot, fields, skip=0):
        moves = start_x(number, slot, fields, HALO, skip)
        return moves, start_y(number, slot, fields)

    def await_all(moves):
        for move, _, receives in moves:
            pl.when(receives)(move.wait_recv)

    def drain(moves):
        for move, sends, _ in moves:
            pl.when(sends)(move.wait_send)

    def finish_y(moves, slot, fields):
        await_all(moves)
        edge = mask[:, 512:640]
        for f, (ref, index) in enumerate(fields):
            sides = [
                jnp.concatenate(
                    [
                        recv_y[side, slot + f],
                        jnp.where(early8, recv_k[side, 1, slot + f], recv_k[side, 0, slot + f]),
                    ],
                    axis=0,
                )
                for side in range(2)
            ]
            for k in range(layers):
                left = pltpu.roll(sides[0], 128 - (4 * k + 4), 1)
                right = pltpu.roll(sides[1], 128 - 4 * k, 1) if k else sides[1]
                both = jnp.where(lane24 < 64, right, left)
                ref[index + (k, slice(0, ROWS), slice(512, 640))] = jnp.where(edge > 0.0, both, 0.0)

    def finish_x(moves, slot, fields, depth, skip=0):
        recv = recv_x if depth == HALO else recv_w
        await_all(moves)
        for f, (ref, index) in enumerate(fields):
            for k in range(layers):
                rows = slice((depth - skip) * k, (depth - skip) * (k + 1))
                after = jnp.where(in_x[0], recv[1, slot + f, rows, :], 0.0)
                before = jnp.where(in_x[1], recv[0, slot + f, rows, :], 0.0)
                ref[index + (k, slice(16 + skip, 16 + depth), slice(0, 512))] = after
                ref[index + (k, slice(ROWS - depth, ROWS - skip), slice(0, 512))] = before

    def finish(moves, slot, fields, skip=0):
        finish_y(moves[1], slot, fields)
        finish_x(moves[0], slot, fields, HALO, skip)

    loads[1].wait()
    loads[2].wait()

    def convert(k, carry):
        soil[k, 0:16, 0:512] = soil_ref[k].astype(jnp.float32)
        return carry

    lax.fori_loop(0, layers, convert, 0)

    pl.semaphore_wait(barrier, devices - 1)

    def scatter(x, y):
        pltpu.make_async_remote_copy(
            src_ref=send_c.at[x * size_y + y, pl.ds(0, 7)],
            dst_ref=recv_c.at[slab(x)],
            send_sem=sem_c.at[0],
            recv_sem=sem_c.at[1],
            device_id=(x, y),
            device_id_type=MESH,
        ).start()

    opening = [(head, ()), (soil, ())]
    near = start_x(0, 0, opening, 1), start_y(0, 0, opening)
    started = [*near]
    ringwise(scatter)

    def look_up(rows, lanes):
        def layer(k, carry):
            kind = soil[k, rows, lanes]
            values = [jnp.zeros(kind.shape, jnp.float32) for _ in range(3)]
            for c in range(table_ref.shape[1]):
                match = kind == float(c)
                values = [jnp.where(match, table_ref[p, c], v) for p, v in enumerate(values)]
            ksat[k, rows, lanes] = values[0] * mask[rows, lanes]
            steep[k, rows, lanes] = values[1]
            cap[k, rows, lanes] = values[2]
            return carry

        lax.fori_loop(0, layers, layer, 0, unroll=2)

    loads[5].wait()
    look_up(*OWN)

    def saturate(rows, lanes, keep):
        def layer(k, carry):
            a, ks, c = (ref[k, rows, lanes] for ref in (steep, ksat, cap))
            s = logistic(a * head[k, rows, lanes])
            rise = a * s * (1.0 - s)
            conduct[k, rows, lanes] = ks * (0.1 + 0.9 * s * s)
            slope[k, rows, lanes] = 0.9 * ks * s * rise
            coef[0, k, rows, lanes] = STORAGE * c * rise
            keep(k, s, c)
            return carry

        lax.fori_loop(0, layers, layer, 0, unroll=2)

    def keep_old(k, s, c):
        wet[k] = s
        theta_old[k] = c * s

    def keep_residual(k, s, c):
        basis[0, k, 0:16, 0:512] = STORAGE * (c * s - theta_old[k]) - source[k]

    def keep_none(k, s, c):
        pass

    saturate(*OWN, keep_old)

    loads[3].wait()
    within = lax.broadcasted_iota(jnp.int32, (256, 512), 0)

    def seats_of(x):
        slot = jnp.maximum(slot_ref[pl.ds(x, 1), :], 0)
        shift = (size_y * CAP).bit_length() - 1
        seat = ((slot >> shift) - gx + quarter) & (size_x - 1)
        return (seat << shift) + (slot & (size_y * CAP - 1))

    def spot(x, carry):
        slot = seats_of(x)
        hot[x] = jnp.where(within == (slot & 255), 1.0, 0.0).astype(jnp.bfloat16)
        return carry

    lax.fori_loop(0, 16, spot, 0)

    finish_y(near[1], 0, opening)
    finish_x(near[0], 0, opening, 1)
    for region in RIM:
        look_up(*region)

    def around(k):
        return jnp.minimum(k + 1, layers - 1), jnp.maximum(k - 1, 0)

    def balance(added):
        def layer(k, carry):
            h, kk = head[k], conduct[k]
            total = basis[0, k, 0:16, 0:512] if added else 0.0
            for axis in range(2):
                flow = 0.5 * (kk + ahead(kk, axis)) * (h - ahead(h, axis))
                total = total + (flow - behind(flow, axis))[0:16, 0:512]
            below, above = around(k)
            h, kk = own(head, k), own(conduct, k)
            flow = 0.5 * (kk + own(conduct, below)) * (h - own(head, below) + 1.0)
            total = total + jnp.where(k == layers - 1, kk, flow)
            flow = 0.5 * (own(conduct, above) + kk) * (own(head, above) - h + 1.0)
            basis[0, k, 0:16, 0:512] = total - jnp.where(k == 0, 0.0, flow)
            return carry

        lax.fori_loop(0, layers, layer, 0, unroll=5)

    def linearize():
        def layer(k, carry):
            scaled = mask[...] * (1.0 / SCALE)
            h, kk, dk = head[k], conduct[k], slope[k]
            diagonal = coef[0, k] - SHIFT
            for axis, at in ((0, 1), (1, 3)):
                drop = h - ahead(h, axis)
                mean = 0.5 * (kk + ahead(kk, axis))
                mine = dk * drop + mean
                other = ahead(dk, axis) * drop - mean
                diagonal = diagonal + mine - behind(other, axis)
                coef[at, k] = other * scaled
                coef[at + 1, k] = -behind(mine, axis) * scaled
            below, above = around(k)
            bottom, top = k == layers - 1, k == 0
            drop = h - head[below] + 1.0
            mean = 0.5 * (kk + conduct[below])
            diagonal = diagonal + jnp.where(bottom, 2.0 * dk, dk * drop + mean)
            coef[5, k] = jnp.where(bottom, 0.0, slope[below] * drop - mean) * scaled
            drop = head[above] - h + 1.0
            mean = 0.5 * (kk + conduct[above])
            diagonal = diagonal - jnp.where(top, 0.0, dk * drop - mean)
            coef[6, k] = -jnp.where(top, 0.0, slope[above] * drop + mean) * scaled
            coef[0, k] = diagonal * scaled
            return carry

        lax.fori_loop(0, layers, layer, 0, unroll=5)

    for region in RIM:
        saturate(*region, keep_none)
    balance(False)
    deep = start_x(4, 0, opening, HALO)
    started.append(deep)

    blocks = devices // 4
    low = lax.broadcasted_iota(jnp.int32, (blocks, 128), 1) < CAP
    which = lax.broadcasted_iota(jnp.int32, (blocks, 512), 0)

    def choose():
        arrived = send_c.at[pl.ds(0, devices - 1), pl.ds(0, 7)]
        pltpu.make_async_copy(arrived, arrived, sem_c.at[1]).wait()

        def put(r, left, right):
            value = jnp.concatenate([left, right], axis=1)
            high = value.astype(jnp.bfloat16)
            rows = slice(blocks * r, blocks * (r + 1))
            split[rows, 0:256] = high
            split[rows, 256:512] = (value - high.astype(jnp.float32)).astype(jnp.bfloat16)

        for r in range(7):
            plain = [recv_c[pl.ds(r + 8 * c, blocks, stride=32), :] for c in range(4)]
            moved = [pltpu.roll(x, CAP, 1) for x in plain]
            put(r, jnp.where(low, plain[0], moved[1]), jnp.where(low, plain[2], moved[3]))
            if r >= 1:
                put(r + 6, jnp.where(low, moved[0], plain[1]), jnp.where(low, moved[2], plain[3]))

        def select(x, carry):
            found = jnp.dot(
                split[...], jnp.concatenate([hot[x], hot[x]], axis=0), preferred_element_type=jnp.float32
            )
            match = which == seats_of(x) >> 8
            for r in range(13):
                piece = jnp.where(match, found[blocks * r : blocks * (r + 1)], 0.0)
                records[r, pl.ds(x, 1), :] = jnp.sum(piece, axis=0, keepdims=True)
            return carry

        lax.fori_loop(0, 16, select, 0, unroll=16)

    choose()
    loads[4].wait()
    sunlight, air, humidity, rainfall = (forcing_ref[i] for i in range(4))
    leaf, albedo, resist = (records[i] for i in range(3))
    total, roots = jnp.zeros_like(leaf), jnp.zeros_like(leaf)
    for k in range(layers):
        total = total + records[3 + k] * wet[k]
        roots = roots + records[3 + k]
    conductance = total / roots * leaf / (leaf + resist)
    exchange_coef = 0.5 + 0.3 * leaf
    radiation = (1.0 - albedo) * sunlight + 0.3
    surface = air
    for _ in range(2):
        vapour = 0.5 * jnp.exp(2.0 * (surface - air))
        square = surface * surface
        excess = (
            radiation
            - 0.3 * square * square
            - exchange_coef * (surface - air)
            - conductance * (vapour - humidity)
        )
        tangent = -1.2 * square * surface - exchange_coef - 2.0 * conductance * vapour
        surface = surface - excess / tangent
    evaporation = conductance * (0.5 * jnp.exp(2.0 * (surface - air)) - humidity)
    ks_top = own(ksat, 0)
    infiltration = rainfall * ks_top / (rainfall + ks_top)
    land = slot_ref[0:16, :] >= 0
    evaporation = jnp.where(land, evaporation, 0.0)
    infiltration = jnp.where(land, infiltration, 0.0)
    flux_ref[0] = evaporation
    flux_ref[1] = infiltration
    share = evaporation / total
    for k in range(layers):
        gain = -jnp.where(land, share * records[3 + k] * wet[k], 0.0)
        if k == 0:
            gain = gain + infiltration
        source[k] = gain
        basis[0, k, 0:16, 0:512] -= gain

    def fold(product):
        tall = product[0:8] + product[8:16]
        return (tall[:, 0:128] + tall[:, 128:256]) + (tall[:, 256:384] + tall[:, 384:512])

    lane1 = lax.broadcasted_iota(jnp.int32, (1, 128), 1)

    def place(partial, at, sums):
        for i, value in enumerate(sums):
            line = jnp.sum(value, axis=0, keepdims=True)
            partial = jnp.where(lane1 == at + i, jnp.sum(line, axis=1, keepdims=True), partial)
        return partial

    def matvec(j):
        rows, lanes = (slice(0, ROWS), slice(0, LANES)) if j + 1 < KRYLOV else (slice(0, 16), slice(0, 512))

        def layer(k, carry):
            v = basis[j, k]
            below, above = around(k)

            def term(i, value):
                return coef[i, k, rows, lanes] * value[rows, lanes]

            w = term(0, v)
            w = w + term(1, ahead(v, 0)) + term(2, behind(v, 0))
            w = w + term(3, ahead(v, 1)) + term(4, behind(v, 1))
            w = w + coef[5, k, rows, lanes] * basis[j, below, rows, lanes]
            w = w + coef[6, k, rows, lanes] * basis[j, above, rows, lanes]
            if j + 1 < KRYLOV:
                basis[j + 1, k] = w
            mine = w[0:16, 0:512]
            sums = [fold(mine * basis[i, k, 0:16, 0:512]) for i in range(j + 1)]
            sums.append(fold(mine * mine))
            return tuple(a + b for a, b in zip(carry, sums))

        zeros = tuple(jnp.zeros((8, 128), jnp.float32) for _ in range(j + 2))
        return lax.fori_loop(0, layers, layer, zeros, unroll=5)

    def square_of_start():
        def layer(k, carry):
            value = basis[0, k, 0:16, 0:512]
            return carry + fold(value * value)

        return [lax.fori_loop(0, layers, layer, jnp.zeros((8, 128), jnp.float32))]

    def reduce_all(n, partial):
        mine = part.at[n]
        mine[...] = partial
        gather[n, me] = partial

        def send(x, y):
            pltpu.make_async_remote_copy(
                src_ref=mine,
                dst_ref=gather.at[n, me],
                send_sem=sem_g.at[0, n],
                recv_sem=sem_g.at[1, n],
                device_id=(x, y),
                device_id_type=MESH,
            ).start()

        others(send)
        rest = gather.at[n, pl.ds(0, devices - 1)]
        pltpu.make_async_copy(rest, rest, sem_g.at[1, n]).wait()
        sums = [gather[n, i] for i in range(4)]
        for i in range(4, devices, 4):
            sums = [a + gather[n, i + k] for k, a in enumerate(sums)]
        return (sums[0] + sums[1]) + (sums[2] + sums[3])

    for n in range(NEWTON):
        field = [(basis, (0,))]
        moves = start(1 + n, 2 + n, field)
        started.extend(moves)
        partial = place(jnp.zeros((1, 128), jnp.float32), 0, square_of_start())
        if not n:
            finish_x(deep, 0, opening, HALO)
            look_up(*RIM[0])
            saturate(*RIM[0], keep_none)
            linearize()
        else:
            finish(head_moves, 4, [(head, ())], skip=1)
            for region in RIM:
                saturate(*region, keep_none)
            linearize()
        finish(moves, 2 + n, field)
        for j, at in ((0, 1), (1, 3), (2, 6)):
            partial = place(partial, at, matvec(j))
        sums = reduce_all(n, partial)
        gram = [[None] * 4 for _ in range(4)]
        at = 0
        for i in range(4):
            for j in range(i + 1):
                gram[i][j] = gram[j][i] = jnp.broadcast_to(sums[:, at : at + 1], (1, 128))
                at += 1
        weights = [w[:, 0:1] for w in krylov_weights(gram)]
        last = n + 1 == NEWTON
        rows, lanes = (slice(0, 16), slice(0, 512)) if last else (slice(0, ROWS), slice(0, LANES))

        def update(k, carry):
            value = head[k, rows, lanes]
            for i in range(KRYLOV):
                value = value - weights[i] * basis[i, k, rows, lanes]
            if last:
                out_ref[k] = value
            else:
                head[k] = value
            return carry

        lax.fori_loop(0, layers, update, 0)
        if not last:
            head_moves = start(3, 4, [(head, ())], skip=1)
            started.extend(head_moves)
            saturate(*OWN, keep_residual)
            for region in RIM:
                saturate(*region, keep_none)
            balance(True)

    for moves in started:
        drain(moves)
    sent = send_c.at[pl.ds(0, devices - 1), pl.ds(0, 7)]
    pltpu.make_async_copy(sent, sent, sem_c.at[0]).wait()
    for n in range(NEWTON):
        sent = gather.at[n, pl.ds(0, devices - 1)]
        pltpu.make_async_copy(sent, sent, sem_g.at[0, n]).wait()


def shards(sizes, head_old, soil_type, soil_table, forcing, canopy, column_slot):
    inputs = (head_old, soil_type, soil_table, forcing, canopy, column_slot)
    layers = head_old.shape[0]
    devices = sizes[0] * sizes[1]
    f32 = jnp.float32
    wide = (layers, ROWS, LANES)
    tile = (layers, 16, 512)
    vmem, anywhere = pl.BlockSpec(memory_space=pltpu.VMEM), pl.BlockSpec(memory_space=pl.ANY)
    return pl.pallas_call(
        functools.partial(kernel, sizes),
        out_shape=(
            jax.ShapeDtypeStruct(head_old.shape, f32),
            jax.ShapeDtypeStruct((2, 16, 512), f32),
        ),
        in_specs=[anywhere] * 6,
        out_specs=(vmem, vmem),
        scratch_shapes=[
            pltpu.SMEM(soil_table.shape, f32),
            pltpu.VMEM(tile, jnp.int32),
            pltpu.VMEM(forcing.shape, f32),
            pltpu.VMEM((2,) + canopy.shape, f32),
            pltpu.VMEM((24, 512), jnp.int32),
            pltpu.VMEM((devices, 8, 128), f32),
            pltpu.VMEM((devices * 8, 128), f32),
            pltpu.VMEM((13 * (devices // 4), 512), jnp.bfloat16),
            pltpu.VMEM((16, 256, 512), jnp.bfloat16),
            pltpu.VMEM((14, 16, 512), f32),
            pltpu.VMEM(wide, f32),
            pltpu.VMEM(wide, f32),
            pltpu.VMEM(wide, f32),
            pltpu.VMEM(wide, f32),
            pltpu.VMEM(wide, f32),
            pltpu.VMEM(wide, f32),
            pltpu.VMEM(wide, f32),
            pltpu.VMEM((7,) + wide, f32),
            pltpu.VMEM((KRYLOV,) + wide, f32),
            pltpu.VMEM(tile, f32),
            pltpu.VMEM(tile, f32),
            pltpu.VMEM(tile, f32),
            pltpu.VMEM((ROWS, LANES), f32),
            pltpu.VMEM((2, 6, 32, 512), f32),
            pltpu.VMEM((2, 6, 32, 512), f32),
            pltpu.VMEM((2, 3, 16, 512), f32),
            pltpu.VMEM((2, 3, 16, 512), f32),
            pltpu.VMEM((2, 5, 16, 128), f32),
            pltpu.VMEM((2, 5, 16, 128), f32),
            pltpu.VMEM((2, 2, 5, 8, 128), f32),
            pltpu.VMEM((NEWTON + 8, 1, 128), f32),
            pltpu.VMEM((NEWTON + 1, devices, 1, 128), f32),
            pltpu.SemaphoreType.DMA((6,)),
            pltpu.SemaphoreType.DMA((3,)),
            pltpu.SemaphoreType.DMA((2, 5, 8)),
            pltpu.SemaphoreType.DMA((2, NEWTON)),
        ],
        compiler_params=pltpu.CompilerParams(
            collective_id=0, has_side_effects=True, vmem_limit_bytes=48 * 1024 * 1024
        ),
        name="coupled_step",
    )(*(pltpu.with_memory_space_constraint(x, pltpu.HBM) for x in inputs))


def solution(mesh):
    sizes = (mesh.shape["gx"], mesh.shape["gy"])
    return jax.shard_map(
        functools.partial(shards, sizes),
        mesh=mesh,
        in_specs=(
            P(None, "gx", "gy"),
            P(None, "gx", "gy"),
            P(),
            P(None, "gx", "gy"),
            P(None, ("gx", "gy")),
            P("gx", "gy"),
        ),
        out_specs=(P(None, "gx", "gy"), P(None, "gx", "gy")),
        check_vma=False,
    )
```
